32 devices in a mesh: tm: 32 (over z, y, x, core).
Axes of the slice: x: 2, y: 2, z: 4, core: 2. Of those that a mesh axis runs over, the one named last changes fastest.
Arguments:
- hidden: bfloat16 [12288, 8192], P('tm'), may hold values from -6 to 6
- norm_gain: float32 [8192], replicated, may hold values from 0.1 to 1.9
- w_in: bfloat16 [8192, 768], replicated, may hold values from -0.0625 to 0.0625
- w_short: float32 [768, 7], replicated, may hold values from -2 to 2
- residues: float32 [8, 16], replicated, may hold values from -4 to 4
- rates: float32 [8, 16], replicated, may hold values from 1.6276042e-05 to 0.0333333333, as said below
- skip: float32 [256], replicated, may hold values from -4 to 4
- w_out: bfloat16 [256, 8192], replicated, may hold values from -0.375 to 0.375
Outputs:
- mixed: bfloat16 [12288, 8192], P('tm')
The draws below stay inside these ranges and needn't reach their ends.
Inputs may be any that keep to these rules, and one draw needn't show every extreme that they name: `rates`: every rate is positive.
All inputs are finite; a program needn't handle non-finite values.
Results may differ from the reference program's by a relative error of at most 0.0088.
Values may be sent and summed in bfloat16 or wider, within the bound.
A program may use at most 256 MiB of HBM per device.

```python
import jax
import jax.numpy as jnp
from jax import lax

D = 8192
C = 32
GROUPS = 8
M = 16
TAPS = 7
TOK_DEV = 384
CT = 256
TOKENS = 12288
N_TM = 32


def draw_rates(key, part):
    key_order = jax.random.fold_in(key, 11)
    key_slow = jax.random.fold_in(key, 12)
    key_fast = jax.random.fold_in(key, 13)
    order = jax.vmap(lambda sub: jax.random.permutation(sub, M))(jax.random.split(key_order, GROUPS))
    slow_low = jnp.log(0.2 / TOKENS)
    slow_high = jnp.log(2.0 / TOKENS)
    fast_low = jnp.log(1.0 / (2.0 * TOK_DEV))
    fast_high = jnp.log(1.0 / 30.0)
    slow_draw = slow_low + (slow_high - slow_low) * jax.random.uniform(key_slow, (GROUPS, M), jnp.float32)
    fast_draw = fast_low + (fast_high - fast_low) * jax.random.uniform(key_fast, (GROUPS, M), jnp.float32)
    slow_count = M // 2
    chosen = jnp.where(order < slow_count, slow_draw, fast_draw)
    return jnp.exp(chosen).astype(jnp.float32)


def shard_levels(own_key, dims, cuts, smallest, high):
    def one(dim, shards_of):
        heights = jax.random.uniform(jax.random.fold_in(jax.random.fold_in(own_key, 6), dim), (shards_of,), jnp.float32, smallest / len(cuts), high / len(cuts))
        return jnp.repeat(jnp.exp(heights), dims[dim] // shards_of).reshape((-1,) + (1,) * (len(dims) - dim - 1))

    loudness = one(*cuts[0])
    for cut in cuts[1:]:
        loudness = loudness * one(*cut)
    return loudness


def bell_draw(stream_key, shape, scale, most, cuts=(), held_as=jnp.bfloat16):
    drawn = jax.random.normal(stream_key, shape, jnp.float32) * scale
    if len(cuts) > 0:
        drawn = shard_levels(stream_key, shape, cuts, -0.22, 0.18) * drawn
    return jnp.clip(drawn, min=-most, max=most).astype(held_as)


def setup_inputs(seed: int = 0) -> dict:
    seeds = jax.random.split(jax.random.key(seed), 9)
    return {
        "hidden": bell_draw(seeds[0], (TOKENS, D), 1.0, 6.0, ((0, 32),)),
        "norm_gain": jnp.clip(1.0 + 0.18 * jax.random.normal(seeds[1], (D,), jnp.float32), 0.1, 1.9),
        "w_in": bell_draw(seeds[2], (D, 3 * CT), D ** -0.5, 0.0625),
        "w_short": bell_draw(seeds[3], (3 * CT, TAPS), TAPS ** -0.5, 2.0, (), jnp.float32),
        "residues": bell_draw(seeds[4], (GROUPS, M), 1.0, 4.0, (), jnp.float32),
        "rates": draw_rates(jax.random.fold_in(seeds[8], 71), 0),
        "skip": bell_draw(seeds[6], (CT,), 1.0, 4.0, (), jnp.float32),
        "w_out": bell_draw(seeds[7], (CT, D), CT ** -0.5, 0.375),
    }


def filter_taps(lag_values, rates, residues):
    weights = residues * jnp.sqrt(2.0 * rates)
    lagged = lag_values.astype(jnp.float32)
    values = lax.optimization_barrier(jnp.sum(weights * jnp.exp(-rates * jnp.maximum(lagged, 0.0)[..., None, None]), axis=-1))
    return jnp.where((lagged >= 0.0)[..., None], values, 0.0)

def reference(hidden, norm_gain, w_in, w_short, residues, rates, skip, w_out):

    def project_in(segment):
        widened = segment.astype(jnp.float32)
        inv_scale = lax.rsqrt(lax.optimization_barrier(jnp.mean(widened * widened, axis=1, keepdims=True)) + 1e-06)
        normed = (widened * inv_scale * norm_gain).astype(jnp.bfloat16)
        return jnp.dot(normed, w_in, preferred_element_type=jnp.float32).astype(jnp.bfloat16)
    projected = lax.map(project_in, hidden.reshape(N_TM, TOK_DEV, D)).reshape(TOKENS, 3 * CT)
    padded = jnp.concatenate([jnp.zeros((TAPS - 1, 3 * CT), jnp.bfloat16), projected], axis=0).astype(jnp.float32)
    features = jnp.zeros((TOKENS, 3 * CT), jnp.float32)
    for offset_tap in range(TAPS):
        features = features + w_short[:, offset_tap] * padded[TAPS - 1 - offset_tap:TAPS - 1 - offset_tap + TOKENS]
    queries = features[:, :CT]
    keyed = features[:, CT:2 * CT]
    valued = features[:, 2 * CT:]
    product = (keyed * valued).astype(jnp.bfloat16).astype(jnp.float32)
    filt = filter_taps(jnp.arange(TOKENS, dtype=jnp.int32), rates, residues)
    filt_channels = jnp.repeat(filt, C, axis=1)
    length = 2 * TOKENS
    spectrum = jnp.fft.rfft(filt_channels, n=length, axis=0) * jnp.fft.rfft(product, n=length, axis=0)
    convolved = jnp.fft.irfft(spectrum, n=length, axis=0)[:TOKENS].astype(jnp.float32)
    gated = (queries * (convolved + skip * product)).astype(jnp.bfloat16)

    def project_out(segment):
        return jnp.dot(segment, w_out, preferred_element_type=jnp.float32).astype(jnp.bfloat16)
    return lax.map(project_out, gated.reshape(N_TM, TOK_DEV, CT)).reshape(TOKENS, D)
```

```python
import functools

import jax
import jax.numpy as jnp
from jax import lax
from jax.experimental import pallas as pl
from jax.experimental.pallas import tpu as pltpu
from jax.sharding import PartitionSpec as P

HIGHEST = lax.Precision.HIGHEST
MESH = pl.DeviceIdType.MESH
LANES = 128
EDGE = 8
F32 = jnp.float32
BF16 = jnp.bfloat16


def iota(shape, dim):
    return lax.broadcasted_iota(jnp.int32, shape, dim)


def dot(a, b):
    return jnp.dot(a, b, preferred_element_type=F32)


def split(x):
    high = x.astype(BF16)
    return high, (x - high.astype(F32)).astype(BF16)


def mixer(
    n, depth, hidden, w_in, gain, taps, rates, residues, skip, out,
    held, w_kv, w_q, acc_kv, acc_q, squares, proj_kv, proj_q, prod, feat_q,
    fall, rise, lag_row, toeplitz, own, slots,
    held_sem, kv_sem, q_sem, edge_sem, send_sem, recv_sem,
):
    me = lax.axis_index("tm")
    following = lax.rem(me + 1, n)
    tok, width = hidden.shape
    chan = prod.shape[1]
    groups, modes = rates.shape
    every = groups * modes
    per_group = chan // groups
    chunks = width // depth

    barrier = pltpu.get_barrier_semaphore()

    @pl.loop(0, me)
    def _(d):
        pl.semaphore_signal(barrier, inc=1, device_id=(d,), device_id_type=MESH)

    def held_copy(k):
        cols = pl.ds(pl.multiple_of(k * depth, depth), depth)
        return pltpu.make_async_copy(hidden.at[:, cols], held.at[k], held_sem.at[k])

    def kv_copy(k):
        rows = pl.ds(pl.multiple_of(k * depth, depth), depth)
        return pltpu.make_async_copy(w_in.at[rows, pl.ds(chan, 2 * chan)], w_kv.at[k], kv_sem.at[k])

    def q_copy(k):
        rows = pl.ds(pl.multiple_of(k * depth, depth), depth)
        return pltpu.make_async_copy(w_in.at[rows, pl.ds(0, chan)], w_q.at[k], q_sem.at[k])

    @pl.loop(0, chunks)
    def _(k):
        held_copy(k).start()
        kv_copy(k).start()

    @pl.loop(0, chunks)
    def _(k):
        q_copy(k).start()

    pick = (iota((modes, every), 1) % modes == iota((modes, every), 0)).astype(F32)
    mine = iota((groups, every), 1) // modes == iota((groups, every), 0)
    spread = (iota((groups, chan), 1) // per_group == iota((groups, chan), 0)).astype(F32)
    diagonal = iota((every, every), 0) == iota((every, every), 1)
    weights = residues[...] * jnp.sqrt(2.0 * rates[...])

    def as_row(x):
        wide = jnp.dot(x, pick, precision=HIGHEST, preferred_element_type=F32)
        return jnp.sum(jnp.where(mine, wide, 0.0), axis=0, keepdims=True)

    def as_column(row):
        return jnp.sum(jnp.where(diagonal, row, 0.0), axis=1, keepdims=True)

    def by_channel(x):
        return lax.dot_general(
            x, spread, (((0,), (0,)), ((), ())), precision=HIGHEST, preferred_element_type=F32
        )

    rate_row = as_row(rates[...])
    rate_col = as_column(rate_row)
    weight_col = as_column(as_row(weights))
    rate_mc = by_channel(rates[...])
    weight_mc = by_channel(weights)
    high, low = split(jnp.exp(-rate_col * (tok - 1 - iota((every, tok), 1)).astype(F32)))
    fall[:every], fall[every:] = high, low
    high, low = split(jnp.exp(-rate_row * (iota((tok, every), 0) + 1).astype(F32)))
    rise[:, :every], rise[:, every:] = high, low
    back = lax.rem(tok - iota((every, tok), 1), tok).astype(F32)
    terms = weight_col * jnp.exp(-rate_col * back)
    for g in range(groups):
        lag_row[g : g + 1] = jnp.sum(terms[g * modes : (g + 1) * modes], axis=0, keepdims=True)

    acc_kv[...] = jnp.zeros_like(acc_kv)
    acc_q[...] = jnp.zeros_like(acc_q)
    squares[...] = jnp.zeros_like(squares)

    @pl.loop(0, chunks)
    def _(k):
        held_copy(k).wait()
        kv_copy(k).wait()
        scale = gain[:, pl.ds(pl.multiple_of(k * depth, depth), depth)]
        parts = []
        for r in range(0, tok, 16):
            x = held[k, r : r + 16].astype(F32)
            sq = x * x
            total = squares[r : r + 16]
            for j in range(0, depth, LANES):
                total = total + sq[:, j : j + LANES]
            squares[r : r + 16] = total
            parts.append((x * scale).astype(BF16))
        scaled = jnp.concatenate(parts, axis=0)
        held[k] = scaled
        acc_kv[...] += dot(scaled, w_kv[k])

    inv = lax.rsqrt(jnp.sum(squares[...], axis=1, keepdims=True) / width + 1e-06)
    proj_kv[EDGE:] = acc_kv[...] * inv

    @pl.when(me == 0)
    def _():
        proj_kv[:EDGE] = jnp.zeros((EDGE, 2 * chan), F32)
        proj_q[:EDGE] = jnp.zeros((EDGE, chan), F32)

    @pl.when(me < n - 1)
    def _():
        pl.semaphore_wait(barrier, n - 1 - me)

    def edge_copy(buf, i):
        return pltpu.make_async_remote_copy(
            src_ref=buf.at[pl.ds(tok, EDGE)], dst_ref=buf.at[pl.ds(0, EDGE)],
            send_sem=edge_sem.at[2 * i], recv_sem=edge_sem.at[2 * i + 1],
            device_id=(following,), device_id_type=MESH,
        )

    @pl.when(me < n - 1)
    def _():
        edge_copy(proj_kv, 0).start()

    half = chunks // 2
    strip = tok // half

    def feature(buf, r, rows, first, tap_first):
        total = jnp.zeros((rows, chan), F32)
        for t in range(taps.shape[0]):
            total = total + taps[t : t + 1, tap_first : tap_first + chan] * buf[
                pl.ds(r + EDGE - t, rows), first : first + chan
            ]
        return total

    def query_step(k, start):
        q_copy(k).wait()
        for r in range(0, strip, 32):
            keyed = feature(proj_kv, start + r, 32, 0, chan)
            valued = feature(proj_kv, start + r, 32, chan, 2 * chan)
            prod[pl.ds(start + r, 32)] = (keyed * valued).astype(BF16)
        acc_q[...] += dot(held[k], w_q[k])

    tiles = tok // LANES
    causal = iota((LANES, LANES), 0) >= iota((LANES, LANES), 1)
    share = groups // (chunks - half)

    def toeplitz_step(k):
        q_copy(k).wait()
        for e in range(share):
            g = (k - half) * share + e
            first = jnp.broadcast_to(lag_row[pl.ds(g, 1)], (LANES, tok))
            moved = pltpu.roll(first, 0, 1, stride=1, stride_axis=0)
            lags = []
            for i in range(tiles):
                at = (tiles - i) % tiles * LANES
                tile = moved[:, at : at + LANES]
                lags.append((jnp.where(causal, tile, 0.0) if i == 0 else tile).astype(BF16))
            for i in range(tiles):
                for j in range(tiles):
                    value = lags[i - j] if i >= j else jnp.zeros((LANES, LANES), BF16)
                    toeplitz[g, i * LANES : (i + 1) * LANES, j * LANES : (j + 1) * LANES] = value
        acc_q[...] += dot(held[k], w_q[k])

    for k in range(1, half):
        query_step(k, k * strip)

    early = half + (chunks - half) // 2

    pl.loop(half, early)(toeplitz_step)

    @pl.when(me > 0)
    def _():
        edge_copy(proj_kv, 0).wait_recv()

    query_step(0, 0)

    both = dot(fall[...], prod[...])
    wide = both[:every] + both[every:]
    group_of = iota((modes, chan), 1) // per_group
    packed = jnp.zeros((modes, chan), F32)
    for g in range(groups):
        packed = packed + jnp.where(group_of == g, wide[g * modes : (g + 1) * modes], 0.0)
    own[...] = packed.astype(BF16)

    def state_copy(source, target):
        return pltpu.make_async_remote_copy(
            src_ref=own, dst_ref=slots.at[source],
            send_sem=send_sem.at[target], recv_sem=recv_sem.at[source],
            device_id=(target,), device_id_type=MESH,
        )

    @pl.loop(me + 1, n)
    def _(d):
        state_copy(me, d).start()

    pl.loop(early, chunks)(toeplitz_step)

    proj_q[EDGE:] = acc_q[...] * inv

    @pl.when(me < n - 1)
    def _():
        edge_copy(proj_q, 1).start()

    product = prod[...]
    channel_group = iota((tok, chan), 1) // per_group
    block = 2 * LANES

    def convolve(some):
        total = []
        for s0 in range(0, tok, block):
            s1 = min(s0 + block, tok)
            here = None
            for g in some:
                part = jnp.where(channel_group[s0:s1] == g, product[s0:s1], jnp.zeros_like(product[s0:s1]))
                term = dot(toeplitz[g, s0:, s0:s1], part)
                here = term if here is None else here + term
            total.append((s0, here))
        return total

    def add(parts):
        for s0, value in parts:
            acc_q[s0:] += value

    acc_q[...] = skip[...] * product.astype(F32)
    add(convolve(range(groups // 2)))

    for r in range(32, tok, 32):
        feat_q[r : r + 32] = feature(proj_q, r, 32, 0, 0)
    add(convolve(range(groups // 2, groups)))

    decay = jnp.exp(-rate_mc * float(tok))

    def gather(d, state):
        state_copy(d, following).wait_recv()
        return decay * state + slots[d].astype(F32)

    @pl.when(me > 0)
    def _():
        edge_copy(proj_q, 1).wait_recv()

    feat_q[:32] = feature(proj_q, 0, 32, 0, 0)
    state = lax.fori_loop(0, me, gather, jnp.zeros((modes, chan), F32)) * weight_mc
    stacked = jnp.concatenate([state] * groups, axis=0)
    same = iota((every, chan), 0) // modes == iota((every, chan), 1) // per_group
    high, low = split(jnp.where(same, stacked, 0.0))
    far = dot(rise[...], jnp.concatenate([high, high], axis=0)) + dot(rise[:, :every], low)
    out[...] = (feat_q[...] * (acc_q[...] + far)).astype(BF16)

    @pl.when(me < n - 1)
    def _():
        edge_copy(proj_kv, 0).wait_send()
        edge_copy(proj_q, 1).wait_send()

    @pl.loop(me + 1, n)
    def _(d):
        state_copy(me, d).wait_send()


def project_out(gated, w_out, mixed, held, sem):
    parts, _, block = held.shape

    def copy(k):
        return pltpu.make_async_copy(held.at[k], mixed.at[:, pl.ds(k * block, block)], sem.at[k])

    for k in range(parts):
        held[k] = dot(gated[...], w_out[:, k * block : (k + 1) * block]).astype(BF16)
        copy(k).start()
    for k in range(parts):
        copy(k).wait()


def on_device(n, hidden, norm_gain, w_in, w_short, residues, rates, skip, w_out):
    tok, width = hidden.shape
    chan = w_short.shape[0] // 3
    groups, modes = rates.shape
    every = groups * modes
    depth = min(1024, width)
    chunks = width // depth
    vmem = pl.BlockSpec(memory_space=pltpu.VMEM)
    in_hbm = pl.BlockSpec(memory_space=pltpu.HBM)
    gated = pl.pallas_call(
        functools.partial(mixer, n, depth),
        out_shape=pltpu.VMEM((tok, chan), BF16),
        in_specs=[in_hbm, in_hbm] + [vmem] * 5,
        out_specs=vmem,
        scratch_shapes=[
            pltpu.VMEM((chunks, tok, depth), BF16),
            pltpu.VMEM((chunks, depth, 2 * chan), BF16),
            pltpu.VMEM((chunks, depth, chan), BF16),
            pltpu.VMEM((tok, 2 * chan), F32),
            pltpu.VMEM((tok, chan), F32),
            pltpu.VMEM((tok, LANES), F32),
            pltpu.VMEM((EDGE + tok, 2 * chan), F32),
            pltpu.VMEM((EDGE + tok, chan), F32),
            pltpu.VMEM((tok, chan), BF16),
            pltpu.VMEM((tok, chan), F32),
            pltpu.VMEM((2 * every, tok), BF16),
            pltpu.VMEM((tok, 2 * every), BF16),
            pltpu.VMEM((groups, tok), F32),
            pltpu.VMEM((groups, tok, tok), BF16),
            pltpu.VMEM((modes, chan), BF16),
            pltpu.VMEM((n, modes, chan), BF16),
            pltpu.SemaphoreType.DMA((chunks,)),
            pltpu.SemaphoreType.DMA((chunks,)),
            pltpu.SemaphoreType.DMA((chunks,)),
            pltpu.SemaphoreType.DMA((4,)),
            pltpu.SemaphoreType.DMA((n,)),
            pltpu.SemaphoreType.DMA((n,)),
        ],
        compiler_params=pltpu.CompilerParams(
            collective_id=0, has_side_effects=True, vmem_limit_bytes=58 * 1024 * 1024
        ),
        name="mixer",
        cost_estimate=pl.CostEstimate(
            flops=2 * tok * width * 3 * chan, bytes_accessed=2 * width * (tok + 3 * chan), transcendentals=0
        ),
    )(hidden, w_in, norm_gain.reshape(1, width), w_short.T, rates, residues, skip.reshape(1, chan))
    parts = 16
    return pl.pallas_call(
        project_out,
        out_shape=jax.ShapeDtypeStruct((tok, width), BF16),
        in_specs=[vmem, vmem],
        out_specs=in_hbm,
        scratch_shapes=[
            pltpu.VMEM((parts, tok, width // parts), BF16),
            pltpu.SemaphoreType.DMA((parts,)),
        ],
        name="project_out",
        compiler_params=pltpu.CompilerParams(vmem_limit_bytes=24 * 1024 * 1024),
        cost_estimate=pl.CostEstimate(
            flops=2 * tok * width * chan, bytes_accessed=2 * width * (tok + chan), transcendentals=0
        ),
    )(gated, w_out)


def solution(mesh):
    return jax.shard_map(
        functools.partial(on_device, mesh.shape["tm"]),
        mesh=mesh,
        in_specs=(P("tm", None), P(), P(), P(), P(), P(), P(), P()),
        out_specs=P("tm", None),
        check_vma=False,
    )
```

```python
import functools

import jax
import jax.numpy as jnp
from jax import lax
from jax.experimental import pallas as pl
from jax.experimental.pallas import tpu as pltpu
from jax.sharding import PartitionSpec as P

HIGHEST = lax.Precision.HIGHEST
MESH = pl.DeviceIdType.MESH
LANES = 128
EDGE = 8
F32 = jnp.float32
BF16 = jnp.bfloat16


def iota(shape, dim):
    return lax.broadcasted_iota(jnp.int32, shape, dim)


def dot(a, b):
    return jnp.dot(a, b, preferred_element_type=F32)


def split(x):
    high = x.astype(BF16)
    return high, (x - high.astype(F32)).astype(BF16)


def mixer(
    n, depth, hidden, w_in, w_out, gain_far, taps_far, rates_far, residues_far, skip_far, out, w_out_near,
    gain, taps, rates, residues, skip,
    held, w_kv, w_q, acc_kv, acc_q, squares, proj_kv, proj_q, prod, feat_q,
    fall, rise, lag_row, toeplitz, own, slots,
    held_sem, kv_sem, q_sem, edge_sem, send_sem, recv_sem, out_sem, small_sem,
):
    me = lax.axis_index("tm")
    following = lax.rem(me + 1, n)
    tok, width = hidden.shape
    chan = prod.shape[1]
    groups, modes = rates.shape
    every = groups * modes
    per_group = chan // groups
    chunks = width // depth

    small = [
        pltpu.make_async_copy(source, target, small_sem.at[i])
        for i, (source, target) in enumerate(
            [(rates_far, rates), (residues_far, residues), (gain_far, gain), (taps_far, taps), (skip_far, skip)]
        )
    ]
    for copy in small:
        copy.start()

    def held_copy(k):
        cols = pl.ds(pl.multiple_of(k * depth, depth), depth)
        return pltpu.make_async_copy(hidden.at[:, cols], held.at[k], held_sem.at[k])

    def kv_copy(k):
        rows = pl.ds(pl.multiple_of(k * depth, depth), depth)
        return pltpu.make_async_copy(w_in.at[rows, pl.ds(chan, 2 * chan)], w_kv.at[k], kv_sem.at[k])

    def q_copy(k):
        rows = pl.ds(pl.multiple_of(k * depth, depth), depth)
        return pltpu.make_async_copy(w_in.at[rows, pl.ds(0, chan)], w_q.at[k], q_sem.at[k])

    @pl.loop(0, chunks)
    def _(k):
        held_copy(k).start()
        kv_copy(k).start()

    @pl.loop(0, chunks)
    def _(k):
        q_copy(k).start(priority=1)

    out_copy = pltpu.make_async_copy(w_out, w_out_near, out_sem)
    out_copy.start(priority=1)

    barrier = pltpu.get_barrier_semaphore()

    @pl.loop(0, me)
    def _(d):
        pl.semaphore_signal(barrier, inc=1, device_id=(d,), device_id_type=MESH)

    for copy in small:
        copy.wait()

    pick = (iota((modes, every), 1) % modes == iota((modes, every), 0)).astype(F32)
    mine = iota((groups, every), 1) // modes == iota((groups, every), 0)
    spread = (iota((groups, chan), 1) // per_group == iota((groups, chan), 0)).astype(F32)
    diagonal = iota((every, every), 0) == iota((every, every), 1)
    weights = residues[...] * jnp.sqrt(2.0 * rates[...])

    def as_row(x):
        wide = jnp.dot(x, pick, precision=HIGHEST, preferred_element_type=F32)
        return jnp.sum(jnp.where(mine, wide, 0.0), axis=0, keepdims=True)

    def as_column(row):
        return jnp.sum(jnp.where(diagonal, row, 0.0), axis=1, keepdims=True)

    def by_channel(x):
        return lax.dot_general(
            x, spread, (((0,), (0,)), ((), ())), precision=HIGHEST, preferred_element_type=F32
        )

    rate_row = as_row(rates[...])
    rate_col = as_column(rate_row)
    weight_col = as_column(as_row(weights))
    rate_mc = by_channel(rates[...])
    weight_mc = by_channel(weights)
    high, low = split(jnp.exp(-rate_col * (tok - 1 - iota((every, tok), 1)).astype(F32)))
    fall[:every], fall[every:] = high, low
    high, low = split(jnp.exp(-rate_row * (iota((tok, every), 0) + 1).astype(F32)))
    rise[:, :every], rise[:, every:] = high, low
    back = lax.rem(tok - iota((every, tok), 1), tok).astype(F32)
    terms = weight_col * jnp.exp(-rate_col * back)
    for g in range(groups):
        lag_row[g : g + 1] = jnp.sum(terms[g * modes : (g + 1) * modes], axis=0, keepdims=True)

    acc_kv[...] = jnp.zeros_like(acc_kv)
    acc_q[...] = jnp.zeros_like(acc_q)
    squares[...] = jnp.zeros_like(squares)

    @pl.loop(0, chunks)
    def _(k):
        held_copy(k).wait()
        kv_copy(k).wait()
        scale = gain[:, pl.ds(pl.multiple_of(k * depth, depth), depth)]
        parts = []
        for r in range(0, tok, 16):
            x = held[k, r : r + 16].astype(F32)
            sq = x * x
            total = squares[r : r + 16]
            for j in range(0, depth, LANES):
                total = total + sq[:, j : j + LANES]
            squares[r : r + 16] = total
            parts.append((x * scale).astype(BF16))
        scaled = jnp.concatenate(parts, axis=0)
        held[k] = scaled
        acc_kv[...] += dot(scaled, w_kv[k])

    inv = lax.rsqrt(jnp.sum(squares[...], axis=1, keepdims=True) / width + 1e-06)
    proj_kv[EDGE:] = acc_kv[...] * inv

    @pl.when(me == 0)
    def _():
        proj_kv[:EDGE] = jnp.zeros((EDGE, 2 * chan), F32)
        proj_q[:EDGE] = jnp.zeros((EDGE, chan), F32)

    @pl.when(me < n - 1)
    def _():
        pl.semaphore_wait(barrier, n - 1 - me)

    def edge_copy(buf, i):
        return pltpu.make_async_remote_copy(
            src_ref=buf.at[pl.ds(tok, EDGE)], dst_ref=buf.at[pl.ds(0, EDGE)],
            send_sem=edge_sem.at[2 * i], recv_sem=edge_sem.at[2 * i + 1],
            device_id=(following,), device_id_type=MESH,
        )

    @pl.when(me < n - 1)
    def _():
        edge_copy(proj_kv, 0).start()

    def feature(buf, r, rows, first, tap_first):
        total = jnp.zeros((rows, chan), F32)
        for t in range(taps.shape[0]):
            total = total + taps[t : t + 1, tap_first : tap_first + chan] * buf[
                pl.ds(r + EDGE - t, rows), first : first + chan
            ]
        return total

    def key_value(r):
        keyed = feature(proj_kv, r, 32, 0, chan)
        valued = feature(proj_kv, r, 32, chan, 2 * chan)
        prod[pl.ds(r, 32)] = (keyed * valued).astype(BF16)

    def query_step(k):
        q_copy(k).wait()
        acc_q[...] += dot(held[k], w_q[k])

    tiles = tok // LANES
    causal = iota((LANES, LANES), 0) >= iota((LANES, LANES), 1)
    def toeplitz_step(g):
        first = jnp.broadcast_to(lag_row[pl.ds(g, 1)], (LANES, tok))
        moved = pltpu.roll(first, 0, 1, stride=1, stride_axis=0)
        lags = []
        for i in range(tiles):
            at = (tiles - i) % tiles * LANES
            tile = moved[:, at : at + LANES]
            lags.append((jnp.where(causal, tile, 0.0) if i == 0 else tile).astype(BF16))
        for i in range(tiles):
            for j in range(tiles):
                value = lags[i - j] if i >= j else jnp.zeros((LANES, LANES), BF16)
                toeplitz[g, i * LANES : (i + 1) * LANES, j * LANES : (j + 1) * LANES] = value

    for r in range(32, tok, 32):
        key_value(r)

    pl.loop(0, groups)(toeplitz_step)

    early = chunks // 2
    pl.loop(0, early)(query_step)

    @pl.when(me > 0)
    def _():
        edge_copy(proj_kv, 0).wait_recv()

    key_value(0)

    both = dot(fall[...], prod[...])
    wide = both[:every] + both[every:]
    group_of = iota((modes, chan), 1) // per_group
    packed = jnp.zeros((modes, chan), F32)
    for g in range(groups):
        packed = packed + jnp.where(group_of == g, wide[g * modes : (g + 1) * modes], 0.0)
    own[...] = packed.astype(BF16)

    def state_copy(source, target):
        return pltpu.make_async_remote_copy(
            src_ref=own, dst_ref=slots.at[source],
            send_sem=send_sem.at[target], recv_sem=recv_sem.at[source],
            device_id=(target,), device_id_type=MESH,
        )

    @pl.loop(me + 1, n)
    def _(d):
        state_copy(me, d).start()

    pl.loop(early, chunks)(query_step)

    proj_q[EDGE:] = acc_q[...] * inv

    @pl.when(me < n - 1)
    def _():
        edge_copy(proj_q, 1).start()

    product = prod[...]
    channel_group = iota((tok, chan), 1) // per_group
    block = 2 * LANES

    def convolve(some):
        total = []
        for s0 in range(0, tok, block):
            s1 = min(s0 + block, tok)
            here = None
            for g in some:
                part = jnp.where(channel_group[s0:s1] == g, product[s0:s1], jnp.zeros_like(product[s0:s1]))
                term = dot(toeplitz[g, s0:, s0:s1], part)
                here = term if here is None else here + term
            total.append((s0, here))
        return total

    def add(parts):
        for s0, value in parts:
            acc_q[s0:] += value

    acc_q[...] = skip[...] * product.astype(F32)
    add(convolve(range(groups // 2)))

    for r in range(32, tok, 32):
        feat_q[r : r + 32] = feature(proj_q, r, 32, 0, 0)
    add(convolve(range(groups // 2, groups)))

    decay = jnp.exp(-rate_mc * float(tok))

    def gather(d, state):
        state_copy(d, following).wait_recv()
        return decay * state + slots[d].astype(F32)

    @pl.when(me > 0)
    def _():
        edge_copy(proj_q, 1).wait_recv()

    feat_q[:32] = feature(proj_q, 0, 32, 0, 0)
    state = lax.fori_loop(0, me, gather, jnp.zeros((modes, chan), F32)) * weight_mc
    stacked = jnp.concatenate([state] * groups, axis=0)
    same = iota((every, chan), 0) // modes == iota((every, chan), 1) // per_group
    high, low = split(jnp.where(same, stacked, 0.0))
    far = dot(rise[...], jnp.concatenate([high, high], axis=0)) + dot(rise[:, :every], low)
    out[...] = (feat_q[...] * (acc_q[...] + far)).astype(BF16)

    out_copy.wait()

    @pl.when(me < n - 1)
    def _():
        edge_copy(proj_kv, 0).wait_send()
        edge_copy(proj_q, 1).wait_send()

    @pl.loop(me + 1, n)
    def _(d):
        state_copy(me, d).wait_send()


def project_out(gated, w_out, mixed, held, sem):
    parts, _, block = held.shape

    def copy(k):
        return pltpu.make_async_copy(held.at[k], mixed.at[:, pl.ds(k * block, block)], sem.at[k])

    for k in range(parts):
        held[k] = dot(gated[...], w_out[:, k * block : (k + 1) * block]).astype(BF16)
        copy(k).start()
    for k in range(parts):
        copy(k).wait()


def on_device(n, hidden, norm_gain, w_in, w_short, residues, rates, skip, w_out):
    tok, width = hidden.shape
    chan = w_short.shape[0] // 3
    groups, modes = rates.shape
    every = groups * modes
    depth = min(1024, width)
    chunks = width // depth
    vmem = pl.BlockSpec(memory_space=pltpu.VMEM)
    in_hbm = pl.BlockSpec(memory_space=pltpu.HBM)
    gated, w_out_near = pl.pallas_call(
        functools.partial(mixer, n, depth),
        out_shape=[pltpu.VMEM((tok, chan), BF16), pltpu.VMEM((chan, width), BF16)],
        in_specs=[in_hbm] * 8,
        out_specs=[vmem, vmem],
        scratch_shapes=[
            pltpu.VMEM((1, width), F32),
            pltpu.VMEM((w_short.shape[1], 3 * chan), F32),
            pltpu.VMEM((groups, modes), F32),
            pltpu.VMEM((groups, modes), F32),
            pltpu.VMEM((1, chan), F32),
            pltpu.VMEM((chunks, tok, depth), BF16),
            pltpu.VMEM((chunks, depth, 2 * chan), BF16),
            pltpu.VMEM((chunks, depth, chan), BF16),
            pltpu.VMEM((tok, 2 * chan), F32),
            pltpu.VMEM((tok, chan), F32),
            pltpu.VMEM((tok, LANES), F32),
            pltpu.VMEM((EDGE + tok, 2 * chan), F32),
            pltpu.VMEM((EDGE + tok, chan), F32),
            pltpu.VMEM((tok, chan), BF16),
            pltpu.VMEM((tok, chan), F32),
            pltpu.VMEM((2 * every, tok), BF16),
            pltpu.VMEM((tok, 2 * every), BF16),
            pltpu.VMEM((groups, tok), F32),
            pltpu.VMEM((groups, tok, tok), BF16),
            pltpu.VMEM((modes, chan), BF16),
            pltpu.VMEM((n, modes, chan), BF16),
            pltpu.SemaphoreType.DMA((chunks,)),
            pltpu.SemaphoreType.DMA((chunks,)),
            pltpu.SemaphoreType.DMA((chunks,)),
            pltpu.SemaphoreType.DMA((4,)),
            pltpu.SemaphoreType.DMA((n,)),
            pltpu.SemaphoreType.DMA((n,)),
            pltpu.SemaphoreType.DMA,
            pltpu.SemaphoreType.DMA((5,)),
        ],
        compiler_params=pltpu.CompilerParams(
            collective_id=0, has_side_effects=True, vmem_limit_bytes=48 * 1024 * 1024
        ),
        name="mixer",
        cost_estimate=pl.CostEstimate(
            flops=2 * tok * width * 3 * chan, bytes_accessed=2 * width * (tok + 3 * chan), transcendentals=0
        ),
    )(
        hidden, w_in, w_out,
        *(
            pltpu.with_memory_space_constraint(x, pltpu.HBM)
            for x in (norm_gain.reshape(1, width), w_short.T, rates, residues, skip.reshape(1, chan))
        ),
    )
    parts = 16
    return pl.pallas_call(
        project_out,
        out_shape=jax.ShapeDtypeStruct((tok, width), BF16),
        in_specs=[vmem, vmem],
        out_specs=in_hbm,
        scratch_shapes=[
            pltpu.VMEM((parts, tok, width // parts), BF16),
            pltpu.SemaphoreType.DMA((parts,)),
        ],
        name="project_out",
        compiler_params=pltpu.CompilerParams(vmem_limit_bytes=24 * 1024 * 1024),
        cost_estimate=pl.CostEstimate(
            flops=2 * tok * width * chan, bytes_accessed=2 * width * (tok + chan), transcendentals=0
        ),
    )(gated, w_out_near)


def solution(mesh):
    return jax.shard_map(
        functools.partial(on_device, mesh.shape["tm"]),
        mesh=mesh,
        in_specs=(P("tm", None), P(), P(), P(), P(), P(), P(), P()),
        out_specs=P("tm", None),
        check_vma=False,
    )
```

```python
import functools

import jax
import jax.numpy as jnp
from jax import lax
from jax.experimental import pallas as pl
from jax.experimental.pallas import tpu as pltpu
from jax.sharding import PartitionSpec as P

HIGHEST = lax.Precision.HIGHEST
MESH = pl.DeviceIdType.MESH
LANES = 128
EDGE = 8
F32 = jnp.float32
BF16 = jnp.bfloat16


def iota(shape, dim):
    return lax.broadcasted_iota(jnp.int32, shape, dim)


def dot(a, b):
    return jnp.dot(a, b, preferred_element_type=F32)


def split(x):
    high = x.astype(BF16)
    return high, (x - high.astype(F32)).astype(BF16)


def mixer(
    n, depth, hidden, w_in, w_out, gain_far, taps_far, rates_far, residues_far, skip_far, out, w_out_near,
    gain, taps, rates, residues, skip,
    held, w_kv, w_q, acc_kv, acc_q, squares, proj_kv, proj_q, prod, feat_q,
    fall, rise, lag_row, toeplitz, lead, other_lead, edge_fall, mine_state, other_state, even_state, own, slots,
    held_sem, kv_sem, q_sem, near_send, near_recv, send_sem, recv_sem, out_sem, small_sem,
):
    me = lax.axis_index("tm")
    following = lax.rem(me + 1, n)
    pairs = n // 2
    pair, side = me // 2, lax.rem(me, 2)
    sibling = me + 1 - 2 * side
    tok, width = hidden.shape
    chan = prod.shape[1]
    groups, modes = rates.shape
    every = groups * modes
    per_group = chan // groups
    chunks = width // depth

    small = [
        pltpu.make_async_copy(source, target, small_sem.at[i])
        for i, (source, target) in enumerate(
            [(rates_far, rates), (residues_far, residues), (gain_far, gain), (taps_far, taps), (skip_far, skip)]
        )
    ]
    for copy in small:
        copy.start()

    def held_copy(k):
        cols = pl.ds(pl.multiple_of(k * depth, depth), depth)
        return pltpu.make_async_copy(hidden.at[:, cols], held.at[k], held_sem.at[k])

    def kv_copy(k):
        rows = pl.ds(pl.multiple_of(k * depth, depth), depth)
        return pltpu.make_async_copy(w_in.at[rows, pl.ds(chan, 2 * chan)], w_kv.at[k], kv_sem.at[k])

    def q_copy(k):
        rows = pl.ds(pl.multiple_of(k * depth, depth), depth)
        return pltpu.make_async_copy(w_in.at[rows, pl.ds(0, chan)], w_q.at[k], q_sem.at[k])

    @pl.loop(0, chunks)
    def _(k):
        held_copy(k).start()
        kv_copy(k).start()

    @pl.loop(0, chunks)
    def _(k):
        q_copy(k).start(priority=1)

    out_copy = pltpu.make_async_copy(w_out, w_out_near, out_sem)
    out_copy.start(priority=1)

    barrier = pltpu.get_barrier_semaphore()

    def greet(d):
        pl.semaphore_signal(barrier, inc=1, device_id=(d,), device_id_type=MESH)

    @pl.loop(0, pair)
    def _(p):
        greet(2 * p + side)

    greet(sibling)

    @pl.when(jnp.logical_and(side == 0, pair > 0))
    def _():
        greet(me - 1)

    for copy in small:
        copy.wait()

    pick = (iota((modes, every), 1) % modes == iota((modes, every), 0)).astype(F32)
    mine = iota((groups, every), 1) // modes == iota((groups, every), 0)
    spread = (iota((groups, chan), 1) // per_group == iota((groups, chan), 0)).astype(F32)
    diagonal = iota((every, every), 0) == iota((every, every), 1)
    weights = residues[...] * jnp.sqrt(2.0 * rates[...])

    def as_row(x):
        wide = jnp.dot(x, pick, precision=HIGHEST, preferred_element_type=F32)
        return jnp.sum(jnp.where(mine, wide, 0.0), axis=0, keepdims=True)

    def as_column(row):
        return jnp.sum(jnp.where(diagonal, row, 0.0), axis=1, keepdims=True)

    def by_channel(x):
        return lax.dot_general(
            x, spread, (((0,), (0,)), ((), ())), precision=HIGHEST, preferred_element_type=F32
        )

    rate_row = as_row(rates[...])
    rate_col = as_column(rate_row)
    weight_col = as_column(as_row(weights))
    rate_mc = by_channel(rates[...])
    weight_mc = by_channel(weights)
    high, low = split(jnp.exp(-rate_col * (tok - 1 - iota((every, tok), 1)).astype(F32)))
    early_rows = iota((every, tok), 1) < EDGE
    fall[:every] = jnp.where(early_rows, jnp.zeros_like(high), high)
    fall[every:] = jnp.where(early_rows, jnp.zeros_like(low), low)
    for r in range(EDGE):
        edge_fall[r] = jnp.exp(-rate_mc * float(tok - 1 - r))
    high, low = split(jnp.exp(-rate_row * (iota((tok, every), 0) + 1).astype(F32)))
    rise[:, :every], rise[:, every:] = high, low
    back = lax.rem(tok - iota((every, tok), 1), tok).astype(F32)
    terms = weight_col * jnp.exp(-rate_col * back)
    for g in range(groups):
        lag_row[g : g + 1] = jnp.sum(terms[g * modes : (g + 1) * modes], axis=0, keepdims=True)

    even_state[...] = jnp.zeros_like(even_state)
    acc_kv[...] = jnp.zeros_like(acc_kv)
    acc_q[...] = jnp.zeros_like(acc_q)
    squares[...] = jnp.zeros_like(squares)

    @pl.loop(0, chunks)
    def _(k):
        held_copy(k).wait()
        kv_copy(k).wait()
        scale = gain[:, pl.ds(pl.multiple_of(k * depth, depth), depth)]
        parts = []
        for r in range(0, tok, 16):
            x = held[k, r : r + 16].astype(F32)
            sq = x * x
            total = squares[r : r + 16]
            for j in range(0, depth, LANES):
                total = total + sq[:, j : j + LANES]
            squares[r : r + 16] = total
            parts.append((x * scale).astype(BF16))
        scaled = jnp.concatenate(parts, axis=0)
        held[k] = scaled
        acc_kv[...] += dot(scaled, w_kv[k])

    inv = lax.rsqrt(jnp.sum(squares[...], axis=1, keepdims=True) / width + 1e-06)
    proj_kv[...] = acc_kv[...] * inv
    pl.semaphore_wait(barrier, pairs - pair + side * jnp.minimum(pairs - 1 - pair, 1))

    def near_copy(i, source, target, device):
        return pltpu.make_async_remote_copy(
            src_ref=source, dst_ref=target, send_sem=near_send.at[i], recv_sem=near_recv.at[i],
            device_id=(device,), device_id_type=MESH,
        )

    before, first = pl.ds(0, EDGE), pl.ds(EDGE, EDGE)
    last = proj_kv.at[pl.ds(tok - EDGE, EDGE)]
    halo = near_copy(0, last, lead.at[before], following)
    far_halo = near_copy(1, last, other_lead.at[before], lax.rem(me + 2, n))
    heading = near_copy(2, proj_kv.at[before], other_lead.at[first], sibling)
    swap = near_copy(3, mine_state, other_state, sibling)
    q_halo = near_copy(4, proj_q.at[pl.ds(tok, EDGE)], proj_q.at[before], following)
    has_next = me < n - 1
    sends_far = jnp.logical_and(side == 1, has_next)

    @pl.when(has_next)
    def _():
        halo.start()

    @pl.when(sends_far)
    def _():
        far_halo.start()

    @pl.when(side == 0)
    def _():
        heading.start()

    lead[EDGE:] = proj_kv[:EDGE]

    @pl.when(me == 0)
    def _():
        lead[:EDGE] = jnp.zeros((EDGE, 2 * chan), F32)
        proj_q[:EDGE] = jnp.zeros((EDGE, chan), F32)

    @pl.when(me == 1)
    def _():
        other_lead[:EDGE] = jnp.zeros((EDGE, 2 * chan), F32)

    def feature(buf, r, rows, first, tap_first):
        total = jnp.zeros((rows, chan), F32)
        for t in range(taps.shape[0]):
            total = total + taps[t : t + 1, tap_first : tap_first + chan] * buf[
                pl.ds(r - t, rows), first : first + chan
            ]
        return total

    def key_value(buf, r, rows):
        keyed = feature(buf, r, rows, 0, chan)
        valued = feature(buf, r, rows, chan, 2 * chan)
        return (keyed * valued).astype(BF16)

    def edge_state(product):
        total = jnp.zeros((modes, chan), F32)
        for r in range(EDGE):
            total = total + edge_fall[r] * product[r : r + 1].astype(F32)
        return total

    def query_step(k):
        q_copy(k).wait()
        acc_q[...] += dot(held[k], w_q[k])

    tiles = tok // LANES
    causal = iota((LANES, LANES), 0) >= iota((LANES, LANES), 1)
    def toeplitz_step(g):
        first = jnp.broadcast_to(lag_row[pl.ds(g, 1)], (LANES, tok))
        moved = pltpu.roll(first, 0, 1, stride=1, stride_axis=0)
        lags = []
        for i in range(tiles):
            at = (tiles - i) % tiles * LANES
            tile = moved[:, at : at + LANES]
            lags.append((jnp.where(causal, tile, 0.0) if i == 0 else tile).astype(BF16))
        for i in range(tiles):
            for j in range(tiles):
                value = lags[i - j] if i >= j else jnp.zeros((LANES, LANES), BF16)
                toeplitz[g, i * LANES : (i + 1) * LANES, j * LANES : (j + 1) * LANES] = value

    zeros = jnp.zeros((EDGE, chan), BF16)
    prod[:32] = jnp.concatenate([zeros, key_value(proj_kv, EDGE, 32 - EDGE)], axis=0)
    for r in range(32, tok, 32):
        prod[r : r + 32] = key_value(proj_kv, r, 32)

    both = dot(fall[...], prod[...])
    wide = both[:every] + both[every:]
    group_of = iota((modes, chan), 1) // per_group
    packed = jnp.zeros((modes, chan), F32)
    for g in range(groups):
        packed = packed + jnp.where(group_of == g, wide[g * modes : (g + 1) * modes], 0.0)

    @pl.when(side == 0)
    def _():
        mine_state[...] = packed
        swap.start()

    pl.loop(0, groups // 2)(toeplitz_step)

    @pl.when(side == 1)
    def _():
        halo.wait_recv()
        rows = key_value(lead, EDGE, EDGE)
        prod[:EDGE] = rows
        mine_state[...] = packed + edge_state(rows)
        swap.start()

    pl.loop(groups // 2, groups)(toeplitz_step)

    early = chunks // 2
    pl.loop(0, early)(query_step)
    decay = jnp.exp(-rate_mc * float(tok))

    @pl.when(jnp.logical_and(side == 0, me > 0))
    def _():
        halo.wait_recv()

    @pl.when(side == 0)
    def _():
        rows = key_value(lead, EDGE, EDGE)
        prod[:EDGE] = rows
        whole = packed + edge_state(rows)
        swap.wait_recv()
        own[...] = (decay * whole + other_state[...]).astype(BF16)

    @pl.when(jnp.logical_and(side == 1, pair > 0))
    def _():
        far_halo.wait_recv()

    @pl.when(side == 1)
    def _():
        heading.wait_recv()
        swap.wait_recv()
        whole = other_state[...] + edge_state(key_value(other_lead, EDGE, EDGE))
        even_state[...] = whole
        own[...] = (decay * whole + mine_state[...]).astype(BF16)

    def state_copy(source, target):
        return pltpu.make_async_remote_copy(
            src_ref=own, dst_ref=slots.at[source],
            send_sem=send_sem.at[target], recv_sem=recv_sem.at[source],
            device_id=(2 * target + side,), device_id_type=MESH,
        )

    @pl.loop(0, pairs - 1 - pair)
    def _(i):
        state_copy(pair, pairs - 1 - i).start()

    pl.loop(early, chunks)(query_step)

    proj_q[EDGE:] = acc_q[...] * inv

    @pl.when(has_next)
    def _():
        q_halo.start()

    product = prod[...]
    channel_group = iota((tok, chan), 1) // per_group
    block = 2 * LANES

    def convolve(some):
        total = []
        for s0 in range(0, tok, block):
            s1 = min(s0 + block, tok)
            here = None
            for g in some:
                part = jnp.where(channel_group[s0:s1] == g, product[s0:s1], jnp.zeros_like(product[s0:s1]))
                term = dot(toeplitz[g, s0:, s0:s1], part)
                here = term if here is None else here + term
            total.append((s0, here))
        return total

    def add(parts):
        for s0, value in parts:
            acc_q[s0:] += value

    acc_q[...] = skip[...] * product.astype(F32)
    add(convolve(range(groups // 2)))

    for r in range(32, tok, 32):
        feat_q[r : r + 32] = feature(proj_q, EDGE + r, 32, 0, 0)
    add(convolve(range(groups // 2, groups)))

    pair_decay = jnp.exp(-rate_mc * float(2 * tok))

    def gather(p, state):
        state_copy(p, pair).wait_recv()
        return pair_decay * state + slots[p].astype(F32)

    @pl.when(me > 0)
    def _():
        q_halo.wait_recv()

    feat_q[:32] = feature(proj_q, EDGE, 32, 0, 0)
    state = lax.fori_loop(0, pair, gather, jnp.zeros((modes, chan), F32))
    state = jnp.where(side == 1, decay * state + even_state[...], state) * weight_mc
    stacked = jnp.concatenate([state] * groups, axis=0)
    same = iota((every, chan), 0) // modes == iota((every, chan), 1) // per_group
    high, low = split(jnp.where(same, stacked, 0.0))
    far = dot(rise[...], jnp.concatenate([high, high], axis=0)) + dot(rise[:, :every], low)
    out[...] = (feat_q[...] * (acc_q[...] + far)).astype(BF16)

    out_copy.wait()

    swap.wait_send()

    @pl.when(has_next)
    def _():
        halo.wait_send()
        q_halo.wait_send()

    @pl.when(sends_far)
    def _():
        far_halo.wait_send()

    @pl.when(side == 0)
    def _():
        heading.wait_send()

    @pl.loop(pair + 1, pairs)
    def _(p):
        state_copy(pair, p).wait_send()


def project_out(gated, w_out, mixed, held, sem):
    parts, _, block = held.shape

    def copy(k):
        return pltpu.make_async_copy(held.at[k], mixed.at[:, pl.ds(k * block, block)], sem.at[k])

    for k in range(parts):
        held[k] = dot(gated[...], w_out[:, k * block : (k + 1) * block]).astype(BF16)
        copy(k).start()
    for k in range(parts):
        copy(k).wait()


def on_device(n, hidden, norm_gain, w_in, w_short, residues, rates, skip, w_out):
    tok, width = hidden.shape
    chan = w_short.shape[0] // 3
    groups, modes = rates.shape
    every = groups * modes
    depth = min(1024, width)
    chunks = width // depth
    vmem = pl.BlockSpec(memory_space=pltpu.VMEM)
    in_hbm = pl.BlockSpec(memory_space=pltpu.HBM)
    gated, w_out_near = pl.pallas_call(
        functools.partial(mixer, n, depth),
        out_shape=[pltpu.VMEM((tok, chan), BF16), pltpu.VMEM((chan, width), BF16)],
        in_specs=[in_hbm] * 8,
        out_specs=[vmem, vmem],
        scratch_shapes=[
            pltpu.VMEM((1, width), F32),
            pltpu.VMEM((w_short.shape[1], 3 * chan), F32),
            pltpu.VMEM((groups, modes), F32),
            pltpu.VMEM((groups, modes), F32),
            pltpu.VMEM((1, chan), F32),
            pltpu.VMEM((chunks, tok, depth), BF16),
            pltpu.VMEM((chunks, depth, 2 * chan), BF16),
            pltpu.VMEM((chunks, depth, chan), BF16),
            pltpu.VMEM((tok, 2 * chan), F32),
            pltpu.VMEM((tok, chan), F32),
            pltpu.VMEM((tok, LANES), F32),
            pltpu.VMEM((tok, 2 * chan), F32),
            pltpu.VMEM((EDGE + tok, chan), F32),
            pltpu.VMEM((tok, chan), BF16),
            pltpu.VMEM((tok, chan), F32),
            pltpu.VMEM((2 * every, tok), BF16),
            pltpu.VMEM((tok, 2 * every), BF16),
            pltpu.VMEM((groups, tok), F32),
            pltpu.VMEM((groups, tok, tok), BF16),
            pltpu.VMEM((2 * EDGE, 2 * chan), F32),
            pltpu.VMEM((2 * EDGE, 2 * chan), F32),
            pltpu.VMEM((EDGE, modes, chan), F32),
            pltpu.VMEM((modes, chan), F32),
            pltpu.VMEM((modes, chan), F32),
            pltpu.VMEM((modes, chan), F32),
            pltpu.VMEM((modes, chan), BF16),
            pltpu.VMEM((n // 2, modes, chan), BF16),
            pltpu.SemaphoreType.DMA((chunks,)),
            pltpu.SemaphoreType.DMA((chunks,)),
            pltpu.SemaphoreType.DMA((chunks,)),
            pltpu.SemaphoreType.DMA((5,)),
            pltpu.SemaphoreType.DMA((5,)),
            pltpu.SemaphoreType.DMA((n // 2,)),
            pltpu.SemaphoreType.DMA((n // 2,)),
            pltpu.SemaphoreType.DMA,
            pltpu.SemaphoreType.DMA((5,)),
        ],
        compiler_params=pltpu.CompilerParams(
            collective_id=0, has_side_effects=True, vmem_limit_bytes=48 * 1024 * 1024
        ),
        name="mixer",
        cost_estimate=pl.CostEstimate(
            flops=2 * tok * width * 3 * chan, bytes_accessed=2 * width * (tok + 3 * chan), transcendentals=0
        ),
    )(
        hidden, w_in, w_out,
        *(
            pltpu.with_memory_space_constraint(x, pltpu.HBM)
            for x in (norm_gain.reshape(1, width), w_short.T, rates, residues, skip.reshape(1, chan))
        ),
    )
    parts = 16
    return pl.pallas_call(
        project_out,
        out_shape=jax.ShapeDtypeStruct((tok, width), BF16),
        in_specs=[vmem, vmem],
        out_specs=in_hbm,
        scratch_shapes=[
            pltpu.VMEM((parts, tok, width // parts), BF16),
            pltpu.SemaphoreType.DMA((parts,)),
        ],
        name="project_out",
        compiler_params=pltpu.CompilerParams(vmem_limit_bytes=24 * 1024 * 1024),
        cost_estimate=pl.CostEstimate(
            flops=2 * tok * width * chan, bytes_accessed=2 * width * (tok + chan), transcendentals=0
        ),
    )(gated, w_out_near)


def solution(mesh):
    return jax.shard_map(
        functools.partial(on_device, mesh.shape["tm"]),
        mesh=mesh,
        in_specs=(P("tm", None), P(), P(), P(), P(), P(), P(), P()),
        out_specs=P("tm", None),
        check_vma=False,
    )
```

```python
import functools

import jax
import jax.numpy as jnp
from jax import lax
from jax.experimental import pallas as pl
from jax.experimental.pallas import tpu as pltpu
from jax.sharding import PartitionSpec as P

HIGHEST = lax.Precision.HIGHEST
MESH = pl.DeviceIdType.MESH
LANES = 128
EDGE = 8
TAIL = 16
F32 = jnp.float32
BF16 = jnp.bfloat16


def iota(shape, dim):
    return lax.broadcasted_iota(jnp.int32, shape, dim)


def dot(a, b):
    return jnp.dot(a, b, preferred_element_type=F32)


def split(x):
    high = x.astype(BF16)
    return high, (x - high.astype(F32)).astype(BF16)


def mixer(
    n, depth, hidden, w_in, w_out, gain_far, taps_far, rates_far, residues_far, skip_far, out, w_out_near,
    gain, taps, rates, residues, skip,
    held, w_kv, w_q, acc_kv, acc_q, squares, proj_kv, proj_q, prod, feat_q,
    fall, rise, lag_row, toeplitz, lead, other_lead, edge_fall, mine_state, other_state, even_state, own, slots,
    held_sem, kv_sem, q_sem, tail_sem, near_send, near_recv, send_sem, recv_sem, out_sem, small_sem,
):
    me = lax.axis_index("tm")
    following = lax.rem(me + 1, n)
    pairs = n // 2
    pair, side = me // 2, lax.rem(me, 2)
    sibling = me + 1 - 2 * side
    tok, width = hidden.shape
    chan = prod.shape[1]
    groups, modes = rates.shape
    every = groups * modes
    per_group = chan // groups
    chunks = width // depth

    small = [
        pltpu.make_async_copy(source, target, small_sem.at[i])
        for i, (source, target) in enumerate(
            [(rates_far, rates), (residues_far, residues), (gain_far, gain), (taps_far, taps), (skip_far, skip)]
        )
    ]
    for copy in small:
        copy.start()

    late = chunks // 2
    body = tok - TAIL

    def held_copy(k):
        cols = pl.ds(pl.multiple_of(k * depth, depth), depth)
        if k < late:
            return pltpu.make_async_copy(hidden.at[:, cols], held.at[k], held_sem.at[k])
        rows = pl.ds(0, body)
        return pltpu.make_async_copy(hidden.at[rows, cols], held.at[k, rows], held_sem.at[k])

    def tail_copy(k):
        cols = pl.ds(pl.multiple_of(k * depth, depth), depth)
        rows = pl.ds(body, TAIL)
        return pltpu.make_async_copy(hidden.at[rows, cols], held.at[k, rows], tail_sem.at[k])

    def kv_copy(k):
        rows = pl.ds(pl.multiple_of(k * depth, depth), depth)
        return pltpu.make_async_copy(w_in.at[rows, pl.ds(chan, 2 * chan)], w_kv.at[k], kv_sem.at[k])

    def q_copy(k):
        rows = pl.ds(pl.multiple_of(k * depth, depth), depth)
        return pltpu.make_async_copy(w_in.at[rows, pl.ds(0, chan)], w_q.at[k], q_sem.at[k])

    for k in range(chunks):
        kv_copy(k).start()
        (held_copy if k < late else tail_copy)(k).start()
    for k in range(late, chunks):
        held_copy(k).start()

    @pl.loop(0, chunks)
    def _(k):
        q_copy(k).start(priority=1)

    out_copy = pltpu.make_async_copy(w_out, w_out_near, out_sem)
    out_copy.start(priority=1)

    barrier = pltpu.get_barrier_semaphore()

    def greet(d):
        pl.semaphore_signal(barrier, inc=1, device_id=(d,), device_id_type=MESH)

    @pl.loop(0, pair)
    def _(p):
        greet(2 * p + side)

    greet(sibling)

    @pl.when(jnp.logical_and(side == 0, pair > 0))
    def _():
        greet(me - 1)

    for copy in small:
        copy.wait()

    pick = (iota((modes, every), 1) % modes == iota((modes, every), 0)).astype(F32)
    mine = iota((groups, every), 1) // modes == iota((groups, every), 0)
    spread = (iota((groups, chan), 1) // per_group == iota((groups, chan), 0)).astype(F32)
    diagonal = iota((every, every), 0) == iota((every, every), 1)
    weights = residues[...] * jnp.sqrt(2.0 * rates[...])

    def as_row(x):
        wide = jnp.dot(x, pick, precision=HIGHEST, preferred_element_type=F32)
        return jnp.sum(jnp.where(mine, wide, 0.0), axis=0, keepdims=True)

    def as_column(row):
        return jnp.sum(jnp.where(diagonal, row, 0.0), axis=1, keepdims=True)

    def by_channel(x):
        return lax.dot_general(
            x, spread, (((0,), (0,)), ((), ())), precision=HIGHEST, preferred_element_type=F32
        )

    rate_row = as_row(rates[...])
    rate_col = as_column(rate_row)
    weight_col = as_column(as_row(weights))
    rate_mc = by_channel(rates[...])
    weight_mc = by_channel(weights)
    tiles = tok // LANES
    causal = iota((LANES, LANES), 0) >= iota((LANES, LANES), 1)

    def make_fall():
        high, low = split(jnp.exp(-rate_col * (tok - 1 - iota((every, tok), 1)).astype(F32)))
        early_rows = iota((every, tok), 1) < EDGE
        fall[:every] = jnp.where(early_rows, jnp.zeros_like(high), high)
        fall[every:] = jnp.where(early_rows, jnp.zeros_like(low), low)

    def make_rise():
        high, low = split(jnp.exp(-rate_row * (iota((tok, every), 0) + 1).astype(F32)))
        rise[:, :every], rise[:, every:] = high, low

    def make_lags():
        for r in range(EDGE):
            edge_fall[r] = jnp.exp(-rate_mc * float(tok - 1 - r))
        back = lax.rem(tok - iota((every, tok), 1), tok).astype(F32)
        terms = weight_col * jnp.exp(-rate_col * back)
        for g in range(groups):
            lag_row[g : g + 1] = jnp.sum(terms[g * modes : (g + 1) * modes], axis=0, keepdims=True)

    def make_toeplitz(some):
        for g in some:
            top = jnp.broadcast_to(lag_row[g : g + 1], (LANES, tok))
            moved = pltpu.roll(top, 0, 1, stride=1, stride_axis=0)
            lags = []
            for i in range(tiles):
                at = (tiles - i) % tiles * LANES
                tile = moved[:, at : at + LANES]
                lags.append((jnp.where(causal, tile, 0.0) if i == 0 else tile).astype(BF16))
            for i in range(tiles):
                for j in range(tiles):
                    value = lags[i - j] if i >= j else jnp.zeros((LANES, LANES), BF16)
                    toeplitz[g, i * LANES : (i + 1) * LANES, j * LANES : (j + 1) * LANES] = value

    even_state[...] = jnp.zeros_like(even_state)

    def ingest(k, first, stop):
        scale = gain[:, k * depth : (k + 1) * depth]
        parts = []
        for r in range(first, stop, 16):
            x = held[k, r : r + 16].astype(F32)
            sq = x * x
            total = sq[:, :LANES] if k == 0 else squares[r : r + 16] + sq[:, :LANES]
            for j in range(LANES, depth, LANES):
                total = total + sq[:, j : j + LANES]
            squares[r : r + 16] = total
            parts.append((x * scale).astype(BF16))
        scaled = jnp.concatenate(parts, axis=0)
        held[k, first:stop] = scaled
        if k == 0:
            acc_kv[first:stop] = dot(scaled, w_kv[k])
        else:
            acc_kv[first:stop] += dot(scaled, w_kv[k])

    jobs = [make_lags, make_fall] + [functools.partial(make_toeplitz, [g]) for g in range(groups)]
    where = [k for k in range(chunks) if 0 < k < chunks - 1] or [0]

    def beside(k):
        for i, job in enumerate(jobs):
            if where[i * len(where) // len(jobs)] == k:
                job()

    for k in range(late):
        held_copy(k).wait()
        kv_copy(k).wait()
        ingest(k, 0, tok)
        beside(k)
    for k in range(late, chunks):
        kv_copy(k).wait()
        tail_copy(k).wait()
        ingest(k, body, tok)

    def inverse(rows):
        return lax.rsqrt(jnp.sum(squares[rows], axis=1, keepdims=True) / width + 1e-06)

    tail_inv = inverse(slice(body, tok))
    proj_kv[body:] = acc_kv[body:] * tail_inv
    pl.semaphore_wait(barrier, pairs - pair + side * jnp.minimum(pairs - 1 - pair, 1))

    def near_copy(i, source, target, device):
        return pltpu.make_async_remote_copy(
            src_ref=source, dst_ref=target, send_sem=near_send.at[i], recv_sem=near_recv.at[i],
            device_id=(device,), device_id_type=MESH,
        )

    before, first = pl.ds(0, EDGE), pl.ds(EDGE, EDGE)
    last = proj_kv.at[pl.ds(tok - EDGE, EDGE)]
    halo = near_copy(0, last, lead.at[before], following)
    far_halo = near_copy(1, last, other_lead.at[before], lax.rem(me + 2, n))
    heading = near_copy(2, proj_kv.at[before], other_lead.at[first], sibling)
    swap = near_copy(3, mine_state, other_state, sibling)
    q_halo = near_copy(4, proj_q.at[pl.ds(tok, EDGE)], proj_q.at[before], following)
    has_next = me < n - 1
    sends_far = jnp.logical_and(side == 1, has_next)

    @pl.when(has_next)
    def _():
        halo.start()

    @pl.when(sends_far)
    def _():
        far_halo.start()

    for k in range(late, chunks):
        held_copy(k).wait()
        ingest(k, 0, body)
        beside(k)

    inv = jnp.concatenate([inverse(slice(0, body)), tail_inv], axis=0)
    proj_kv[:body] = acc_kv[:body] * inv[:body]

    @pl.when(side == 0)
    def _():
        heading.start()

    lead[EDGE:] = proj_kv[:EDGE]

    @pl.when(me == 0)
    def _():
        lead[:EDGE] = jnp.zeros((EDGE, 2 * chan), F32)
        proj_q[:EDGE] = jnp.zeros((EDGE, chan), F32)

    @pl.when(me == 1)
    def _():
        other_lead[:EDGE] = jnp.zeros((EDGE, 2 * chan), F32)

    def feature(buf, r, rows, first, tap_first):
        total = jnp.zeros((rows, chan), F32)
        for t in range(taps.shape[0]):
            total = total + taps[t : t + 1, tap_first : tap_first + chan] * buf[
                pl.ds(r - t, rows), first : first + chan
            ]
        return total

    def key_value(buf, r, rows):
        keyed = feature(buf, r, rows, 0, chan)
        valued = feature(buf, r, rows, chan, 2 * chan)
        return (keyed * valued).astype(BF16)

    def edge_state(product):
        total = jnp.zeros((modes, chan), F32)
        for r in range(EDGE):
            total = total + edge_fall[r] * product[r : r + 1].astype(F32)
        return total

    half = tok // 2

    def query_steps(some, first):
        for k in some:
            q_copy(k).wait()
        for r in (0, half):
            total = None
            for k in some:
                term = dot(held[k, r : r + half], w_q[k])
                total = term if total is None else total + term
            acc_q[r : r + half] = total if first else acc_q[r : r + half] + total

    zeros = jnp.zeros((EDGE, chan), BF16)
    prod[:32] = jnp.concatenate([zeros, key_value(proj_kv, EDGE, 32 - EDGE)], axis=0)
    for r in range(32, tok, 32):
        prod[r : r + 32] = key_value(proj_kv, r, 32)

    wide = dot(fall[:every], prod[...]) + dot(fall[every:], prod[...])
    group_of = iota((modes, chan), 1) // per_group
    packed = jnp.zeros((modes, chan), F32)
    for g in range(groups):
        packed = packed + jnp.where(group_of == g, wide[g * modes : (g + 1) * modes], 0.0)

    @pl.when(side == 0)
    def _():
        mine_state[...] = packed
        swap.start()

    @pl.when(side == 1)
    def _():
        halo.wait_recv()
        rows = key_value(lead, EDGE, EDGE)
        prod[:EDGE] = rows
        mine_state[...] = packed + edge_state(rows)
        swap.start()

    early = max(1, chunks // 4)
    query_steps(range(early), True)
    decay = jnp.exp(-rate_mc * float(tok))

    @pl.when(jnp.logical_and(side == 0, me > 0))
    def _():
        halo.wait_recv()

    @pl.when(side == 0)
    def _():
        rows = key_value(lead, EDGE, EDGE)
        prod[:EDGE] = rows
        whole = packed + edge_state(rows)
        swap.wait_recv()
        own[...] = (decay * whole + other_state[...]).astype(BF16)

    @pl.when(jnp.logical_and(side == 1, pair > 0))
    def _():
        far_halo.wait_recv()

    @pl.when(side == 1)
    def _():
        heading.wait_recv()
        swap.wait_recv()
        whole = other_state[...] + edge_state(key_value(other_lead, EDGE, EDGE))
        even_state[...] = whole
        own[...] = (decay * whole + mine_state[...]).astype(BF16)

    def state_copy(source, target):
        return pltpu.make_async_remote_copy(
            src_ref=own, dst_ref=slots.at[source],
            send_sem=send_sem.at[target], recv_sem=recv_sem.at[source],
            device_id=(2 * target + side,), device_id_type=MESH,
        )

    @pl.loop(0, pairs - 1 - pair)
    def _(i):
        state_copy(pair, pairs - 1 - i).start()

    query_steps(range(early, chunks), False)
    proj_q[EDGE:] = acc_q[...] * inv

    @pl.when(has_next)
    def _():
        q_halo.start()

    product = prod[...]
    channel_group = iota((tok, chan), 1) // per_group
    block = 2 * LANES

    def convolve(some):
        for s0 in range(0, tok, block):
            s1 = min(s0 + block, tok)
            parts = [
                jnp.where(channel_group[s0:s1] == g, product[s0:s1], jnp.zeros_like(product[s0:s1])) for g in some
            ]
            step = (tok - s0) // 2
            for r in (s0, s0 + step):
                total = None
                for g, part in zip(some, parts):
                    term = dot(toeplitz[g, r : r + step, s0:s1], part)
                    total = term if total is None else total + term
                acc_q[r : r + step] += total

    acc_q[...] = skip[...] * product.astype(F32)
    convolve(range(groups // 2))
    make_rise()

    for r in range(32, tok, 32):
        feat_q[r : r + 32] = feature(proj_q, EDGE + r, 32, 0, 0)
    convolve(range(groups // 2, groups))

    pair_decay = jnp.exp(-rate_mc * float(2 * tok))

    def gather(p, state):
        state_copy(p, pair).wait_recv()
        return pair_decay * state + slots[p].astype(F32)

    @pl.when(me > 0)
    def _():
        q_halo.wait_recv()

    feat_q[:32] = feature(proj_q, EDGE, 32, 0, 0)
    state = lax.fori_loop(0, pair, gather, jnp.zeros((modes, chan), F32))
    state = jnp.where(side == 1, decay * state + even_state[...], state) * weight_mc
    stacked = jnp.concatenate([state] * groups, axis=0)
    same = iota((every, chan), 0) // modes == iota((every, chan), 1) // per_group
    high, low = split(jnp.where(same, stacked, 0.0))
    paired = jnp.concatenate([high, high], axis=0)
    for r in (0, half):
        rows = slice(r, r + half)
        far = dot(rise[rows], paired) + dot(rise[rows, :every], low)
        out[rows] = (feat_q[rows] * (acc_q[rows] + far)).astype(BF16)

    out_copy.wait()

    swap.wait_send()

    @pl.when(has_next)
    def _():
        halo.wait_send()
        q_halo.wait_send()

    @pl.when(sends_far)
    def _():
        far_halo.wait_send()

    @pl.when(side == 0)
    def _():
        heading.wait_send()

    @pl.loop(pair + 1, pairs)
    def _(p):
        state_copy(pair, p).wait_send()


def project_out(gated, w_out, mixed, held, sem):
    parts, _, block = held.shape

    def copy(k):
        return pltpu.make_async_copy(held.at[k], mixed.at[:, pl.ds(k * block, block)], sem.at[k])

    for k in range(parts):
        held[k] = dot(gated[...], w_out[:, k * block : (k + 1) * block]).astype(BF16)
        copy(k).start()
    for k in range(parts):
        copy(k).wait()


def on_device(n, hidden, norm_gain, w_in, w_short, residues, rates, skip, w_out):
    tok, width = hidden.shape
    chan = w_short.shape[0] // 3
    groups, modes = rates.shape
    every = groups * modes
    depth = min(1024, width)
    chunks = width // depth
    vmem = pl.BlockSpec(memory_space=pltpu.VMEM)
    in_hbm = pl.BlockSpec(memory_space=pltpu.HBM)
    gated, w_out_near = pl.pallas_call(
        functools.partial(mixer, n, depth),
        out_shape=[pltpu.VMEM((tok, chan), BF16), pltpu.VMEM((chan, width), BF16)],
        in_specs=[in_hbm] * 8,
        out_specs=[vmem, vmem],
        scratch_shapes=[
            pltpu.VMEM((1, width), F32),
            pltpu.VMEM((w_short.shape[1], 3 * chan), F32),
            pltpu.VMEM((groups, modes), F32),
            pltpu.VMEM((groups, modes), F32),
            pltpu.VMEM((1, chan), F32),
            pltpu.VMEM((chunks, tok, depth), BF16),
            pltpu.VMEM((chunks, depth, 2 * chan), BF16),
            pltpu.VMEM((chunks, depth, chan), BF16),
            pltpu.VMEM((tok, 2 * chan), F32),
            pltpu.VMEM((tok, chan), F32),
            pltpu.VMEM((tok, LANES), F32),
            pltpu.VMEM((tok, 2 * chan), F32),
            pltpu.VMEM((EDGE + tok, chan), F32),
            pltpu.VMEM((tok, chan), BF16),
            pltpu.VMEM((tok, chan), F32),
            pltpu.VMEM((2 * every, tok), BF16),
            pltpu.VMEM((tok, 2 * every), BF16),
            pltpu.VMEM((groups, tok), F32),
            pltpu.VMEM((groups, tok, tok), BF16),
            pltpu.VMEM((2 * EDGE, 2 * chan), F32),
            pltpu.VMEM((2 * EDGE, 2 * chan), F32),
            pltpu.VMEM((EDGE, modes, chan), F32),
            pltpu.VMEM((modes, chan), F32),
            pltpu.VMEM((modes, chan), F32),
            pltpu.VMEM((modes, chan), F32),
            pltpu.VMEM((modes, chan), BF16),
            pltpu.VMEM((n // 2, modes, chan), BF16),
            pltpu.SemaphoreType.DMA((chunks,)),
            pltpu.SemaphoreType.DMA((chunks,)),
            pltpu.SemaphoreType.DMA((chunks,)),
            pltpu.SemaphoreType.DMA((chunks,)),
            pltpu.SemaphoreType.DMA((5,)),
            pltpu.SemaphoreType.DMA((5,)),
            pltpu.SemaphoreType.DMA((n // 2,)),
            pltpu.SemaphoreType.DMA((n // 2,)),
            pltpu.SemaphoreType.DMA,
            pltpu.SemaphoreType.DMA((5,)),
        ],
        compiler_params=pltpu.CompilerParams(
            collective_id=0, has_side_effects=True, vmem_limit_bytes=48 * 1024 * 1024
        ),
        name="mixer",
        cost_estimate=pl.CostEstimate(
            flops=2 * tok * width * 3 * chan, bytes_accessed=2 * width * (tok + 3 * chan), transcendentals=0
        ),
    )(
        hidden, w_in, w_out,
        *(
            pltpu.with_memory_space_constraint(x, pltpu.HBM)
            for x in (norm_gain.reshape(1, width), w_short.T, rates, residues, skip.reshape(1, chan))
        ),
    )
    parts = 16
    return pl.pallas_call(
        project_out,
        out_shape=jax.ShapeDtypeStruct((tok, width), BF16),
        in_specs=[vmem, vmem],
        out_specs=in_hbm,
        scratch_shapes=[
            pltpu.VMEM((parts, tok, width // parts), BF16),
            pltpu.SemaphoreType.DMA((parts,)),
        ],
        name="project_out",
        compiler_params=pltpu.CompilerParams(vmem_limit_bytes=24 * 1024 * 1024),
        cost_estimate=pl.CostEstimate(
            flops=2 * tok * width * chan, bytes_accessed=2 * width * (tok + chan), transcendentals=0
        ),
    )(gated, w_out_near)


def solution(mesh):
    return jax.shard_map(
        functools.partial(on_device, mesh.shape["tm"]),
        mesh=mesh,
        in_specs=(P("tm", None), P(), P(), P(), P(), P(), P(), P()),
        out_specs=P("tm", None),
        check_vma=False,
    )
```

```python
import functools

import jax
import jax.numpy as jnp
from jax import lax
from jax.experimental import pallas as pl
from jax.experimental.pallas import tpu as pltpu
from jax.sharding import PartitionSpec as P

HIGHEST = lax.Precision.HIGHEST
MESH = pl.DeviceIdType.MESH
LANES = 128
EDGE = 8
TAIL = 16
GROUP = 3
F32 = jnp.float32
BF16 = jnp.bfloat16


def iota(shape, dim):
    return lax.broadcasted_iota(jnp.int32, shape, dim)


def dot(a, b):
    return jnp.dot(a, b, preferred_element_type=F32)


def split(x):
    high = x.astype(BF16)
    return high, (x - high.astype(F32)).astype(BF16)


def mixer(
    n, depth, hidden, w_in, w_out, gain_far, taps_far, rates_far, residues_far, skip_far, out, w_out_near,
    gain, taps, rates, residues, skip,
    held, w_kv, w_q, tail, acc_kv, acc_q, squares, proj_kv, proj_q, prod, feat_q,
    fall, rise, lag_row, toeplitz, lead, other_lead, edge_fall, mine_state, other_state, even_state, own, slots,
    held_sem, kv_sem, q_sem, tail_sem, near_send, near_recv, send_sem, recv_sem, out_sem, small_sem,
):
    me = lax.axis_index("tm")
    following = lax.rem(me + 1, n)
    pairs = n // 2
    pair, side = me // 2, lax.rem(me, 2)
    sibling = me + 1 - 2 * side
    tok, width = hidden.shape
    chan = prod.shape[1]
    groups, modes = rates.shape
    every = groups * modes
    per_group = chan // groups
    chunks = width // depth

    small = [
        pltpu.make_async_copy(source, target, small_sem.at[i])
        for i, (source, target) in enumerate(
            [(rates_far, rates), (residues_far, residues), (gain_far, gain), (taps_far, taps), (skip_far, skip)]
        )
    ]
    for copy in small:
        copy.start()

    late = chunks * 5 // 8
    body = tok - TAIL

    def held_copy(k, rows):
        rows, cols = pl.ds(0, rows), pl.ds(pl.multiple_of(k * depth, depth), depth)
        return pltpu.make_async_copy(hidden.at[rows, cols], held.at[k, rows], held_sem.at[k])

    tail_copy = pltpu.make_async_copy(
        hidden.at[pl.ds(body, TAIL), pl.ds(late * depth, width - late * depth)], tail, tail_sem
    )

    def kv_copy(k):
        rows = pl.ds(pl.multiple_of(k * depth, depth), depth)
        return pltpu.make_async_copy(w_in.at[rows, pl.ds(chan, 2 * chan)], w_kv.at[k], kv_sem.at[k])

    parts = 2 if chunks % 2 == 0 else 1
    deep = width // parts

    def q_copy(i):
        rows = pl.ds(i * deep, deep)
        return pltpu.make_async_copy(w_in.at[rows, pl.ds(0, chan)], w_q.at[rows], q_sem.at[i])

    @pl.loop(0, late)
    def _(k):
        held_copy(k, tok).start()
        kv_copy(k).start()

    tail_copy.start()

    @pl.loop(late, chunks)
    def _(k):
        kv_copy(k).start()

    @pl.loop(late, chunks)
    def _(k):
        held_copy(k, body).start()

    out_copy = pltpu.make_async_copy(w_out, w_out_near, out_sem)

    barrier = pltpu.get_barrier_semaphore()

    def greet(d):
        pl.semaphore_signal(barrier, inc=1, device_id=(d,), device_id_type=MESH)

    @pl.loop(0, pair)
    def _(p):
        greet(2 * p + side)

    greet(sibling)

    @pl.when(jnp.logical_and(side == 0, pair > 0))
    def _():
        greet(me - 1)

    for copy in small:
        copy.wait()

    pick = (iota((modes, every), 1) % modes == iota((modes, every), 0)).astype(F32)
    mine = iota((groups, every), 1) // modes == iota((groups, every), 0)
    spread = (iota((groups, chan), 1) // per_group == iota((groups, chan), 0)).astype(F32)
    diagonal = iota((every, every), 0) == iota((every, every), 1)
    weights = residues[...] * jnp.sqrt(2.0 * rates[...])

    def as_row(x):
        wide = jnp.dot(x, pick, precision=HIGHEST, preferred_element_type=F32)
        return jnp.sum(jnp.where(mine, wide, 0.0), axis=0, keepdims=True)

    def as_column(row):
        return jnp.sum(jnp.where(diagonal, row, 0.0), axis=1, keepdims=True)

    def by_channel(x):
        return lax.dot_general(
            x, spread, (((0,), (0,)), ((), ())), precision=HIGHEST, preferred_element_type=F32
        )

    rate_row = as_row(rates[...])
    rate_col = as_column(rate_row)
    weight_col = as_column(as_row(weights))
    rate_mc = by_channel(rates[...])
    weight_mc = by_channel(weights)
    tiles = tok // LANES
    causal = iota((LANES, LANES), 0) >= iota((LANES, LANES), 1)

    def make_fall():
        high, low = split(jnp.exp(-rate_col * (tok - 1 - iota((every, tok), 1)).astype(F32)))
        early_rows = iota((every, tok), 1) < EDGE
        fall[:every] = jnp.where(early_rows, jnp.zeros_like(high), high)
        fall[every:] = jnp.where(early_rows, jnp.zeros_like(low), low)

    def make_rise():
        high, low = split(jnp.exp(-rate_row * (iota((tok, every), 0) + 1).astype(F32)))
        rise[:, :every], rise[:, every:] = high, low

    def make_lags():
        for r in range(EDGE):
            edge_fall[r] = jnp.exp(-rate_mc * float(tok - 1 - r))
        back = lax.rem(tok - iota((every, tok), 1), tok).astype(F32)
        terms = weight_col * jnp.exp(-rate_col * back)
        for g in range(groups):
            lag_row[g : g + 1] = jnp.sum(terms[g * modes : (g + 1) * modes], axis=0, keepdims=True)

    def make_toeplitz(some):
        for g in some:
            top = jnp.broadcast_to(lag_row[g : g + 1], (LANES, tok))
            moved = pltpu.roll(top, 0, 1, stride=1, stride_axis=0)
            lags = []
            for i in range(tiles):
                at = (tiles - i) % tiles * LANES
                tile = moved[:, at : at + LANES]
                lags.append((jnp.where(causal, tile, 0.0) if i == 0 else tile).astype(BF16))
            for i in range(tiles):
                for j in range(tiles):
                    value = lags[i - j] if i >= j else jnp.zeros((LANES, LANES), BF16)
                    toeplitz[g, i * LANES : (i + 1) * LANES, j * LANES : (j + 1) * LANES] = value

    even_state[...] = jnp.zeros_like(even_state)

    def ingest(k, first, stop):
        scale = gain[:, k * depth : (k + 1) * depth]
        parts = []
        for r in range(first, stop, 16):
            x = held[k, r : r + 16].astype(F32)
            sq = x * x
            total = sq[:, :LANES] if k == 0 else squares[r : r + 16] + sq[:, :LANES]
            for j in range(LANES, depth, LANES):
                total = total + sq[:, j : j + LANES]
            squares[r : r + 16] = total
            parts.append((x * scale).astype(BF16))
        scaled = jnp.concatenate(parts, axis=0)
        held[k, first:stop] = scaled
        if k == 0:
            acc_kv[first:stop] = dot(scaled, w_kv[k])
        else:
            acc_kv[first:stop] += dot(scaled, w_kv[k])

    jobs = [make_lags, make_fall] + [functools.partial(make_toeplitz, [g]) for g in range(groups)]
    where = [k for k in range(chunks) if 0 < k < chunks - 1] or [0]

    def beside(k):
        for i, job in enumerate(jobs):
            if where[i * len(where) // len(jobs)] == k:
                job()

    for k in range(late):
        held_copy(k, tok).wait()
        kv_copy(k).wait()
        ingest(k, 0, tok)
        beside(k)
    for i in range(parts):
        q_copy(i).start(priority=1)
    out_copy.start(priority=1)
    tail_copy.wait()
    for k in range(late, chunks):
        held[k, body:] = tail[:, (k - late) * depth : (k - late + 1) * depth]
    for k in range(late, chunks):
        kv_copy(k).wait()
        ingest(k, body, tok)

    def inverse(rows):
        return lax.rsqrt(jnp.sum(squares[rows], axis=1, keepdims=True) / width + 1e-06)

    tail_inv = inverse(slice(body, tok))
    proj_kv[body:] = acc_kv[body:] * tail_inv
    pl.semaphore_wait(barrier, pairs - pair + side * jnp.minimum(pairs - 1 - pair, 1))

    def near_copy(i, source, target, device):
        return pltpu.make_async_remote_copy(
            src_ref=source, dst_ref=target, send_sem=near_send.at[i], recv_sem=near_recv.at[i],
            device_id=(device,), device_id_type=MESH,
        )

    before, first = pl.ds(0, EDGE), pl.ds(EDGE, EDGE)
    last = proj_kv.at[pl.ds(tok - EDGE, EDGE)]
    halo = near_copy(0, last, lead.at[before], following)
    far_halo = near_copy(1, last, other_lead.at[before], lax.rem(me + 2, n))
    heading = near_copy(2, proj_kv.at[before], other_lead.at[first], sibling)
    swap = near_copy(3, mine_state, other_state, sibling)
    q_halo = near_copy(4, proj_q.at[pl.ds(tok, EDGE)], proj_q.at[before], following)
    has_next = me < n - 1
    sends_far = jnp.logical_and(side == 1, has_next)

    @pl.when(has_next)
    def _():
        halo.start()

    @pl.when(sends_far)
    def _():
        far_halo.start()

    for k in range(late, chunks):
        held_copy(k, body).wait()
        ingest(k, 0, body)
        beside(k)

    inv = jnp.concatenate([inverse(slice(0, body)), tail_inv], axis=0)
    proj_kv[:body] = acc_kv[:body] * inv[:body]

    @pl.when(side == 0)
    def _():
        heading.start()

    lead[EDGE:] = proj_kv[:EDGE]

    @pl.when(me == 0)
    def _():
        lead[:EDGE] = jnp.zeros((EDGE, 2 * chan), F32)
        proj_q[:EDGE] = jnp.zeros((EDGE, chan), F32)

    @pl.when(me == 1)
    def _():
        other_lead[:EDGE] = jnp.zeros((EDGE, 2 * chan), F32)

    def feature(buf, r, rows, first, tap_first):
        shifted = [buf[pl.ds(r - EDGE, EDGE + rows), first : first + chan]]
        for i in range(1, GROUP):
            shifted.append(pltpu.roll(shifted[0], i, 0))
        total = None
        for t in reversed(range(0, taps.shape[0], GROUP)):
            if total is not None:
                total = pltpu.roll(total, GROUP, 0)
            for i in range(min(GROUP, taps.shape[0] - t)):
                term = taps[t + i : t + i + 1, tap_first : tap_first + chan] * shifted[i]
                total = term if total is None else total + term
        return total[EDGE:]

    def key_value(buf, r, rows):
        keyed = feature(buf, r, rows, 0, chan)
        valued = feature(buf, r, rows, chan, 2 * chan)
        return (keyed * valued).astype(BF16)

    def edge_state(product):
        total = jnp.zeros((modes, chan), F32)
        for r in range(EDGE):
            total = total + edge_fall[r] * product[r : r + 1].astype(F32)
        return total

    half = tok // 2

    def query_steps(some, first):
        for i in range(parts):
            if any(k * depth == i * deep for k in some):
                q_copy(i).wait()
        for r in (0, half):
            total = None
            for k in some:
                term = dot(held[k, r : r + half], w_q[k * depth : (k + 1) * depth])
                total = term if total is None else total + term
            acc_q[r : r + half] = total if first else acc_q[r : r + half] + total

    zeros = jnp.zeros((EDGE, chan), BF16)
    strip = 64 if tok % 64 == 0 else 32
    prod[:strip] = jnp.concatenate([zeros, key_value(proj_kv, EDGE, strip - EDGE)], axis=0)
    for r in range(strip, tok, strip):
        prod[r : r + strip] = key_value(proj_kv, r, strip)

    wide = dot(fall[:every], prod[...]) + dot(fall[every:], prod[...])
    group_of = iota((modes, chan), 1) // per_group
    packed = jnp.zeros((modes, chan), F32)
    for g in range(groups):
        packed = packed + jnp.where(group_of == g, wide[g * modes : (g + 1) * modes], 0.0)

    @pl.when(side == 0)
    def _():
        mine_state[...] = packed
        swap.start()

    @pl.when(side == 1)
    def _():
        halo.wait_recv()
        rows = key_value(lead, EDGE, EDGE)
        prod[:EDGE] = rows
        mine_state[...] = packed + edge_state(rows)
        swap.start()

    early = max(1, chunks * 3 // 8)
    query_steps(range(early), True)
    decay = jnp.exp(-rate_mc * float(tok))

    @pl.when(jnp.logical_and(side == 0, me > 0))
    def _():
        halo.wait_recv()

    @pl.when(side == 0)
    def _():
        rows = key_value(lead, EDGE, EDGE)
        prod[:EDGE] = rows
        whole = packed + edge_state(rows)
        swap.wait_recv()
        own[...] = (decay * whole + other_state[...]).astype(BF16)

    @pl.when(jnp.logical_and(side == 1, pair > 0))
    def _():
        far_halo.wait_recv()

    @pl.when(side == 1)
    def _():
        heading.wait_recv()
        swap.wait_recv()
        whole = other_state[...] + edge_state(key_value(other_lead, EDGE, EDGE))
        even_state[...] = whole
        own[...] = (decay * whole + mine_state[...]).astype(BF16)

    def state_copy(source, target):
        return pltpu.make_async_remote_copy(
            src_ref=own, dst_ref=slots.at[source],
            send_sem=send_sem.at[target], recv_sem=recv_sem.at[source],
            device_id=(2 * target + side,), device_id_type=MESH,
        )

    @pl.loop(0, pairs - 1 - pair)
    def _(i):
        state_copy(pair, pairs - 1 - i).start()

    query_steps(range(early, chunks), False)
    proj_q[EDGE:] = acc_q[...] * inv

    @pl.when(has_next)
    def _():
        q_halo.start()

    product = prod[...]
    channel_group = iota((tok, chan), 1) // per_group
    block = 2 * LANES

    def convolve(some):
        for s0 in range(0, tok, block):
            s1 = min(s0 + block, tok)
            parts = [
                jnp.where(channel_group[s0:s1] == g, product[s0:s1], jnp.zeros_like(product[s0:s1])) for g in some
            ]
            step = (tok - s0) // 2
            for r in (s0, s0 + step):
                total = None
                for g, part in zip(some, parts):
                    term = dot(toeplitz[g, r : r + step, s0:s1], part)
                    total = term if total is None else total + term
                acc_q[r : r + step] += total

    acc_q[...] = skip[...] * product.astype(F32)
    convolve(range(groups // 2))
    make_rise()

    for r in range(strip, tok, strip):
        feat_q[r : r + strip] = feature(proj_q, EDGE + r, strip, 0, 0)
    convolve(range(groups // 2, groups))

    pair_decay = jnp.exp(-rate_mc * float(2 * tok))

    def gather(p, state):
        state_copy(p, pair).wait_recv()
        return pair_decay * state + slots[p].astype(F32)

    @pl.when(me > 0)
    def _():
        q_halo.wait_recv()

    feat_q[:strip] = feature(proj_q, EDGE, strip, 0, 0)
    state = lax.fori_loop(0, pair, gather, jnp.zeros((modes, chan), F32))
    state = jnp.where(side == 1, decay * state + even_state[...], state) * weight_mc
    stacked = jnp.concatenate([state] * groups, axis=0)
    same = iota((every, chan), 0) // modes == iota((every, chan), 1) // per_group
    high, low = split(jnp.where(same, stacked, 0.0))
    paired = jnp.concatenate([high, high], axis=0)
    for r in (0, half):
        rows = slice(r, r + half)
        far = dot(rise[rows], paired) + dot(rise[rows, :every], low)
        out[rows] = (feat_q[rows] * (acc_q[rows] + far)).astype(BF16)

    out_copy.wait()

    swap.wait_send()

    @pl.when(has_next)
    def _():
        halo.wait_send()
        q_halo.wait_send()

    @pl.when(sends_far)
    def _():
        far_halo.wait_send()

    @pl.when(side == 0)
    def _():
        heading.wait_send()

    @pl.loop(pair + 1, pairs)
    def _(p):
        state_copy(pair, p).wait_send()


def project_out(gated, w_out, mixed, held, sem):
    parts, _, block = held.shape

    def copy(k):
        return pltpu.make_async_copy(held.at[k], mixed.at[:, pl.ds(k * block, block)], sem.at[k])

    for k in range(parts):
        held[k] = dot(gated[...], w_out[:, k * block : (k + 1) * block]).astype(BF16)
        copy(k).start()
    for k in range(parts):
        copy(k).wait()


def on_device(n, hidden, norm_gain, w_in, w_short, residues, rates, skip, w_out):
    tok, width = hidden.shape
    chan = w_short.shape[0] // 3
    groups, modes = rates.shape
    every = groups * modes
    depth = min(1024, width)
    chunks = width // depth
    vmem = pl.BlockSpec(memory_space=pltpu.VMEM)
    in_hbm = pl.BlockSpec(memory_space=pltpu.HBM)
    gated, w_out_near = pl.pallas_call(
        functools.partial(mixer, n, depth),
        out_shape=[pltpu.VMEM((tok, chan), BF16), pltpu.VMEM((chan, width), BF16)],
        in_specs=[in_hbm] * 8,
        out_specs=[vmem, vmem],
        scratch_shapes=[
            pltpu.VMEM((1, width), F32),
            pltpu.VMEM((w_short.shape[1], 3 * chan), F32),
            pltpu.VMEM((groups, modes), F32),
            pltpu.VMEM((groups, modes), F32),
            pltpu.VMEM((1, chan), F32),
            pltpu.VMEM((chunks, tok, depth), BF16),
            pltpu.VMEM((chunks, depth, 2 * chan), BF16),
            pltpu.VMEM((width, chan), BF16),
            pltpu.VMEM((TAIL, width - chunks * 5 // 8 * depth), BF16),
            pltpu.VMEM((tok, 2 * chan), F32),
            pltpu.VMEM((tok, chan), F32),
            pltpu.VMEM((tok, LANES), F32),
            pltpu.VMEM((tok, 2 * chan), F32),
            pltpu.VMEM((EDGE + tok, chan), F32),
            pltpu.VMEM((tok, chan), BF16),
            pltpu.VMEM((tok, chan), F32),
            pltpu.VMEM((2 * every, tok), BF16),
            pltpu.VMEM((tok, 2 * every), BF16),
            pltpu.VMEM((groups, tok), F32),
            pltpu.VMEM((groups, tok, tok), BF16),
            pltpu.VMEM((2 * EDGE, 2 * chan), F32),
            pltpu.VMEM((2 * EDGE, 2 * chan), F32),
            pltpu.VMEM((EDGE, modes, chan), F32),
            pltpu.VMEM((modes, chan), F32),
            pltpu.VMEM((modes, chan), F32),
            pltpu.VMEM((modes, chan), F32),
            pltpu.VMEM((modes, chan), BF16),
            pltpu.VMEM((n // 2, modes, chan), BF16),
            pltpu.SemaphoreType.DMA((chunks,)),
            pltpu.SemaphoreType.DMA((chunks,)),
            pltpu.SemaphoreType.DMA((2,)),
            pltpu.SemaphoreType.DMA,
            pltpu.SemaphoreType.DMA((5,)),
            pltpu.SemaphoreType.DMA((5,)),
            pltpu.SemaphoreType.DMA((n // 2,)),
            pltpu.SemaphoreType.DMA((n // 2,)),
            pltpu.SemaphoreType.DMA,
            pltpu.SemaphoreType.DMA((5,)),
        ],
        compiler_params=pltpu.CompilerParams(
            collective_id=0, has_side_effects=True, vmem_limit_bytes=48 * 1024 * 1024
        ),
        name="mixer",
        cost_estimate=pl.CostEstimate(
            flops=2 * tok * width * 3 * chan, bytes_accessed=2 * width * (tok + 3 * chan), transcendentals=0
        ),
    )(
        hidden, w_in, w_out,
        *(
            pltpu.with_memory_space_constraint(x, pltpu.HBM)
            for x in (norm_gain.reshape(1, width), w_short.T, rates, residues, skip.reshape(1, chan))
        ),
    )
    parts = 16
    return pl.pallas_call(
        project_out,
        out_shape=jax.ShapeDtypeStruct((tok, width), BF16),
        in_specs=[vmem, vmem],
        out_specs=in_hbm,
        scratch_shapes=[
            pltpu.VMEM((parts, tok, width // parts), BF16),
            pltpu.SemaphoreType.DMA((parts,)),
        ],
        name="project_out",
        compiler_params=pltpu.CompilerParams(vmem_limit_bytes=24 * 1024 * 1024),
        cost_estimate=pl.CostEstimate(
            flops=2 * tok * width * chan, bytes_accessed=2 * width * (tok + chan), transcendentals=0
        ),
    )(gated, w_out_near)


def solution(mesh):
    return jax.shard_map(
        functools.partial(on_device, mesh.shape["tm"]),
        mesh=mesh,
        in_specs=(P("tm", None), P(), P(), P(), P(), P(), P(), P()),
        out_specs=P("tm", None),
        check_vma=False,
    )
```

```python
import functools

import jax
import jax.numpy as jnp
from jax import lax
from jax.experimental import pallas as pl
from jax.experimental.pallas import tpu as pltpu
from jax.sharding import PartitionSpec as P

HIGHEST = lax.Precision.HIGHEST
MESH = pl.DeviceIdType.MESH
LANES = 128
EDGE = 8
TAIL = 16
GROUP = 3
F32 = jnp.float32
BF16 = jnp.bfloat16


def iota(shape, dim):
    return lax.broadcasted_iota(jnp.int32, shape, dim)


def dot(a, b):
    return jnp.dot(a, b, preferred_element_type=F32)


def split(x):
    high = x.astype(BF16)
    return high, (x - high.astype(F32)).astype(BF16)


def mixer(
    n, depth, hidden, w_in, w_out, gain_far, taps_far, rates_far, residues_far, skip_far, out, w_out_near,
    gain, taps, rates, residues, skip,
    held, w_kv, w_q, tail, acc_kv, acc_q, squares, proj_kv, proj_q, prod, feat_q,
    fall, rise, lag_row, toeplitz, lead, other_lead, edge_fall, mine_state, other_state, even_state, own, slots,
    load_sem, q_sem, tail_sem, near_recv, recv_sem, out_sem, small_sem,
):
    me = lax.axis_index("tm")
    following = lax.rem(me + 1, n)
    pairs = n // 2
    pair, side = me // 2, lax.rem(me, 2)
    sibling = me + 1 - 2 * side
    tok, width = hidden.shape
    chan = prod.shape[1]
    groups, modes = rates.shape
    every = groups * modes
    per_group = chan // groups
    chunks = width // depth

    small = [
        pltpu.make_async_copy(source, target, small_sem.at[i])
        for i, (source, target) in enumerate(
            [(rates_far, rates), (residues_far, residues), (gain_far, gain), (taps_far, taps), (skip_far, skip)]
        )
    ]
    for copy in small:
        copy.start()

    late = chunks * 5 // 8
    body = tok - TAIL

    def held_copy(k, rows):
        rows, cols = pl.ds(0, rows), pl.ds(pl.multiple_of(k * depth, depth), depth)
        return pltpu.make_async_copy(hidden.at[rows, cols], held.at[k, rows], load_sem.at[k])

    tail_copy = pltpu.make_async_copy(
        hidden.at[pl.ds(body, TAIL), pl.ds(late * depth, width - late * depth)], tail, tail_sem
    )

    def kv_copy(k):
        rows = pl.ds(pl.multiple_of(k * depth, depth), depth)
        return pltpu.make_async_copy(w_in.at[rows, pl.ds(chan, 2 * chan)], w_kv.at[k], load_sem.at[chunks + k])

    parts = 2 if chunks % 2 == 0 else 1
    deep = width // parts

    def q_copy(i):
        rows = pl.ds(i * deep, deep)
        return pltpu.make_async_copy(w_in.at[rows, pl.ds(0, chan)], w_q.at[rows], q_sem.at[i])

    @pl.loop(0, late)
    def _(k):
        held_copy(k, tok).start()
        kv_copy(k).start()

    tail_copy.start()

    @pl.loop(late, chunks)
    def _(k):
        kv_copy(k).start()

    @pl.loop(late, chunks)
    def _(k):
        held_copy(k, body).start()

    out_copy = pltpu.make_async_copy(w_out, w_out_near, out_sem)

    barrier = pltpu.get_barrier_semaphore()

    def greet(d):
        pl.semaphore_signal(barrier, inc=1, device_id=(d,), device_id_type=MESH)

    @pl.loop(0, pair)
    def _(p):
        greet(2 * p + side)

    greet(sibling)

    @pl.when(jnp.logical_and(side == 0, pair > 0))
    def _():
        greet(me - 1)

    for copy in small:
        copy.wait()

    pick = (iota((modes, every), 1) % modes == iota((modes, every), 0)).astype(F32)
    mine = iota((groups, every), 1) // modes == iota((groups, every), 0)
    spread = (iota((groups, chan), 1) // per_group == iota((groups, chan), 0)).astype(F32)
    diagonal = iota((every, every), 0) == iota((every, every), 1)
    weights = residues[...] * jnp.sqrt(2.0 * rates[...])

    def as_row(x):
        wide = jnp.dot(x, pick, precision=HIGHEST, preferred_element_type=F32)
        return jnp.sum(jnp.where(mine, wide, 0.0), axis=0, keepdims=True)

    def as_column(row):
        return jnp.sum(jnp.where(diagonal, row, 0.0), axis=1, keepdims=True)

    def by_channel(x):
        return lax.dot_general(
            x, spread, (((0,), (0,)), ((), ())), precision=HIGHEST, preferred_element_type=F32
        )

    rate_row = as_row(rates[...])
    rate_col = as_column(rate_row)
    weight_col = as_column(as_row(weights))
    rate_mc = by_channel(rates[...])
    weight_mc = by_channel(weights)
    tiles = tok // LANES
    causal = iota((LANES, LANES), 0) >= iota((LANES, LANES), 1)

    def make_fall():
        high, low = split(jnp.exp(-rate_col * (tok - 1 - iota((every, tok), 1)).astype(F32)))
        early_rows = iota((every, tok), 1) < EDGE
        fall[:every] = jnp.where(early_rows, jnp.zeros_like(high), high)
        fall[every:] = jnp.where(early_rows, jnp.zeros_like(low), low)

    def make_rise():
        high, low = split(jnp.exp(-rate_row * (iota((tok, every), 0) + 1).astype(F32)))
        rise[:, :every], rise[:, every:] = high, low

    def make_lags():
        for r in range(EDGE):
            edge_fall[r] = jnp.exp(-rate_mc * float(tok - 1 - r))
        back = lax.rem(tok - iota((every, tok), 1), tok).astype(F32)
        terms = weight_col * jnp.exp(-rate_col * back)
        for g in range(groups):
            lag_row[g : g + 1] = jnp.sum(terms[g * modes : (g + 1) * modes], axis=0, keepdims=True)

    def make_toeplitz(some):
        for g in some:
            top = jnp.broadcast_to(lag_row[g : g + 1], (LANES, tok))
            moved = pltpu.roll(top, 0, 1, stride=1, stride_axis=0)
            lags = []
            for i in range(tiles):
                at = (tiles - i) % tiles * LANES
                tile = moved[:, at : at + LANES]
                lags.append((jnp.where(causal, tile, 0.0) if i == 0 else tile).astype(BF16))
            for i in range(tiles):
                for j in range(tiles):
                    value = lags[i - j] if i >= j else jnp.zeros((LANES, LANES), BF16)
                    toeplitz[g, i * LANES : (i + 1) * LANES, j * LANES : (j + 1) * LANES] = value

    even_state[...] = jnp.zeros_like(even_state)

    def ingest(k, first, stop):
        scale = gain[:, k * depth : (k + 1) * depth]
        parts = []
        for r in range(first, stop, 16):
            x = held[k, r : r + 16].astype(F32)
            sq = x * x
            total = sq[:, :LANES] if k == 0 else squares[r : r + 16] + sq[:, :LANES]
            for j in range(LANES, depth, LANES):
                total = total + sq[:, j : j + LANES]
            squares[r : r + 16] = total
            parts.append((x * scale).astype(BF16))
        scaled = jnp.concatenate(parts, axis=0)
        held[k, first:stop] = scaled
        if k == 0:
            acc_kv[first:stop] = dot(scaled, w_kv[k])
        else:
            acc_kv[first:stop] += dot(scaled, w_kv[k])

    jobs = [make_lags, make_fall] + [functools.partial(make_toeplitz, [g]) for g in range(groups)]
    where = [k for k in range(late) if k > 0] or [0]

    def beside(k):
        for i, job in enumerate(jobs):
            if where[i * len(where) // len(jobs)] == k:
                job()

    for k in range(late):
        held_copy(k, tok).wait()
        kv_copy(k).wait()
        ingest(k, 0, tok)
        beside(k)
    for i in range(parts):
        q_copy(i).start(priority=1)
    out_copy.start(priority=1)
    tail_copy.wait()
    for k in range(late, chunks):
        held[k, body:] = tail[:, (k - late) * depth : (k - late + 1) * depth]
    for k in range(late, chunks):
        kv_copy(k).wait()
        ingest(k, body, tok)

    def inverse(rows):
        return lax.rsqrt(jnp.sum(squares[rows], axis=1, keepdims=True) / width + 1e-06)

    tail_inv = inverse(slice(body, tok))
    proj_kv[body:] = acc_kv[body:] * tail_inv
    pl.semaphore_wait(barrier, pairs - pair + side * jnp.minimum(pairs - 1 - pair, 1))

    def near_copy(i, source, target, device):
        return pltpu.make_async_remote_copy(
            src_ref=source, dst_ref=target, send_sem=small_sem.at[i], recv_sem=near_recv.at[i],
            device_id=(device,), device_id_type=MESH,
        )

    before, first = pl.ds(0, EDGE), pl.ds(EDGE, EDGE)
    last = proj_kv.at[pl.ds(tok - EDGE, EDGE)]
    halo = near_copy(0, last, lead.at[before], following)
    far_halo = near_copy(1, last, other_lead.at[before], lax.rem(me + 2, n))
    heading = near_copy(2, proj_kv.at[before], other_lead.at[first], sibling)
    swap = near_copy(3, mine_state, other_state, sibling)
    q_halo = near_copy(4, proj_q.at[pl.ds(tok, EDGE)], proj_q.at[before], following)
    has_next = me < n - 1
    sends_far = jnp.logical_and(side == 1, has_next)

    @pl.when(has_next)
    def _():
        halo.start()

    @pl.when(sends_far)
    def _():
        far_halo.start()

    def feature(buf, r, rows, first, tap_first):
        shifted = [buf[pl.ds(r - EDGE, EDGE + rows), first : first + chan]]
        for i in range(1, GROUP):
            shifted.append(pltpu.roll(shifted[0], i, 0))
        total = None
        for t in reversed(range(0, taps.shape[0], GROUP)):
            if total is not None:
                total = pltpu.roll(total, GROUP, 0)
            for i in range(min(GROUP, taps.shape[0] - t)):
                term = taps[t + i : t + i + 1, tap_first : tap_first + chan] * shifted[i]
                total = term if total is None else total + term
        return total[EDGE:]

    def key_value(buf, r, rows):
        keyed = feature(buf, r, rows, 0, chan)
        valued = feature(buf, r, rows, chan, 2 * chan)
        return (keyed * valued).astype(BF16)

    def edge_state(product):
        total = jnp.zeros((modes, chan), F32)
        for r in range(EDGE):
            total = total + edge_fall[r] * product[r : r + 1].astype(F32)
        return total

    strip = 64 if tok % 64 == 0 else 32
    mid = tok // 2 // strip * strip
    zeros = jnp.zeros((EDGE, chan), BF16)
    for k in range(late, chunks):
        held_copy(k, body).wait()
        ingest(k, 0, mid)
    for k in range(late, chunks):
        ingest(k, mid, body)
    top_inv = inverse(slice(0, mid))
    proj_kv[:mid] = acc_kv[:mid] * top_inv
    prod[:strip] = jnp.concatenate([zeros, key_value(proj_kv, EDGE, strip - EDGE)], axis=0)
    for r in range(strip, mid, strip):
        prod[r : r + strip] = key_value(proj_kv, r, strip)

    low_inv = inverse(slice(mid, body))
    proj_kv[mid:body] = acc_kv[mid:body] * low_inv
    inv = jnp.concatenate([top_inv, low_inv, tail_inv], axis=0)

    @pl.when(side == 0)
    def _():
        heading.start()

    lead[EDGE:] = proj_kv[:EDGE]

    @pl.when(me == 0)
    def _():
        lead[:EDGE] = jnp.zeros((EDGE, 2 * chan), F32)
        proj_q[:EDGE] = jnp.zeros((EDGE, chan), F32)

    @pl.when(me == 1)
    def _():
        other_lead[:EDGE] = jnp.zeros((EDGE, 2 * chan), F32)

    half = tok // 2

    quarter = tok // 4

    def query_steps(some, starts, first):
        for i in range(parts):
            if starts[0] > 0 and any(k * depth == i * deep for k in some):
                q_copy(i).wait()
        for r in starts:
            total = None
            for k in some:
                term = dot(held[k, r : r + quarter], w_q[k * depth : (k + 1) * depth])
                total = term if total is None else total + term
            acc_q[r : r + quarter] = total if first else acc_q[r : r + quarter] + total

    for r in range(mid, tok, strip):
        prod[r : r + strip] = key_value(proj_kv, r, strip)

    wide = []
    for m in (0, every // 2):
        low_part = dot(fall[every + m : every + m + every // 2], prod[...])
        wide.append(dot(fall[m : m + every // 2], prod[...]) + low_part)
    wide = jnp.concatenate(wide, axis=0)
    group_of = iota((modes, chan), 1) // per_group
    packed = jnp.zeros((modes, chan), F32)
    for g in range(groups):
        packed = packed + jnp.where(group_of == g, wide[g * modes : (g + 1) * modes], 0.0)

    @pl.when(side == 0)
    def _():
        mine_state[...] = packed
        swap.start()

    @pl.when(side == 1)
    def _():
        halo.wait_recv()
        rows = key_value(lead, EDGE, EDGE)
        prod[:EDGE] = rows
        mine_state[...] = packed + edge_state(rows)
        swap.start()

    early = max(1, chunks // 2)
    query_steps(range(early), (half, half + quarter), True)
    decay = jnp.exp(-rate_mc * float(tok))

    @pl.when(jnp.logical_and(side == 0, me > 0))
    def _():
        halo.wait_recv()

    @pl.when(side == 0)
    def _():
        rows = key_value(lead, EDGE, EDGE)
        prod[:EDGE] = rows
        whole = packed + edge_state(rows)
        swap.wait_recv()
        own[...] = (decay * whole + other_state[...]).astype(BF16)

    @pl.when(jnp.logical_and(side == 1, pair > 0))
    def _():
        far_halo.wait_recv()

    @pl.when(side == 1)
    def _():
        heading.wait_recv()
        swap.wait_recv()
        whole = other_state[...] + edge_state(key_value(other_lead, EDGE, EDGE))
        even_state[...] = whole
        own[...] = (decay * whole + mine_state[...]).astype(BF16)

    def state_copy(source, target):
        return pltpu.make_async_remote_copy(
            src_ref=own, dst_ref=slots.at[source],
            send_sem=load_sem.at[target], recv_sem=recv_sem.at[source],
            device_id=(2 * target + side,), device_id_type=MESH,
        )

    @pl.loop(0, pairs - 1 - pair)
    def _(i):
        state_copy(pair, pairs - 1 - i).start()

    if early < chunks:
        query_steps(range(early, chunks), (half, half + quarter), False)
    proj_q[EDGE + half :] = acc_q[half:] * inv[half:]

    @pl.when(has_next)
    def _():
        q_halo.start()

    query_steps(range(chunks), (0, quarter), True)
    proj_q[EDGE : EDGE + half] = acc_q[:half] * inv[:half]

    product = prod[...]
    channel_group = iota((tok, chan), 1) // per_group
    block = 2 * LANES

    def convolve(some):
        for s0 in range(0, tok, block):
            s1 = min(s0 + block, tok)
            parts = [
                jnp.where(channel_group[s0:s1] == g, product[s0:s1], jnp.zeros_like(product[s0:s1])) for g in some
            ]
            step = (tok - s0) // 2
            for r in (s0, s0 + step):
                total = None
                for g, part in zip(some, parts):
                    term = dot(toeplitz[g, r : r + step, s0:s1], part)
                    total = term if total is None else total + term
                acc_q[r : r + step] += total

    acc_q[...] = skip[...] * product.astype(F32)
    convolve(range(groups // 2))
    make_rise()

    for r in range(strip, tok, strip):
        feat_q[r : r + strip] = feature(proj_q, EDGE + r, strip, 0, 0)
    convolve(range(groups // 2, groups))

    pair_decay = jnp.exp(-rate_mc * float(2 * tok))

    def gather(p, state):
        state_copy(p, pair).wait_recv()
        return pair_decay * state + slots[p].astype(F32)

    @pl.when(me > 0)
    def _():
        q_halo.wait_recv()

    feat_q[:strip] = feature(proj_q, EDGE, strip, 0, 0)
    state = lax.fori_loop(0, pair, gather, jnp.zeros((modes, chan), F32))
    state = jnp.where(side == 1, decay * state + even_state[...], state) * weight_mc
    stacked = jnp.concatenate([state] * groups, axis=0)
    same = iota((every, chan), 0) // modes == iota((every, chan), 1) // per_group
    high, low = split(jnp.where(same, stacked, 0.0))
    paired = jnp.concatenate([high, high], axis=0)
    for r in (0, half):
        rows = slice(r, r + half)
        far = dot(rise[rows], paired) + dot(rise[rows, :every], low)
        out[rows] = (feat_q[rows] * (acc_q[rows] + far)).astype(BF16)

    out_copy.wait()

    swap.wait_send()

    @pl.when(has_next)
    def _():
        halo.wait_send()
        q_halo.wait_send()

    @pl.when(sends_far)
    def _():
        far_halo.wait_send()

    @pl.when(side == 0)
    def _():
        heading.wait_send()

    @pl.loop(pair + 1, pairs)
    def _(p):
        state_copy(pair, p).wait_send()


def project_out(gated, w_out, mixed, held, sem):
    parts, _, block = held.shape

    def copy(k):
        return pltpu.make_async_copy(held.at[k], mixed.at[:, pl.ds(k * block, block)], sem.at[k])

    for k in range(parts):
        held[k] = dot(gated[...], w_out[:, k * block : (k + 1) * block]).astype(BF16)
        copy(k).start()
    for k in range(parts):
        copy(k).wait()


def on_device(n, hidden, norm_gain, w_in, w_short, residues, rates, skip, w_out):
    tok, width = hidden.shape
    chan = w_short.shape[0] // 3
    groups, modes = rates.shape
    every = groups * modes
    depth = min(1024, width)
    chunks = width // depth
    vmem = pl.BlockSpec(memory_space=pltpu.VMEM)
    in_hbm = pl.BlockSpec(memory_space=pltpu.HBM)
    gated, w_out_near = pl.pallas_call(
        functools.partial(mixer, n, depth),
        out_shape=[pltpu.VMEM((tok, chan), BF16), pltpu.VMEM((chan, width), BF16)],
        in_specs=[in_hbm] * 8,
        out_specs=[vmem, vmem],
        scratch_shapes=[
            pltpu.VMEM((1, width), F32),
            pltpu.VMEM((w_short.shape[1], 3 * chan), F32),
            pltpu.VMEM((groups, modes), F32),
            pltpu.VMEM((groups, modes), F32),
            pltpu.VMEM((1, chan), F32),
            pltpu.VMEM((chunks, tok, depth), BF16),
            pltpu.VMEM((chunks, depth, 2 * chan), BF16),
            pltpu.VMEM((width, chan), BF16),
            pltpu.VMEM((TAIL, width - chunks * 5 // 8 * depth), BF16),
            pltpu.VMEM((tok, 2 * chan), F32),
            pltpu.VMEM((tok, chan), F32),
            pltpu.VMEM((tok, LANES), F32),
            pltpu.VMEM((tok, 2 * chan), F32),
            pltpu.VMEM((EDGE + tok, chan), F32),
            pltpu.VMEM((tok, chan), BF16),
            pltpu.VMEM((tok, chan), F32),
            pltpu.VMEM((2 * every, tok), BF16),
            pltpu.VMEM((tok, 2 * every), BF16),
            pltpu.VMEM((groups, tok), F32),
            pltpu.VMEM((groups, tok, tok), BF16),
            pltpu.VMEM((2 * EDGE, 2 * chan), F32),
            pltpu.VMEM((2 * EDGE, 2 * chan), F32),
            pltpu.VMEM((EDGE, modes, chan), F32),
            pltpu.VMEM((modes, chan), F32),
            pltpu.VMEM((modes, chan), F32),
            pltpu.VMEM((modes, chan), F32),
            pltpu.VMEM((modes, chan), BF16),
            pltpu.VMEM((n // 2, modes, chan), BF16),
            pltpu.SemaphoreType.DMA((max(2 * chunks, n // 2),)),
            pltpu.SemaphoreType.DMA((2,)),
            pltpu.SemaphoreType.DMA,
            pltpu.SemaphoreType.DMA((5,)),
            pltpu.SemaphoreType.DMA((n // 2,)),
            pltpu.SemaphoreType.DMA,
            pltpu.SemaphoreType.DMA((5,)),
        ],
        compiler_params=pltpu.CompilerParams(
            collective_id=0, has_side_effects=True, vmem_limit_bytes=48 * 1024 * 1024
        ),
        name="mixer",
        cost_estimate=pl.CostEstimate(
            flops=2 * tok * width * 3 * chan, bytes_accessed=2 * width * (tok + 3 * chan), transcendentals=0
        ),
    )(
        hidden, w_in, w_out,
        *(
            pltpu.with_memory_space_constraint(x, pltpu.HBM)
            for x in (norm_gain.reshape(1, width), w_short.T, rates, residues, skip.reshape(1, chan))
        ),
    )
    parts = 16
    return pl.pallas_call(
        project_out,
        out_shape=jax.ShapeDtypeStruct((tok, width), BF16),
        in_specs=[vmem, vmem],
        out_specs=in_hbm,
        scratch_shapes=[
            pltpu.VMEM((parts, tok, width // parts), BF16),
            pltpu.SemaphoreType.DMA((parts,)),
        ],
        name="project_out",
        compiler_params=pltpu.CompilerParams(vmem_limit_bytes=24 * 1024 * 1024),
        cost_estimate=pl.CostEstimate(
            flops=2 * tok * width * chan, bytes_accessed=2 * width * (tok + chan), transcendentals=0
        ),
    )(gated, w_out_near)


def solution(mesh):
    return jax.shard_map(
        functools.partial(on_device, mesh.shape["tm"]),
        mesh=mesh,
        in_specs=(P("tm", None), P(), P(), P(), P(), P(), P(), P()),
        out_specs=P("tm", None),
        check_vma=False,
    )
```

```python
import functools

import jax
import jax.numpy as jnp
from jax import lax
from jax.experimental import pallas as pl
from jax.experimental.pallas import tpu as pltpu
from jax.sharding import PartitionSpec as P

HIGHEST = lax.Precision.HIGHEST
MESH = pl.DeviceIdType.MESH
LANES = 128
EDGE = 8
TAIL = 16
GROUP = 3
F32 = jnp.float32
BF16 = jnp.bfloat16


def iota(shape, dim):
    return lax.broadcasted_iota(jnp.int32, shape, dim)


def dot(a, b):
    return jnp.dot(a, b, preferred_element_type=F32)


def split(x):
    high = x.astype(BF16)
    return high, (x - high.astype(F32)).astype(BF16)


def mixer(
    n, depth, hidden, w_in, w_out, gain_far, taps_far, rates_far, residues_far, skip_far, out, w_out_near,
    gain, taps, rates, residues, skip,
    held, w_kv, w_q, tail, acc_kv, acc_q, squares, proj_kv, proj_q, prod, feat_q,
    fall, rise, lag_row, toeplitz, lead, other_lead, edge_fall, mine_state, other_state, even_state, own, slots, carried,
    load_sem, q_sem, tail_sem, near_recv, recv_sem, out_sem, small_sem,
):
    me = lax.axis_index("tm")
    following = lax.rem(me + 1, n)
    pairs = n // 2
    pair, side = me // 2, lax.rem(me, 2)
    sibling = me + 1 - 2 * side
    tok, width = hidden.shape
    chan = prod.shape[1]
    groups, modes = rates.shape
    every = groups * modes
    per_group = chan // groups
    chunks = width // depth

    small = [
        pltpu.make_async_copy(source, target, small_sem.at[i])
        for i, (source, target) in enumerate(
            [(rates_far, rates), (residues_far, residues), (gain_far, gain), (taps_far, taps), (skip_far, skip)]
        )
    ]
    for copy in small:
        copy.start()

    late = chunks * 5 // 8
    body = tok - TAIL

    def held_copy(k, rows):
        rows, cols = pl.ds(0, rows), pl.ds(pl.multiple_of(k * depth, depth), depth)
        return pltpu.make_async_copy(hidden.at[rows, cols], held.at[k, rows], load_sem.at[k])

    tail_copy = pltpu.make_async_copy(
        hidden.at[pl.ds(body, TAIL), pl.ds(late * depth, width - late * depth)], tail, tail_sem
    )

    def kv_copy(k):
        rows = pl.ds(pl.multiple_of(k * depth, depth), depth)
        return pltpu.make_async_copy(w_in.at[rows, pl.ds(chan, 2 * chan)], w_kv.at[k], load_sem.at[chunks + k])

    parts = 2 if chunks % 2 == 0 else 1
    deep = width // parts

    def q_copy(i):
        rows = pl.ds(i * deep, deep)
        return pltpu.make_async_copy(w_in.at[rows, pl.ds(0, chan)], w_q.at[rows], q_sem.at[i])

    @pl.loop(0, late)
    def _(k):
        held_copy(k, tok).start()
        kv_copy(k).start()

    tail_copy.start()

    @pl.loop(late, chunks)
    def _(k):
        kv_copy(k).start()

    @pl.loop(late, chunks)
    def _(k):
        held_copy(k, body).start()

    out_copy = pltpu.make_async_copy(w_out, w_out_near, out_sem)

    barrier = pltpu.get_barrier_semaphore()

    def greet(d):
        pl.semaphore_signal(barrier, inc=1, device_id=(d,), device_id_type=MESH)

    @pl.loop(0, pair)
    def _(p):
        greet(2 * p + side)

    greet(sibling)

    @pl.when(jnp.logical_and(side == 0, pair > 0))
    def _():
        greet(me - 1)

    for copy in small:
        copy.wait()

    pick = (iota((modes, every), 1) % modes == iota((modes, every), 0)).astype(F32)
    mine = iota((groups, every), 1) // modes == iota((groups, every), 0)
    spread = (iota((groups, chan), 1) // per_group == iota((groups, chan), 0)).astype(F32)
    diagonal = iota((every, every), 0) == iota((every, every), 1)
    weights = residues[...] * jnp.sqrt(2.0 * rates[...])

    def as_row(x):
        wide = jnp.dot(x, pick, precision=HIGHEST, preferred_element_type=F32)
        return jnp.sum(jnp.where(mine, wide, 0.0), axis=0, keepdims=True)

    def as_column(row):
        return jnp.sum(jnp.where(diagonal, row, 0.0), axis=1, keepdims=True)

    def by_channel(x):
        return lax.dot_general(
            x, spread, (((0,), (0,)), ((), ())), precision=HIGHEST, preferred_element_type=F32
        )

    rate_row = as_row(rates[...])
    rate_col = as_column(rate_row)
    weight_col = as_column(as_row(weights))
    rate_mc = by_channel(rates[...])
    weight_mc = by_channel(weights)
    tiles = tok // LANES
    causal = iota((LANES, LANES), 0) >= iota((LANES, LANES), 1)

    def make_fall():
        high, low = split(jnp.exp(-rate_col * (tok - 1 - iota((every, tok), 1)).astype(F32)))
        early_rows = iota((every, tok), 1) < EDGE
        fall[:every] = jnp.where(early_rows, jnp.zeros_like(high), high)
        fall[every:] = jnp.where(early_rows, jnp.zeros_like(low), low)

    def make_rise():
        high, low = split(jnp.exp(-rate_row * (iota((tok, every), 0) + 1).astype(F32)))
        rise[:, :every], rise[:, every:] = high, low

    def make_lags():
        for r in range(EDGE):
            edge_fall[r] = jnp.exp(-rate_mc * float(tok - 1 - r))
        back = lax.rem(tok - iota((every, tok), 1), tok).astype(F32)
        terms = weight_col * jnp.exp(-rate_col * back)
        for g in range(groups):
            lag_row[g : g + 1] = jnp.sum(terms[g * modes : (g + 1) * modes], axis=0, keepdims=True)

    def make_toeplitz(some):
        for g in some:
            top = jnp.broadcast_to(lag_row[g : g + 1], (LANES, tok))
            moved = pltpu.roll(top, 0, 1, stride=1, stride_axis=0)
            lags = []
            for i in range(tiles):
                at = (tiles - i) % tiles * LANES
                tile = moved[:, at : at + LANES]
                lags.append((jnp.where(causal, tile, 0.0) if i == 0 else tile).astype(BF16))
            for i in range(tiles):
                for j in range(tiles):
                    value = lags[i - j] if i >= j else jnp.zeros((LANES, LANES), BF16)
                    toeplitz[g, i * LANES : (i + 1) * LANES, j * LANES : (j + 1) * LANES] = value

    even_state[...] = jnp.zeros_like(even_state)

    def ingest(k, first, stop):
        scale = gain[:, k * depth : (k + 1) * depth]
        parts = []
        for r in range(first, stop, 16):
            x = held[k, r : r + 16].astype(F32)
            sq = x * x
            total = sq[:, :LANES] if k == 0 else squares[r : r + 16] + sq[:, :LANES]
            for j in range(LANES, depth, LANES):
                total = total + sq[:, j : j + LANES]
            squares[r : r + 16] = total
            parts.append((x * scale).astype(BF16))
        scaled = jnp.concatenate(parts, axis=0)
        held[k, first:stop] = scaled
        if k == 0:
            acc_kv[first:stop] = dot(scaled, w_kv[k])
        else:
            acc_kv[first:stop] += dot(scaled, w_kv[k])

    jobs = [make_lags, make_fall] + [functools.partial(make_toeplitz, [g]) for g in range(groups)]
    where = [k for k in range(late) if k > 0] or [0]

    def beside(k):
        for i, job in enumerate(jobs):
            if where[i * len(where) // len(jobs)] == k:
                job()

    for k in range(late):
        held_copy(k, tok).wait()
        kv_copy(k).wait()
        ingest(k, 0, tok)
        beside(k)
    for i in range(parts):
        q_copy(i).start(priority=1)
    out_copy.start(priority=1)
    tail_copy.wait()
    for k in range(late, chunks):
        held[k, body:] = tail[:, (k - late) * depth : (k - late + 1) * depth]
    for k in range(late, chunks):
        kv_copy(k).wait()
        ingest(k, body, tok)

    def inverse(rows):
        return lax.rsqrt(jnp.sum(squares[rows], axis=1, keepdims=True) / width + 1e-06)

    tail_inv = inverse(slice(body, tok))
    proj_kv[body:] = acc_kv[body:] * tail_inv
    pl.semaphore_wait(barrier, pairs - pair + side * jnp.minimum(pairs - 1 - pair, 1))

    def near_copy(i, source, target, device):
        return pltpu.make_async_remote_copy(
            src_ref=source, dst_ref=target, send_sem=small_sem.at[i], recv_sem=near_recv.at[i],
            device_id=(device,), device_id_type=MESH,
        )

    before, first = pl.ds(0, EDGE), pl.ds(EDGE, EDGE)
    last = proj_kv.at[pl.ds(tok - EDGE, EDGE)]
    halo = near_copy(0, last, lead.at[before], following)
    far_halo = near_copy(1, last, other_lead.at[before], lax.rem(me + 2, n))
    heading = near_copy(2, proj_kv.at[before], other_lead.at[first], sibling)
    swap = near_copy(3, mine_state, other_state, sibling)
    q_halo = near_copy(4, proj_q.at[pl.ds(tok, EDGE)], proj_q.at[before], following)
    has_next = me < n - 1
    sends_far = jnp.logical_and(side == 1, has_next)

    @pl.when(has_next)
    def _():
        halo.start()

    @pl.when(sends_far)
    def _():
        far_halo.start()

    def feature(buf, r, rows, first, tap_first):
        shifted = [buf[pl.ds(r - EDGE, EDGE + rows), first : first + chan]]
        for i in range(1, GROUP):
            shifted.append(pltpu.roll(shifted[0], i, 0))
        total = None
        for t in reversed(range(0, taps.shape[0], GROUP)):
            if total is not None:
                total = pltpu.roll(total, GROUP, 0)
            for i in range(min(GROUP, taps.shape[0] - t)):
                term = taps[t + i : t + i + 1, tap_first : tap_first + chan] * shifted[i]
                total = term if total is None else total + term
        return total[EDGE:]

    def key_value(buf, r, rows):
        keyed = feature(buf, r, rows, 0, chan)
        valued = feature(buf, r, rows, chan, 2 * chan)
        return (keyed * valued).astype(BF16)

    def edge_state(product):
        total = jnp.zeros((modes, chan), F32)
        for r in range(EDGE):
            total = total + edge_fall[r] * product[r : r + 1].astype(F32)
        return total

    strip = 64 if tok % 64 == 0 else 32
    mid = tok // 2 // strip * strip
    zeros = jnp.zeros((EDGE, chan), BF16)
    for k in range(late, chunks):
        held_copy(k, body).wait()
        ingest(k, 0, mid)
    for k in range(late, chunks):
        ingest(k, mid, body)
    top_inv = inverse(slice(0, mid))
    proj_kv[:mid] = acc_kv[:mid] * top_inv
    prod[:strip] = jnp.concatenate([zeros, key_value(proj_kv, EDGE, strip - EDGE)], axis=0)
    for r in range(strip, mid, strip):
        prod[r : r + strip] = key_value(proj_kv, r, strip)

    low_inv = inverse(slice(mid, body))
    proj_kv[mid:body] = acc_kv[mid:body] * low_inv
    inv = jnp.concatenate([top_inv, low_inv, tail_inv], axis=0)

    @pl.when(side == 0)
    def _():
        heading.start()

    lead[EDGE:] = proj_kv[:EDGE]

    @pl.when(me == 0)
    def _():
        lead[:EDGE] = jnp.zeros((EDGE, 2 * chan), F32)
        proj_q[:EDGE] = jnp.zeros((EDGE, chan), F32)

    @pl.when(me == 1)
    def _():
        other_lead[:EDGE] = jnp.zeros((EDGE, 2 * chan), F32)

    half = tok // 2

    quarter = tok // 4

    def query_steps(some, starts, first):
        for i in range(parts):
            if starts[0] > 0 and any(k * depth == i * deep for k in some):
                q_copy(i).wait()
        for r in starts:
            total = None
            for k in some:
                term = dot(held[k, r : r + quarter], w_q[k * depth : (k + 1) * depth])
                total = term if total is None else total + term
            acc_q[r : r + quarter] = total if first else acc_q[r : r + quarter] + total

    for r in range(mid, tok, strip):
        prod[r : r + strip] = key_value(proj_kv, r, strip)

    wide = []
    for m in (0, every // 2):
        low_part = dot(fall[every + m : every + m + every // 2], prod[...])
        wide.append(dot(fall[m : m + every // 2], prod[...]) + low_part)
    wide = jnp.concatenate(wide, axis=0)
    group_of = iota((modes, chan), 1) // per_group
    packed = jnp.zeros((modes, chan), F32)
    for g in range(groups):
        packed = packed + jnp.where(group_of == g, wide[g * modes : (g + 1) * modes], 0.0)

    @pl.when(side == 0)
    def _():
        mine_state[...] = packed
        swap.start()

    @pl.when(side == 1)
    def _():
        halo.wait_recv()
        rows = key_value(lead, EDGE, EDGE)
        prod[:EDGE] = rows
        mine_state[...] = packed + edge_state(rows)
        swap.start()

    early = max(1, chunks // 2)
    query_steps(range(early), (half, half + quarter), True)
    decay = jnp.exp(-rate_mc * float(tok))
    side_chan = chan // 2
    low_rows = (half, half + quarter)

    def finish_low():
        if early < chunks:
            query_steps(range(early, chunks), low_rows, False)
        proj_q[EDGE + half :] = acc_q[half:] * inv[half:]

    pl.when(side == 1)(finish_low)

    @pl.when(jnp.logical_and(side == 0, me > 0))
    def _():
        halo.wait_recv()

    @pl.when(side == 0)
    def _():
        rows = key_value(lead, EDGE, EDGE)
        prod[:EDGE] = rows
        whole = packed + edge_state(rows)
        swap.wait_recv()
        own[...] = (decay * whole + other_state[...])[:, :side_chan].astype(BF16)

    @pl.when(jnp.logical_and(side == 1, pair > 0))
    def _():
        far_halo.wait_recv()

    @pl.when(side == 1)
    def _():
        heading.wait_recv()
        swap.wait_recv()
        whole = other_state[...] + edge_state(key_value(other_lead, EDGE, EDGE))
        even_state[...] = whole
        own[...] = (decay * whole + mine_state[...])[:, side_chan:].astype(BF16)

    def state_copy(source, target):
        return pltpu.make_async_remote_copy(
            src_ref=own, dst_ref=slots.at[source],
            send_sem=load_sem.at[target], recv_sem=recv_sem.at[source],
            device_id=(2 * target + side,), device_id_type=MESH,
        )

    @pl.loop(0, pairs - 1 - pair)
    def _(i):
        state_copy(pair, pairs - 1 - i).start()

    pl.when(side == 0)(finish_low)

    @pl.when(has_next)
    def _():
        q_halo.start()

    query_steps(range(chunks), (0, quarter), True)
    proj_q[EDGE : EDGE + half] = acc_q[:half] * inv[:half]

    product = prod[...]
    channel_group = iota((tok, chan), 1) // per_group
    block = 2 * LANES

    def convolve(some):
        for s0 in range(0, tok, block):
            s1 = min(s0 + block, tok)
            parts = [
                jnp.where(channel_group[s0:s1] == g, product[s0:s1], jnp.zeros_like(product[s0:s1])) for g in some
            ]
            step = (tok - s0) // 2
            for r in (s0, s0 + step):
                total = None
                for g, part in zip(some, parts):
                    term = dot(toeplitz[g, r : r + step, s0:s1], part)
                    total = term if total is None else total + term
                acc_q[r : r + step] += total

    acc_q[...] = skip[...] * product.astype(F32)
    convolve(range(groups // 2))
    make_rise()

    for r in range(strip, tok, strip):
        feat_q[r : r + strip] = feature(proj_q, EDGE + r, strip, 0, 0)
    convolve(range(groups // 2, groups))

    pair_decay = jnp.exp(-rate_mc * float(2 * tok))
    pair_decay = jnp.where(side == 1, pair_decay[:, side_chan:], pair_decay[:, :side_chan])
    trade = near_copy(5, carried.at[side], carried.at[side], sibling)

    def gather(p, state):
        state_copy(p, pair).wait_recv()
        return pair_decay * state + slots[p].astype(F32)

    carried[side] = lax.fori_loop(0, pair, gather, jnp.zeros((modes, side_chan), F32))
    trade.start()

    @pl.when(me > 0)
    def _():
        q_halo.wait_recv()

    feat_q[:strip] = feature(proj_q, EDGE, strip, 0, 0)
    trade.wait_recv()
    state = jnp.concatenate([carried[0], carried[1]], axis=1)
    state = jnp.where(side == 1, decay * state + even_state[...], state) * weight_mc
    stacked = jnp.concatenate([state] * groups, axis=0)
    same = iota((every, chan), 0) // modes == iota((every, chan), 1) // per_group
    high, low = split(jnp.where(same, stacked, 0.0))
    paired = jnp.concatenate([high, high], axis=0)
    for r in (0, half):
        rows = slice(r, r + half)
        far = dot(rise[rows], paired) + dot(rise[rows, :every], low)
        out[rows] = (feat_q[rows] * (acc_q[rows] + far)).astype(BF16)

    out_copy.wait()

    swap.wait_send()
    trade.wait_send()

    @pl.when(has_next)
    def _():
        halo.wait_send()
        q_halo.wait_send()

    @pl.when(sends_far)
    def _():
        far_halo.wait_send()

    @pl.when(side == 0)
    def _():
        heading.wait_send()

    @pl.loop(pair + 1, pairs)
    def _(p):
        state_copy(pair, p).wait_send()


def project_out(gated, w_out, mixed, held, sem):
    parts, _, block = held.shape

    def copy(k):
        return pltpu.make_async_copy(held.at[k], mixed.at[:, pl.ds(k * block, block)], sem.at[k])

    for k in range(parts):
        held[k] = dot(gated[...], w_out[:, k * block : (k + 1) * block]).astype(BF16)
        copy(k).start()
    for k in range(parts):
        copy(k).wait()


def on_device(n, hidden, norm_gain, w_in, w_short, residues, rates, skip, w_out):
    tok, width = hidden.shape
    chan = w_short.shape[0] // 3
    groups, modes = rates.shape
    every = groups * modes
    depth = min(1024, width)
    chunks = width // depth
    vmem = pl.BlockSpec(memory_space=pltpu.VMEM)
    in_hbm = pl.BlockSpec(memory_space=pltpu.HBM)
    gated, w_out_near = pl.pallas_call(
        functools.partial(mixer, n, depth),
        out_shape=[pltpu.VMEM((tok, chan), BF16), pltpu.VMEM((chan, width), BF16)],
        in_specs=[in_hbm] * 8,
        out_specs=[vmem, vmem],
        scratch_shapes=[
            pltpu.VMEM((1, width), F32),
            pltpu.VMEM((w_short.shape[1], 3 * chan), F32),
            pltpu.VMEM((groups, modes), F32),
            pltpu.VMEM((groups, modes), F32),
            pltpu.VMEM((1, chan), F32),
            pltpu.VMEM((chunks, tok, depth), BF16),
            pltpu.VMEM((chunks, depth, 2 * chan), BF16),
            pltpu.VMEM((width, chan), BF16),
            pltpu.VMEM((TAIL, width - chunks * 5 // 8 * depth), BF16),
            pltpu.VMEM((tok, 2 * chan), F32),
            pltpu.VMEM((tok, chan), F32),
            pltpu.VMEM((tok, LANES), F32),
            pltpu.VMEM((tok, 2 * chan), F32),
            pltpu.VMEM((EDGE + tok, chan), F32),
            pltpu.VMEM((tok, chan), BF16),
            pltpu.VMEM((tok, chan), F32),
            pltpu.VMEM((2 * every, tok), BF16),
            pltpu.VMEM((tok, 2 * every), BF16),
            pltpu.VMEM((groups, tok), F32),
            pltpu.VMEM((groups, tok, tok), BF16),
            pltpu.VMEM((2 * EDGE, 2 * chan), F32),
            pltpu.VMEM((2 * EDGE, 2 * chan), F32),
            pltpu.VMEM((EDGE, modes, chan), F32),
            pltpu.VMEM((modes, chan), F32),
            pltpu.VMEM((modes, chan), F32),
            pltpu.VMEM((modes, chan), F32),
            pltpu.VMEM((modes, chan // 2), BF16),
            pltpu.VMEM((n // 2, modes, chan // 2), BF16),
            pltpu.VMEM((2, modes, chan // 2), F32),
            pltpu.SemaphoreType.DMA((max(2 * chunks, n // 2),)),
            pltpu.SemaphoreType.DMA((2,)),
            pltpu.SemaphoreType.DMA,
            pltpu.SemaphoreType.DMA((6,)),
            pltpu.SemaphoreType.DMA((n // 2,)),
            pltpu.SemaphoreType.DMA,
            pltpu.SemaphoreType.DMA((6,)),
        ],
        compiler_params=pltpu.CompilerParams(
            collective_id=0, has_side_effects=True, vmem_limit_bytes=48 * 1024 * 1024
        ),
        name="mixer",
        cost_estimate=pl.CostEstimate(
            flops=2 * tok * width * 3 * chan, bytes_accessed=2 * width * (tok + 3 * chan), transcendentals=0
        ),
    )(
        hidden, w_in, w_out,
        *(
            pltpu.with_memory_space_constraint(x, pltpu.HBM)
            for x in (norm_gain.reshape(1, width), w_short.T, rates, residues, skip.reshape(1, chan))
        ),
    )
    parts = 16
    return pl.pallas_call(
        project_out,
        out_shape=jax.ShapeDtypeStruct((tok, width), BF16),
        in_specs=[vmem, vmem],
        out_specs=in_hbm,
        scratch_shapes=[
            pltpu.VMEM((parts, tok, width // parts), BF16),
            pltpu.SemaphoreType.DMA((parts,)),
        ],
        name="project_out",
        compiler_params=pltpu.CompilerParams(vmem_limit_bytes=24 * 1024 * 1024),
        cost_estimate=pl.CostEstimate(
            flops=2 * tok * width * chan, bytes_accessed=2 * width * (tok + chan), transcendentals=0
        ),
    )(gated, w_out_near)


def solution(mesh):
    return jax.shard_map(
        functools.partial(on_device, mesh.shape["tm"]),
        mesh=mesh,
        in_specs=(P("tm", None), P(), P(), P(), P(), P(), P(), P()),
        out_specs=P("tm", None),
        check_vma=False,
    )
```

```python
import functools

import jax
import jax.numpy as jnp
from jax import lax
from jax.experimental import pallas as pl
from jax.experimental.pallas import tpu as pltpu
from jax.sharding import PartitionSpec as P

HIGHEST = lax.Precision.HIGHEST
MESH = pl.DeviceIdType.MESH
LANES = 128
EDGE = 8
TAIL = 16
GROUP = 3
PARTS = 16
F32 = jnp.float32
BF16 = jnp.bfloat16


def iota(shape, dim):
    return lax.broadcasted_iota(jnp.int32, shape, dim)


def dot(a, b):
    return jnp.dot(a, b, preferred_element_type=F32)


def split(x):
    high = x.astype(BF16)
    return high, (x - high.astype(F32)).astype(BF16)


def mixer(
    n, depth, hidden, w_in, w_out, gain_far, taps_far, rates_far, residues_far, skip_far, out, w_out_near,
    gain, taps, rates, residues, skip,
    held, w_kv, w_q, tail, acc_kv, acc_q, squares, proj_kv, proj_q, prod, feat_q,
    fall, rise, lag_row, toeplitz, lead, other_lead, edge_fall, mine_state, other_state, even_state, own, slots, carried,
    load_sem, q_sem, tail_sem, near_recv, recv_sem, out_sem, small_sem,
):
    me = lax.axis_index("tm")
    following = lax.rem(me + 1, n)
    pairs = n // 2
    pair, side = me // 2, lax.rem(me, 2)
    sibling = me + 1 - 2 * side
    tok, width = hidden.shape
    chan = prod.shape[1]
    groups, modes = rates.shape
    every = groups * modes
    per_group = chan // groups
    chunks = width // depth

    small = [
        pltpu.make_async_copy(source, target, small_sem.at[i])
        for i, (source, target) in enumerate(
            [(rates_far, rates), (residues_far, residues), (gain_far, gain), (taps_far, taps), (skip_far, skip)]
        )
    ]
    for copy in small:
        copy.start()

    late = chunks * 5 // 8
    body = tok - TAIL

    def held_copy(k, rows):
        rows, cols = pl.ds(0, rows), pl.ds(pl.multiple_of(k * depth, depth), depth)
        return pltpu.make_async_copy(hidden.at[rows, cols], held.at[k, rows], load_sem.at[k])

    tail_copy = pltpu.make_async_copy(
        hidden.at[pl.ds(body, TAIL), pl.ds(late * depth, width - late * depth)], tail, tail_sem
    )

    def kv_copy(k):
        rows = pl.ds(pl.multiple_of(k * depth, depth), depth)
        return pltpu.make_async_copy(w_in.at[rows, pl.ds(chan, 2 * chan)], w_kv.at[k], load_sem.at[chunks + k])

    parts = 2 if chunks % 2 == 0 else 1
    deep = width // parts

    def q_copy(i):
        rows = pl.ds(i * deep, deep)
        return pltpu.make_async_copy(w_in.at[rows, pl.ds(0, chan)], w_q.at[rows], q_sem.at[i])

    @pl.loop(0, late)
    def _(k):
        held_copy(k, tok).start()
        kv_copy(k).start()

    tail_copy.start()

    @pl.loop(late, chunks)
    def _(k):
        kv_copy(k).start()

    @pl.loop(late, chunks)
    def _(k):
        held_copy(k, body).start()

    out_copy = pltpu.make_async_copy(w_out, w_out_near, out_sem)

    barrier = pltpu.get_barrier_semaphore()

    def greet(d):
        pl.semaphore_signal(barrier, inc=1, device_id=(d,), device_id_type=MESH)

    @pl.loop(0, pair)
    def _(p):
        greet(2 * p + side)

    greet(sibling)

    @pl.when(jnp.logical_and(side == 0, pair > 0))
    def _():
        greet(me - 1)

    for copy in small:
        copy.wait()

    pick = (iota((modes, every), 1) % modes == iota((modes, every), 0)).astype(F32)
    mine = iota((groups, every), 1) // modes == iota((groups, every), 0)
    spread = (iota((groups, chan), 1) // per_group == iota((groups, chan), 0)).astype(F32)
    diagonal = iota((every, every), 0) == iota((every, every), 1)
    weights = residues[...] * jnp.sqrt(2.0 * rates[...])

    def as_row(x):
        wide = jnp.dot(x, pick, precision=HIGHEST, preferred_element_type=F32)
        return jnp.sum(jnp.where(mine, wide, 0.0), axis=0, keepdims=True)

    def as_column(row):
        return jnp.sum(jnp.where(diagonal, row, 0.0), axis=1, keepdims=True)

    def by_channel(x):
        return lax.dot_general(
            x, spread, (((0,), (0,)), ((), ())), precision=HIGHEST, preferred_element_type=F32
        )

    rate_row = as_row(rates[...])
    rate_col = as_column(rate_row)
    weight_col = as_column(as_row(weights))
    rate_mc = by_channel(rates[...])
    weight_mc = by_channel(weights)
    tiles = tok // LANES
    causal = iota((LANES, LANES), 0) >= iota((LANES, LANES), 1)

    def make_fall():
        high, low = split(jnp.exp(-rate_col * (tok - 1 - iota((every, tok), 1)).astype(F32)))
        early_rows = iota((every, tok), 1) < EDGE
        fall[:every] = jnp.where(early_rows, jnp.zeros_like(high), high)
        fall[every:] = jnp.where(early_rows, jnp.zeros_like(low), low)

    def make_rise():
        high, low = split(jnp.exp(-rate_row * (iota((tok, every), 0) + 1).astype(F32)))
        rise[:, :every], rise[:, every:] = high, low

    def make_lags():
        for r in range(EDGE):
            edge_fall[r] = jnp.exp(-rate_mc * float(tok - 1 - r))
        back = lax.rem(tok - iota((every, tok), 1), tok).astype(F32)
        terms = weight_col * jnp.exp(-rate_col * back)
        for g in range(groups):
            lag_row[g : g + 1] = jnp.sum(terms[g * modes : (g + 1) * modes], axis=0, keepdims=True)

    def make_toeplitz(some):
        for g in some:
            top = jnp.broadcast_to(lag_row[g : g + 1], (LANES, tok))
            moved = pltpu.roll(top, 0, 1, stride=1, stride_axis=0)
            lags = []
            for i in range(tiles):
                at = (tiles - i) % tiles * LANES
                tile = moved[:, at : at + LANES]
                lags.append((jnp.where(causal, tile, 0.0) if i == 0 else tile).astype(BF16))
            for i in range(tiles):
                for j in range(tiles):
                    value = lags[i - j] if i >= j else jnp.zeros((LANES, LANES), BF16)
                    toeplitz[g, i * LANES : (i + 1) * LANES, j * LANES : (j + 1) * LANES] = value

    even_state[...] = jnp.zeros_like(even_state)

    def ingest(k, first, stop):
        scale = gain[:, k * depth : (k + 1) * depth]
        parts = []
        for r in range(first, stop, 16):
            x = held[k, r : r + 16].astype(F32)
            sq = x * x
            total = sq[:, :LANES] if k == 0 else squares[r : r + 16] + sq[:, :LANES]
            for j in range(LANES, depth, LANES):
                total = total + sq[:, j : j + LANES]
            squares[r : r + 16] = total
            parts.append((x * scale).astype(BF16))
        scaled = jnp.concatenate(parts, axis=0)
        held[k, first:stop] = scaled
        if k == 0:
            acc_kv[first:stop] = dot(scaled, w_kv[k])
        else:
            acc_kv[first:stop] += dot(scaled, w_kv[k])

    jobs = [make_lags, make_fall] + [functools.partial(make_toeplitz, [g]) for g in range(groups)]
    where = [k for k in range(late) if k > 0] or [0]

    def beside(k):
        for i, job in enumerate(jobs):
            if where[i * len(where) // len(jobs)] == k:
                job()

    for k in range(late):
        held_copy(k, tok).wait()
        kv_copy(k).wait()
        ingest(k, 0, tok)
        beside(k)
    for i in range(parts):
        q_copy(i).start(priority=1)
    out_copy.start(priority=1)
    tail_copy.wait()
    for k in range(late, chunks):
        held[k, body:] = tail[:, (k - late) * depth : (k - late + 1) * depth]
    for k in range(late, chunks):
        kv_copy(k).wait()
        ingest(k, body, tok)

    def inverse(rows):
        return lax.rsqrt(jnp.sum(squares[rows], axis=1, keepdims=True) / width + 1e-06)

    tail_inv = inverse(slice(body, tok))
    proj_kv[body:] = acc_kv[body:] * tail_inv
    pl.semaphore_wait(barrier, pairs - pair + side * jnp.minimum(pairs - 1 - pair, 1))

    def near_copy(i, source, target, device):
        return pltpu.make_async_remote_copy(
            src_ref=source, dst_ref=target, send_sem=small_sem.at[i], recv_sem=near_recv.at[i],
            device_id=(device,), device_id_type=MESH,
        )

    before, first = pl.ds(0, EDGE), pl.ds(EDGE, EDGE)
    last = proj_kv.at[pl.ds(tok - EDGE, EDGE)]
    halo = near_copy(0, last, lead.at[before], following)
    far_halo = near_copy(1, last, other_lead.at[before], lax.rem(me + 2, n))
    heading = near_copy(2, proj_kv.at[before], other_lead.at[first], sibling)
    swap = near_copy(3, mine_state, other_state, sibling)
    q_halo = near_copy(4, proj_q.at[pl.ds(tok, EDGE)], proj_q.at[before], following)
    has_next = me < n - 1
    sends_far = jnp.logical_and(side == 1, has_next)

    @pl.when(has_next)
    def _():
        halo.start()

    @pl.when(sends_far)
    def _():
        far_halo.start()

    def feature(buf, r, rows, first, tap_first):
        shifted = [buf[pl.ds(r - EDGE, EDGE + rows), first : first + chan]]
        for i in range(1, GROUP):
            shifted.append(pltpu.roll(shifted[0], i, 0))
        total = None
        for t in reversed(range(0, taps.shape[0], GROUP)):
            if total is not None:
                total = pltpu.roll(total, GROUP, 0)
            for i in range(min(GROUP, taps.shape[0] - t)):
                term = taps[t + i : t + i + 1, tap_first : tap_first + chan] * shifted[i]
                total = term if total is None else total + term
        return total[EDGE:]

    def key_value(buf, r, rows):
        keyed = feature(buf, r, rows, 0, chan)
        valued = feature(buf, r, rows, chan, 2 * chan)
        return (keyed * valued).astype(BF16)

    def edge_state(product):
        total = jnp.zeros((modes, chan), F32)
        for r in range(EDGE):
            total = total + edge_fall[r] * product[r : r + 1].astype(F32)
        return total

    strip = 64 if tok % 64 == 0 else 32
    mid = tok // 2 // strip * strip
    zeros = jnp.zeros((EDGE, chan), BF16)
    for k in range(late, chunks):
        held_copy(k, body).wait()
        ingest(k, 0, mid)
    for k in range(late, chunks):
        ingest(k, mid, body)
    top_inv = inverse(slice(0, mid))
    proj_kv[:mid] = acc_kv[:mid] * top_inv
    prod[:strip] = jnp.concatenate([zeros, key_value(proj_kv, EDGE, strip - EDGE)], axis=0)
    for r in range(strip, mid, strip):
        prod[r : r + strip] = key_value(proj_kv, r, strip)

    low_inv = inverse(slice(mid, body))
    proj_kv[mid:body] = acc_kv[mid:body] * low_inv
    inv = jnp.concatenate([top_inv, low_inv, tail_inv], axis=0)

    @pl.when(side == 0)
    def _():
        heading.start()

    lead[EDGE:] = proj_kv[:EDGE]

    @pl.when(me == 0)
    def _():
        lead[:EDGE] = jnp.zeros((EDGE, 2 * chan), F32)
        proj_q[:EDGE] = jnp.zeros((EDGE, chan), F32)

    @pl.when(me == 1)
    def _():
        other_lead[:EDGE] = jnp.zeros((EDGE, 2 * chan), F32)

    half = tok // 2

    quarter = tok // 4

    def query_steps(some, starts, first):
        for r in starts:
            total = None
            for k in some:
                term = dot(held[k, r : r + quarter], w_q[k * depth : (k + 1) * depth])
                total = term if total is None else total + term
            acc_q[r : r + quarter] = total if first else acc_q[r : r + quarter] + total

    for r in range(mid, tok, strip):
        prod[r : r + strip] = key_value(proj_kv, r, strip)

    wide = []
    for m in (0, every // 2):
        low_part = dot(fall[every + m : every + m + every // 2], prod[...])
        wide.append(dot(fall[m : m + every // 2], prod[...]) + low_part)
    wide = jnp.concatenate(wide, axis=0)
    group_of = iota((modes, chan), 1) // per_group
    packed = jnp.zeros((modes, chan), F32)
    for g in range(groups):
        packed = packed + jnp.where(group_of == g, wide[g * modes : (g + 1) * modes], 0.0)

    @pl.when(side == 0)
    def _():
        mine_state[...] = packed
        swap.start()

    @pl.when(side == 1)
    def _():
        halo.wait_recv()
        rows = key_value(lead, EDGE, EDGE)
        prod[:EDGE] = rows
        mine_state[...] = packed + edge_state(rows)
        swap.start()

    early, later = max(1, chunks * 3 // 8), max(1, chunks * 3 // 4)
    for i in range(parts):
        q_copy(i).wait()
    query_steps(range(early), (half, half + quarter), True)
    decay = jnp.exp(-rate_mc * float(tok))
    side_chan = chan // 2
    low_rows = (half, half + quarter)

    def more_low():
        if early < later:
            query_steps(range(early, later), low_rows, False)

    pl.when(side == 1)(more_low)

    @pl.when(jnp.logical_and(side == 0, me > 0))
    def _():
        halo.wait_recv()

    @pl.when(side == 0)
    def _():
        rows = key_value(lead, EDGE, EDGE)
        prod[:EDGE] = rows
        whole = packed + edge_state(rows)
        swap.wait_recv()
        own[...] = (decay * whole + other_state[...])[:, :side_chan].astype(BF16)

    @pl.when(jnp.logical_and(side == 1, pair > 0))
    def _():
        far_halo.wait_recv()

    @pl.when(side == 1)
    def _():
        heading.wait_recv()
        swap.wait_recv()
        whole = other_state[...] + edge_state(key_value(other_lead, EDGE, EDGE))
        even_state[...] = whole
        own[...] = (decay * whole + mine_state[...])[:, side_chan:].astype(BF16)

    def state_copy(source, target):
        return pltpu.make_async_remote_copy(
            src_ref=own, dst_ref=slots.at[source],
            send_sem=load_sem.at[target], recv_sem=recv_sem.at[source],
            device_id=(2 * target + side,), device_id_type=MESH,
        )

    @pl.loop(0, pairs - 1 - pair)
    def _(i):
        state_copy(pair, pairs - 1 - i).start()

    pl.when(side == 0)(more_low)
    if later < chunks:
        query_steps(range(later, chunks), low_rows, False)
    proj_q[EDGE + half :] = acc_q[half:] * inv[half:]

    @pl.when(has_next)
    def _():
        q_halo.start()

    query_steps(range(chunks), (0, quarter), True)
    proj_q[EDGE : EDGE + half] = acc_q[:half] * inv[:half]

    product = prod[...]
    channel_group = iota((tok, chan), 1) // per_group
    block = 2 * LANES

    def convolve(some):
        for s0 in range(0, tok, block):
            s1 = min(s0 + block, tok)
            parts = [
                jnp.where(channel_group[s0:s1] == g, product[s0:s1], jnp.zeros_like(product[s0:s1])) for g in some
            ]
            step = (tok - s0) // 2
            for r in (s0, s0 + step):
                total = None
                for g, part in zip(some, parts):
                    term = dot(toeplitz[g, r : r + step, s0:s1], part)
                    total = term if total is None else total + term
                acc_q[r : r + step] += total

    acc_q[...] = skip[...] * product.astype(F32)
    convolve(range(groups // 2))
    make_rise()

    for r in range(strip, tok, strip):
        feat_q[r : r + strip] = feature(proj_q, EDGE + r, strip, 0, 0)
    convolve(range(groups // 2, groups))

    pair_decay = jnp.exp(-rate_mc * float(2 * tok))
    pair_decay = jnp.where(side == 1, pair_decay[:, side_chan:], pair_decay[:, :side_chan])
    trade = near_copy(5, carried.at[side], carried.at[side], sibling)

    def gather(p, state):
        state_copy(p, pair).wait_recv()
        return pair_decay * state + slots[p].astype(F32)

    carried[side] = lax.fori_loop(0, pair, gather, jnp.zeros((modes, side_chan), F32))
    trade.start()

    @pl.when(me > 0)
    def _():
        q_halo.wait_recv()

    feat_q[:strip] = feature(proj_q, EDGE, strip, 0, 0)
    trade.wait_recv()
    state = jnp.concatenate([carried[0], carried[1]], axis=1)
    state = jnp.where(side == 1, decay * state + even_state[...], state) * weight_mc
    stacked = jnp.concatenate([state] * groups, axis=0)
    same = iota((every, chan), 0) // modes == iota((every, chan), 1) // per_group
    high, low = split(jnp.where(same, stacked, 0.0))
    paired = jnp.concatenate([high, high], axis=0)
    for r in (0, half):
        rows = slice(r, r + half)
        far = dot(rise[rows], paired) + dot(rise[rows, :every], low)
        out[rows] = (feat_q[rows] * (acc_q[rows] + far)).astype(BF16)

    out_copy.wait()

    swap.wait_send()
    trade.wait_send()

    @pl.when(has_next)
    def _():
        halo.wait_send()
        q_halo.wait_send()

    @pl.when(sends_far)
    def _():
        far_halo.wait_send()

    @pl.when(side == 0)
    def _():
        heading.wait_send()

    @pl.loop(pair + 1, pairs)
    def _(p):
        state_copy(pair, p).wait_send()


def project_out(gated, w_out, mixed, held, sem):
    width = mixed.shape[1]
    block = width // PARTS
    for k in range(PARTS):
        cols = slice(k * block, (k + 1) * block)
        held[:, cols] = dot(gated[...], w_out[:, cols]).astype(BF16)
        pltpu.make_async_copy(held.at[:, cols], mixed.at[:, cols], sem).start()
    pltpu.make_async_copy(held, mixed, sem).wait()


def on_device(n, hidden, norm_gain, w_in, w_short, residues, rates, skip, w_out):
    tok, width = hidden.shape
    chan = w_short.shape[0] // 3
    groups, modes = rates.shape
    every = groups * modes
    depth = min(1024, width)
    chunks = width // depth
    vmem = pl.BlockSpec(memory_space=pltpu.VMEM)
    in_hbm = pl.BlockSpec(memory_space=pltpu.HBM)
    gated, w_out_near = pl.pallas_call(
        functools.partial(mixer, n, depth),
        out_shape=[pltpu.VMEM((tok, chan), BF16), pltpu.VMEM((chan, width), BF16)],
        in_specs=[in_hbm] * 8,
        out_specs=[vmem, vmem],
        scratch_shapes=[
            pltpu.VMEM((1, width), F32),
            pltpu.VMEM((w_short.shape[1], 3 * chan), F32),
            pltpu.VMEM((groups, modes), F32),
            pltpu.VMEM((groups, modes), F32),
            pltpu.VMEM((1, chan), F32),
            pltpu.VMEM((chunks, tok, depth), BF16),
            pltpu.VMEM((chunks, depth, 2 * chan), BF16),
            pltpu.VMEM((width, chan), BF16),
            pltpu.VMEM((TAIL, width - chunks * 5 // 8 * depth), BF16),
            pltpu.VMEM((tok, 2 * chan), F32),
            pltpu.VMEM((tok, chan), F32),
            pltpu.VMEM((tok, LANES), F32),
            pltpu.VMEM((tok, 2 * chan), F32),
            pltpu.VMEM((EDGE + tok, chan), F32),
            pltpu.VMEM((tok, chan), BF16),
            pltpu.VMEM((tok, chan), F32),
            pltpu.VMEM((2 * every, tok), BF16),
            pltpu.VMEM((tok, 2 * every), BF16),
            pltpu.VMEM((groups, tok), F32),
            pltpu.VMEM((groups, tok, tok), BF16),
            pltpu.VMEM((2 * EDGE, 2 * chan), F32),
            pltpu.VMEM((2 * EDGE, 2 * chan), F32),
            pltpu.VMEM((EDGE, modes, chan), F32),
            pltpu.VMEM((modes, chan), F32),
            pltpu.VMEM((modes, chan), F32),
            pltpu.VMEM((modes, chan), F32),
            pltpu.VMEM((modes, chan // 2), BF16),
            pltpu.VMEM((n // 2, modes, chan // 2), BF16),
            pltpu.VMEM((2, modes, chan // 2), F32),
            pltpu.SemaphoreType.DMA((max(2 * chunks, n // 2),)),
            pltpu.SemaphoreType.DMA((2,)),
            pltpu.SemaphoreType.DMA,
            pltpu.SemaphoreType.DMA((6,)),
            pltpu.SemaphoreType.DMA((n // 2,)),
            pltpu.SemaphoreType.DMA,
            pltpu.SemaphoreType.DMA((6,)),
        ],
        compiler_params=pltpu.CompilerParams(
            collective_id=0, has_side_effects=True, vmem_limit_bytes=48 * 1024 * 1024
        ),
        name="mixer",
        cost_estimate=pl.CostEstimate(
            flops=2 * tok * width * 3 * chan, bytes_accessed=2 * width * (tok + 3 * chan), transcendentals=0
        ),
    )(
        hidden, w_in, w_out,
        *(
            pltpu.with_memory_space_constraint(x, pltpu.HBM)
            for x in (norm_gain.reshape(1, width), w_short.T, rates, residues, skip.reshape(1, chan))
        ),
    )
    return pl.pallas_call(
        project_out,
        out_shape=jax.ShapeDtypeStruct((tok, width), BF16),
        in_specs=[vmem, vmem],
        out_specs=in_hbm,
        scratch_shapes=[
            pltpu.VMEM((tok, width), BF16),
            pltpu.SemaphoreType.DMA,
        ],
        name="project_out",
        compiler_params=pltpu.CompilerParams(vmem_limit_bytes=24 * 1024 * 1024),
        cost_estimate=pl.CostEstimate(
            flops=2 * tok * width * chan, bytes_accessed=2 * width * (tok + chan), transcendentals=0
        ),
    )(gated, w_out_near)


def solution(mesh):
    return jax.shard_map(
        functools.partial(on_device, mesh.shape["tm"]),
        mesh=mesh,
        in_specs=(P("tm", None), P(), P(), P(), P(), P(), P(), P()),
        out_specs=P("tm", None),
        check_vma=False,
    )
```

```python
import functools

import jax
import jax.numpy as jnp
from jax import lax
from jax.experimental import pallas as pl
from jax.experimental.pallas import tpu as pltpu
from jax.sharding import PartitionSpec as P

HIGHEST = lax.Precision.HIGHEST
MESH = pl.DeviceIdType.MESH
LANES = 128
EDGE = 8
TAIL = 16
GROUP = 3
PARTS = 16
F32 = jnp.float32
BF16 = jnp.bfloat16


def iota(shape, dim):
    return lax.broadcasted_iota(jnp.int32, shape, dim)


def dot(a, b):
    return jnp.dot(a, b, preferred_element_type=F32)


def split(x):
    high = x.astype(BF16)
    return high, (x - high.astype(F32)).astype(BF16)


def mixer(
    n, depth, hidden, w_in, w_out, gain_far, taps_far, rates_far, residues_far, skip_far, out, w_out_near,
    gain, taps, rates, residues, skip,
    held, w_kv, w_q, tail, acc_kv, acc_q, squares, proj_kv, proj_q, prod, feat_q,
    fall, rise, lag_row, toeplitz, lead, other_lead, edge_fall, mine_state, other_state, even_state, own, slots, carried,
    load_sem, near_recv, recv_sem, small_sem,
):
    me = lax.axis_index("tm")
    following = lax.rem(me + 1, n)
    pairs = n // 2
    pair, side = me // 2, lax.rem(me, 2)
    sibling = me + 1 - 2 * side
    tok, width = hidden.shape
    chan = prod.shape[1]
    groups, modes = rates.shape
    every = groups * modes
    per_group = chan // groups
    chunks = width // depth

    small = [
        pltpu.make_async_copy(source, target, small_sem.at[i])
        for i, (source, target) in enumerate(
            [(rates_far, rates), (residues_far, residues), (gain_far, gain), (taps_far, taps), (skip_far, skip)]
        )
    ]
    for copy in small:
        copy.start()

    late = chunks * 6 // 8
    body = tok - TAIL

    def held_copy(k, rows):
        rows, cols = pl.ds(0, rows), pl.ds(pl.multiple_of(k * depth, depth), depth)
        return pltpu.make_async_copy(hidden.at[rows, cols], held.at[k, rows], load_sem.at[k])

    tail_copy = pltpu.make_async_copy(
        hidden.at[pl.ds(body, TAIL), pl.ds(late * depth, width - late * depth)], tail, small_sem.at[5]
    )

    def kv_copy(k):
        rows = pl.ds(pl.multiple_of(k * depth, depth), depth)
        return pltpu.make_async_copy(w_in.at[rows, pl.ds(chan, 2 * chan)], w_kv.at[k], load_sem.at[chunks + k])

    parts = 2 if chunks % 2 == 0 else 1
    deep = width // parts

    def q_copy(i):
        rows = pl.ds(i * deep, deep)
        return pltpu.make_async_copy(w_in.at[rows, pl.ds(0, chan)], w_q.at[rows], load_sem.at[1 + i])

    @pl.loop(0, late)
    def _(k):
        held_copy(k, tok).start()
        kv_copy(k).start()

    tail_copy.start()

    @pl.loop(late, chunks)
    def _(k):
        kv_copy(k).start()

    @pl.loop(late, chunks)
    def _(k):
        held_copy(k, body).start()

    out_copy = pltpu.make_async_copy(w_out, w_out_near, load_sem.at[0])

    barrier = pltpu.get_barrier_semaphore()

    def greet(d):
        pl.semaphore_signal(barrier, inc=1, device_id=(d,), device_id_type=MESH)

    @pl.loop(0, pair)
    def _(p):
        greet(2 * p + side)

    greet(sibling)

    @pl.when(jnp.logical_and(side == 0, pair > 0))
    def _():
        greet(me - 1)

    for copy in small:
        copy.wait()

    pick = (iota((modes, every), 1) % modes == iota((modes, every), 0)).astype(F32)
    mine = iota((groups, every), 1) // modes == iota((groups, every), 0)
    spread = (iota((groups, chan), 1) // per_group == iota((groups, chan), 0)).astype(F32)
    diagonal = iota((every, every), 0) == iota((every, every), 1)
    weights = residues[...] * jnp.sqrt(2.0 * rates[...])

    def as_row(x):
        wide = jnp.dot(x, pick, precision=HIGHEST, preferred_element_type=F32)
        return jnp.sum(jnp.where(mine, wide, 0.0), axis=0, keepdims=True)

    def as_column(row):
        return jnp.sum(jnp.where(diagonal, row, 0.0), axis=1, keepdims=True)

    def by_channel(x):
        return lax.dot_general(
            x, spread, (((0,), (0,)), ((), ())), precision=HIGHEST, preferred_element_type=F32
        )

    rate_row = as_row(rates[...])
    rate_col = as_column(rate_row)
    weight_col = as_column(as_row(weights))
    rate_mc = by_channel(rates[...])
    weight_mc = by_channel(weights)
    tiles = tok // LANES
    causal = iota((LANES, LANES), 0) >= iota((LANES, LANES), 1)

    def make_fall():
        high, low = split(jnp.exp(-rate_col * (tok - 1 - iota((every, tok), 1)).astype(F32)))
        early_rows = iota((every, tok), 1) < EDGE
        fall[:every] = jnp.where(early_rows, jnp.zeros_like(high), high)
        fall[every:] = jnp.where(early_rows, jnp.zeros_like(low), low)

    def make_rise():
        high, low = split(jnp.exp(-rate_row * (iota((tok, every), 0) + 1).astype(F32)))
        rise[:, :every], rise[:, every:] = high, low

    def make_lags():
        for r in range(EDGE):
            edge_fall[r] = jnp.exp(-rate_mc * float(tok - 1 - r))
        back = lax.rem(tok - iota((every, tok), 1), tok).astype(F32)
        terms = weight_col * jnp.exp(-rate_col * back)
        for g in range(groups):
            lag_row[g : g + 1] = jnp.sum(terms[g * modes : (g + 1) * modes], axis=0, keepdims=True)

    def make_toeplitz(some):
        for g in some:
            top = jnp.broadcast_to(lag_row[g : g + 1], (LANES, tok))
            moved = pltpu.roll(top, 0, 1, stride=1, stride_axis=0)
            lags = []
            for i in range(tiles):
                at = (tiles - i) % tiles * LANES
                tile = moved[:, at : at + LANES]
                lags.append((jnp.where(causal, tile, 0.0) if i == 0 else tile).astype(BF16))
            for i in range(tiles):
                for j in range(tiles):
                    value = lags[i - j] if i >= j else jnp.zeros((LANES, LANES), BF16)
                    toeplitz[g, i * LANES : (i + 1) * LANES, j * LANES : (j + 1) * LANES] = value

    even_state[...] = jnp.zeros_like(even_state)

    def ingest(k, first, stop):
        scale = gain[:, k * depth : (k + 1) * depth]
        parts = []
        for r in range(first, stop, 16):
            x = held[k, r : r + 16].astype(F32)
            sq = x * x
            total = sq[:, :LANES] if k == 0 else squares[r : r + 16] + sq[:, :LANES]
            for j in range(LANES, depth, LANES):
                total = total + sq[:, j : j + LANES]
            squares[r : r + 16] = total
            parts.append((x * scale).astype(BF16))
        scaled = jnp.concatenate(parts, axis=0)
        held[k, first:stop] = scaled
        if k == 0:
            acc_kv[first:stop] = dot(scaled, w_kv[k])
        else:
            acc_kv[first:stop] += dot(scaled, w_kv[k])

    jobs = [make_lags, make_fall] + [functools.partial(make_toeplitz, [g]) for g in range(groups)]
    where = [k for k in range(late) if k > 0] or [0]

    def beside(k):
        for i, job in enumerate(jobs):
            if where[i * len(where) // len(jobs)] == k:
                job()

    for k in range(late):
        held_copy(k, tok).wait()
        kv_copy(k).wait()
        ingest(k, 0, tok)
        beside(k)
    for i in range(parts):
        q_copy(i).start(priority=1)
    out_copy.start(priority=1)
    tail_copy.wait()
    for k in range(late, chunks):
        held[k, body:] = tail[:, (k - late) * depth : (k - late + 1) * depth]
    for k in range(late, chunks):
        kv_copy(k).wait()
        ingest(k, body, tok)

    def inverse(rows):
        return lax.rsqrt(jnp.sum(squares[rows], axis=1, keepdims=True) / width + 1e-06)

    tail_inv = inverse(slice(body, tok))
    proj_kv[body:] = acc_kv[body:] * tail_inv
    pl.semaphore_wait(barrier, pairs - pair + side * jnp.minimum(pairs - 1 - pair, 1))

    def near_copy(i, source, target, device):
        return pltpu.make_async_remote_copy(
            src_ref=source, dst_ref=target, send_sem=small_sem.at[i], recv_sem=near_recv.at[i],
            device_id=(device,), device_id_type=MESH,
        )

    before, first = pl.ds(0, EDGE), pl.ds(EDGE, EDGE)
    last = proj_kv.at[pl.ds(tok - EDGE, EDGE)]
    halo = near_copy(0, last, lead.at[before], following)
    far_halo = near_copy(1, last, other_lead.at[before], lax.rem(me + 2, n))
    heading = near_copy(2, proj_kv.at[before], other_lead.at[first], sibling)
    swap = near_copy(3, mine_state, other_state, sibling)
    q_halo = near_copy(4, proj_q.at[pl.ds(tok, EDGE)], proj_q.at[before], following)
    has_next = me < n - 1
    sends_far = jnp.logical_and(side == 1, has_next)

    @pl.when(has_next)
    def _():
        halo.start()

    @pl.when(sends_far)
    def _():
        far_halo.start()

    def feature(buf, r, rows, first, tap_first):
        shifted = [buf[pl.ds(r - EDGE, EDGE + rows), first : first + chan]]
        for i in range(1, GROUP):
            shifted.append(pltpu.roll(shifted[0], i, 0))
        total = None
        for t in reversed(range(0, taps.shape[0], GROUP)):
            if total is not None:
                total = pltpu.roll(total, GROUP, 0)
            for i in range(min(GROUP, taps.shape[0] - t)):
                term = taps[t + i : t + i + 1, tap_first : tap_first + chan] * shifted[i]
                total = term if total is None else total + term
        return total[EDGE:]

    def key_value(buf, r, rows):
        keyed = feature(buf, r, rows, 0, chan)
        valued = feature(buf, r, rows, chan, 2 * chan)
        return (keyed * valued).astype(BF16)

    def edge_state(product):
        total = jnp.zeros((modes, chan), F32)
        for r in range(EDGE):
            total = total + edge_fall[r] * product[r : r + 1].astype(F32)
        return total

    strip = 64 if tok % 64 == 0 else 32
    mid = tok // 2 // strip * strip
    zeros = jnp.zeros((EDGE, chan), BF16)
    for k in range(late, chunks):
        held_copy(k, body).wait()
        ingest(k, 0, mid)
    for k in range(late, chunks):
        ingest(k, mid, body)
    top_inv = inverse(slice(0, mid))
    proj_kv[:mid] = acc_kv[:mid] * top_inv
    prod[:strip] = jnp.concatenate([zeros, key_value(proj_kv, EDGE, strip - EDGE)], axis=0)
    for r in range(strip, mid, strip):
        prod[r : r + strip] = key_value(proj_kv, r, strip)

    low_inv = inverse(slice(mid, body))
    proj_kv[mid:body] = acc_kv[mid:body] * low_inv
    inv = jnp.concatenate([top_inv, low_inv, tail_inv], axis=0)

    @pl.when(side == 0)
    def _():
        heading.start()

    lead[EDGE:] = proj_kv[:EDGE]

    @pl.when(me == 0)
    def _():
        lead[:EDGE] = jnp.zeros((EDGE, 2 * chan), F32)
        proj_q[:EDGE] = jnp.zeros((EDGE, chan), F32)

    @pl.when(me == 1)
    def _():
        other_lead[:EDGE] = jnp.zeros((EDGE, 2 * chan), F32)

    half = tok // 2

    quarter = tok // 4

    def query_steps(some, starts, first):
        for r in starts:
            total = None
            for k in some:
                term = dot(held[k, r : r + quarter], w_q[k * depth : (k + 1) * depth])
                total = term if total is None else total + term
            acc_q[r : r + quarter] = total if first else acc_q[r : r + quarter] + total

    for r in range(mid, tok, strip):
        prod[r : r + strip] = key_value(proj_kv, r, strip)

    wide = []
    for m in (0, every // 2):
        low_part = dot(fall[every + m : every + m + every // 2], prod[...])
        wide.append(dot(fall[m : m + every // 2], prod[...]) + low_part)
    wide = jnp.concatenate(wide, axis=0)
    group_of = iota((modes, chan), 1) // per_group
    packed = jnp.zeros((modes, chan), F32)
    for g in range(groups):
        packed = packed + jnp.where(group_of == g, wide[g * modes : (g + 1) * modes], 0.0)

    @pl.when(side == 0)
    def _():
        mine_state[...] = packed
        swap.start()

    @pl.when(side == 1)
    def _():
        halo.wait_recv()
        rows = key_value(lead, EDGE, EDGE)
        prod[:EDGE] = rows
        mine_state[...] = packed + edge_state(rows)
        swap.start()

    early, later = max(1, chunks * 3 // 8), max(1, chunks * 3 // 4)
    for i in range(parts):
        q_copy(i).wait()
    query_steps(range(early), (half, half + quarter), True)
    decay = jnp.exp(-rate_mc * float(tok))
    side_chan = chan // 2
    low_rows = (half, half + quarter)

    def more_low():
        if early < later:
            query_steps(range(early, later), low_rows, False)

    pl.when(side == 1)(more_low)

    @pl.when(jnp.logical_and(side == 0, me > 0))
    def _():
        halo.wait_recv()

    @pl.when(side == 0)
    def _():
        rows = key_value(lead, EDGE, EDGE)
        prod[:EDGE] = rows
        whole = packed + edge_state(rows)
        swap.wait_recv()
        own[...] = (decay * whole + other_state[...])[:, :side_chan].astype(BF16)

    @pl.when(jnp.logical_and(side == 1, pair > 0))
    def _():
        far_halo.wait_recv()

    @pl.when(side == 1)
    def _():
        heading.wait_recv()
        swap.wait_recv()
        whole = other_state[...] + edge_state(key_value(other_lead, EDGE, EDGE))
        even_state[...] = whole
        own[...] = (decay * whole + mine_state[...])[:, side_chan:].astype(BF16)

    def state_copy(source, target):
        return pltpu.make_async_remote_copy(
            src_ref=own, dst_ref=slots.at[source],
            send_sem=load_sem.at[target], recv_sem=recv_sem.at[source],
            device_id=(2 * target + side,), device_id_type=MESH,
        )

    @pl.loop(0, pairs - 1 - pair)
    def _(i):
        state_copy(pair, pairs - 1 - i).start()

    pl.when(side == 0)(more_low)
    if later < chunks:
        query_steps(range(later, chunks), low_rows, False)
    proj_q[EDGE + half :] = acc_q[half:] * inv[half:]

    @pl.when(has_next)
    def _():
        q_halo.start()

    query_steps(range(chunks), (0, quarter), True)
    proj_q[EDGE : EDGE + half] = acc_q[:half] * inv[:half]

    product = prod[...]
    channel_group = iota((tok, chan), 1) // per_group
    block = 2 * LANES

    def convolve(some):
        for s0 in range(0, tok, block):
            s1 = min(s0 + block, tok)
            parts = [
                jnp.where(channel_group[s0:s1] == g, product[s0:s1], jnp.zeros_like(product[s0:s1])) for g in some
            ]
            step = (tok - s0) // 2
            for r in (s0, s0 + step):
                total = None
                for g, part in zip(some, parts):
                    term = dot(toeplitz[g, r : r + step, s0:s1], part)
                    total = term if total is None else total + term
                acc_q[r : r + step] += total

    acc_q[...] = skip[...] * product.astype(F32)
    convolve(range(groups // 2))
    make_rise()

    for r in range(strip, tok, strip):
        feat_q[r : r + strip] = feature(proj_q, EDGE + r, strip, 0, 0)
    convolve(range(groups // 2, groups))

    pair_decay = jnp.exp(-rate_mc * float(2 * tok))
    pair_decay = jnp.where(side == 1, pair_decay[:, side_chan:], pair_decay[:, :side_chan])
    trade = near_copy(5, carried.at[side], carried.at[side], sibling)

    def gather(p, state):
        state_copy(p, pair).wait_recv()
        return pair_decay * state + slots[p].astype(F32)

    carried[side] = lax.fori_loop(0, pair, gather, jnp.zeros((modes, side_chan), F32))
    trade.start()

    @pl.when(me > 0)
    def _():
        q_halo.wait_recv()

    feat_q[:strip] = feature(proj_q, EDGE, strip, 0, 0)
    trade.wait_recv()
    state = jnp.concatenate([carried[0], carried[1]], axis=1)
    state = jnp.where(side == 1, decay * state + even_state[...], state) * weight_mc
    stacked = jnp.concatenate([state] * groups, axis=0)
    same = iota((every, chan), 0) // modes == iota((every, chan), 1) // per_group
    high, low = split(jnp.where(same, stacked, 0.0))
    paired = jnp.concatenate([high, high], axis=0)
    for r in (0, half):
        rows = slice(r, r + half)
        far = dot(rise[rows], paired) + dot(rise[rows, :every], low)
        out[rows] = (feat_q[rows] * (acc_q[rows] + far)).astype(BF16)

    out_copy.wait()

    swap.wait_send()
    trade.wait_send()

    @pl.when(has_next)
    def _():
        halo.wait_send()
        q_halo.wait_send()

    @pl.when(sends_far)
    def _():
        far_halo.wait_send()

    @pl.when(side == 0)
    def _():
        heading.wait_send()

    @pl.loop(pair + 1, pairs)
    def _(p):
        state_copy(pair, p).wait_send()


def project_out(gated, w_out, mixed, held, sem):
    width = mixed.shape[1]
    block = width // PARTS
    for k in range(PARTS):
        cols = slice(k * block, (k + 1) * block)
        held[:, cols] = dot(gated[...], w_out[:, cols]).astype(BF16)
        pltpu.make_async_copy(held.at[:, cols], mixed.at[:, cols], sem).start()
    pltpu.make_async_copy(held, mixed, sem).wait()


def on_device(n, hidden, norm_gain, w_in, w_short, residues, rates, skip, w_out):
    tok, width = hidden.shape
    chan = w_short.shape[0] // 3
    groups, modes = rates.shape
    every = groups * modes
    depth = min(1024, width)
    chunks = width // depth
    vmem = pl.BlockSpec(memory_space=pltpu.VMEM)
    in_hbm = pl.BlockSpec(memory_space=pltpu.HBM)
    gated, w_out_near = pl.pallas_call(
        functools.partial(mixer, n, depth),
        out_shape=[pltpu.VMEM((tok, chan), BF16), pltpu.VMEM((chan, width), BF16)],
        in_specs=[in_hbm] * 8,
        out_specs=[vmem, vmem],
        scratch_shapes=[
            pltpu.VMEM((1, width), F32),
            pltpu.VMEM((w_short.shape[1], 3 * chan), F32),
            pltpu.VMEM((groups, modes), F32),
            pltpu.VMEM((groups, modes), F32),
            pltpu.VMEM((1, chan), F32),
            pltpu.VMEM((chunks, tok, depth), BF16),
            pltpu.VMEM((chunks, depth, 2 * chan), BF16),
            pltpu.VMEM((width, chan), BF16),
            pltpu.VMEM((TAIL, width - chunks * 6 // 8 * depth), BF16),
            pltpu.VMEM((tok, 2 * chan), F32),
            pltpu.VMEM((tok, chan), F32),
            pltpu.VMEM((tok, LANES), F32),
            pltpu.VMEM((tok, 2 * chan), F32),
            pltpu.VMEM((EDGE + tok, chan), F32),
            pltpu.VMEM((tok, chan), BF16),
            pltpu.VMEM((tok, chan), F32),
            pltpu.VMEM((2 * every, tok), BF16),
            pltpu.VMEM((tok, 2 * every), BF16),
            pltpu.VMEM((groups, tok), F32),
            pltpu.VMEM((groups, tok, tok), BF16),
            pltpu.VMEM((2 * EDGE, 2 * chan), F32),
            pltpu.VMEM((2 * EDGE, 2 * chan), F32),
            pltpu.VMEM((EDGE, modes, chan), F32),
            pltpu.VMEM((modes, chan), F32),
            pltpu.VMEM((modes, chan), F32),
            pltpu.VMEM((modes, chan), F32),
            pltpu.VMEM((modes, chan // 2), BF16),
            pltpu.VMEM((n // 2, modes, chan // 2), BF16),
            pltpu.VMEM((2, modes, chan // 2), F32),
            pltpu.SemaphoreType.DMA((max(2 * chunks, n // 2),)),
            pltpu.SemaphoreType.DMA((6,)),
            pltpu.SemaphoreType.DMA((n // 2,)),
            pltpu.SemaphoreType.DMA((6,)),
        ],
        compiler_params=pltpu.CompilerParams(
            collective_id=0, has_side_effects=True, vmem_limit_bytes=48 * 1024 * 1024
        ),
        name="mixer",
        cost_estimate=pl.CostEstimate(
            flops=2 * tok * width * 3 * chan, bytes_accessed=2 * width * (tok + 3 * chan), transcendentals=0
        ),
    )(
        hidden, w_in, w_out,
        *(
            pltpu.with_memory_space_constraint(x, pltpu.HBM)
            for x in (norm_gain.reshape(1, width), w_short.T, rates, residues, skip.reshape(1, chan))
        ),
    )
    return pl.pallas_call(
        project_out,
        out_shape=jax.ShapeDtypeStruct((tok, width), BF16),
        in_specs=[vmem, vmem],
        out_specs=in_hbm,
        scratch_shapes=[
            pltpu.VMEM((tok, width), BF16),
            pltpu.SemaphoreType.DMA,
        ],
        name="project_out",
        compiler_params=pltpu.CompilerParams(vmem_limit_bytes=24 * 1024 * 1024),
        cost_estimate=pl.CostEstimate(
            flops=2 * tok * width * chan, bytes_accessed=2 * width * (tok + chan), transcendentals=0
        ),
    )(gated, w_out_near)


def solution(mesh):
    return jax.shard_map(
        functools.partial(on_device, mesh.shape["tm"]),
        mesh=mesh,
        in_specs=(P("tm", None), P(), P(), P(), P(), P(), P(), P()),
        out_specs=P("tm", None),
        check_vma=False,
    )
```

```python
import functools

import jax
import jax.numpy as jnp
from jax import lax
from jax.experimental import pallas as pl
from jax.experimental.pallas import tpu as pltpu
from jax.sharding import PartitionSpec as P

HIGHEST = lax.Precision.HIGHEST
MESH = pl.DeviceIdType.MESH
LANES = 128
EDGE = 8
TAIL = 16
GROUP = 3
PARTS = 16
F32 = jnp.float32
BF16 = jnp.bfloat16


def iota(shape, dim):
    return lax.broadcasted_iota(jnp.int32, shape, dim)


def dot(a, b):
    return jnp.dot(a, b, preferred_element_type=F32)


def split(x):
    high = x.astype(BF16)
    return high, (x - high.astype(F32)).astype(BF16)


def mixer(
    n, depth, hidden, w_in, w_out, gain_far, taps_far, rates_far, residues_far, skip_far, out, w_out_near,
    gain, taps, rates, residues, skip,
    held, w_kv, w_q, tail, acc_kv, acc_q, squares, proj_kv, proj_q, prod, feat_q,
    fall, rise, lag_row, toeplitz, lead, other_lead, edge_fall, mine_state, other_state, even_state, own, slots, carried,
    load_sem, near_recv, recv_sem, small_sem,
):
    me = lax.axis_index("tm")
    following = lax.rem(me + 1, n)
    pairs = n // 2
    pair, side = me // 2, lax.rem(me, 2)
    sibling = me + 1 - 2 * side
    tok, width = hidden.shape
    chan = prod.shape[1]
    groups, modes = rates.shape
    every = groups * modes
    per_group = chan // groups
    chunks = width // depth

    small = [
        pltpu.make_async_copy(source, target, small_sem.at[i])
        for i, (source, target) in enumerate(
            [(rates_far, rates), (residues_far, residues), (gain_far, gain), (taps_far, taps), (skip_far, skip)]
        )
    ]
    for copy in small:
        copy.start()

    late = chunks * 6 // 8
    body = tok - TAIL

    def held_copy(k, rows):
        rows, cols = pl.ds(0, rows), pl.ds(pl.multiple_of(k * depth, depth), depth)
        return pltpu.make_async_copy(hidden.at[rows, cols], held.at[k, rows], load_sem.at[k])

    tail_copy = pltpu.make_async_copy(
        hidden.at[pl.ds(body, TAIL), pl.ds(late * depth, width - late * depth)], tail, small_sem.at[5]
    )

    def kv_copy(k):
        rows = pl.ds(pl.multiple_of(k * depth, depth), depth)
        return pltpu.make_async_copy(w_in.at[rows, pl.ds(chan, 2 * chan)], w_kv.at[k], load_sem.at[chunks + k])

    parts = 2 if chunks % 2 == 0 else 1
    deep = width // parts

    def q_copy(i):
        rows = pl.ds(i * deep, deep)
        return pltpu.make_async_copy(w_in.at[rows, pl.ds(0, chan)], w_q.at[rows], load_sem.at[1 + i])

    @pl.loop(0, late)
    def _(k):
        held_copy(k, tok).start()
        kv_copy(k).start()

    tail_copy.start()

    @pl.loop(late, chunks)
    def _(k):
        kv_copy(k).start()

    @pl.loop(late, chunks)
    def _(k):
        held_copy(k, body).start()

    out_copy = pltpu.make_async_copy(w_out, w_out_near, load_sem.at[0])

    barrier = pltpu.get_barrier_semaphore()

    def greet(d):
        pl.semaphore_signal(barrier, inc=1, device_id=(d,), device_id_type=MESH)

    @pl.loop(0, pair)
    def _(p):
        greet(2 * p + side)

    greet(sibling)

    @pl.when(jnp.logical_and(side == 0, pair > 0))
    def _():
        greet(me - 1)

    for copy in small:
        copy.wait()

    pick = (iota((modes, every), 1) % modes == iota((modes, every), 0)).astype(F32)
    mine = iota((groups, every), 1) // modes == iota((groups, every), 0)
    spread = (iota((groups, chan), 1) // per_group == iota((groups, chan), 0)).astype(F32)
    diagonal = iota((every, every), 0) == iota((every, every), 1)
    weights = residues[...] * jnp.sqrt(2.0 * rates[...])

    def as_row(x):
        wide = jnp.dot(x, pick, precision=HIGHEST, preferred_element_type=F32)
        return jnp.sum(jnp.where(mine, wide, 0.0), axis=0, keepdims=True)

    def as_column(row):
        return jnp.sum(jnp.where(diagonal, row, 0.0), axis=1, keepdims=True)

    def by_channel(x):
        return lax.dot_general(
            x, spread, (((0,), (0,)), ((), ())), precision=HIGHEST, preferred_element_type=F32
        )

    rate_row = as_row(rates[...])
    rate_col = as_column(rate_row)
    weight_col = as_column(as_row(weights))
    rate_mc = by_channel(rates[...])
    weight_mc = by_channel(weights)
    tiles = tok // LANES
    causal = iota((LANES, LANES), 0) >= iota((LANES, LANES), 1)

    def make_fall():
        high, low = split(jnp.exp(-rate_col * (tok - 1 - iota((every, tok), 1)).astype(F32)))
        early_rows = iota((every, tok), 1) < EDGE
        fall[:every] = jnp.where(early_rows, jnp.zeros_like(high), high)
        fall[every:] = jnp.where(early_rows, jnp.zeros_like(low), low)

    def make_rise():
        high, low = split(jnp.exp(-rate_row * (iota((tok, every), 0) + 1).astype(F32)))
        rise[:, :every], rise[:, every:] = high, low

    def make_lags():
        for r in range(EDGE):
            edge_fall[r] = jnp.exp(-rate_mc * float(tok - 1 - r))
        back = lax.rem(tok - iota((every, tok), 1), tok).astype(F32)
        terms = weight_col * jnp.exp(-rate_col * back)
        for g in range(groups):
            lag_row[g : g + 1] = jnp.sum(terms[g * modes : (g + 1) * modes], axis=0, keepdims=True)

    def make_toeplitz(some):
        for g in some:
            top = jnp.broadcast_to(lag_row[g : g + 1], (LANES, tok))
            moved = pltpu.roll(top, 0, 1, stride=1, stride_axis=0)
            lags = []
            for i in range(tiles):
                at = (tiles - i) % tiles * LANES
                tile = moved[:, at : at + LANES]
                lags.append((jnp.where(causal, tile, 0.0) if i == 0 else tile).astype(BF16))
            for i in range(tiles):
                for j in range(tiles):
                    value = lags[i - j] if i >= j else jnp.zeros((LANES, LANES), BF16)
                    toeplitz[g, i * LANES : (i + 1) * LANES, j * LANES : (j + 1) * LANES] = value

    even_state[...] = jnp.zeros_like(even_state)

    def ingest(k, first, stop):
        scale = gain[:, k * depth : (k + 1) * depth]
        parts = []
        for r in range(first, stop, 16):
            x = held[k, r : r + 16].astype(F32)
            sq = x * x
            total = sq[:, :LANES] if k == 0 else squares[r : r + 16] + sq[:, :LANES]
            for j in range(LANES, depth, LANES):
                total = total + sq[:, j : j + LANES]
            squares[r : r + 16] = total
            parts.append((x * scale).astype(BF16))
        scaled = jnp.concatenate(parts, axis=0)
        held[k, first:stop] = scaled
        if k == 0:
            acc_kv[first:stop] = dot(scaled, w_kv[k])
        else:
            acc_kv[first:stop] += dot(scaled, w_kv[k])

    jobs = [make_lags, make_fall]
    where = [k for k in range(late) if k > 0] or [0]

    def beside(k):
        for i, job in enumerate(jobs):
            if where[i * len(where) // len(jobs)] == k:
                job()

    for k in range(late):
        held_copy(k, tok).wait()
        kv_copy(k).wait()
        ingest(k, 0, tok)
        beside(k)
    for i in range(parts):
        q_copy(i).start(priority=1)
    out_copy.start(priority=1)
    tail_copy.wait()
    for k in range(late, chunks):
        held[k, body:] = tail[:, (k - late) * depth : (k - late + 1) * depth]
    for k in range(late, chunks):
        kv_copy(k).wait()
        ingest(k, body, tok)

    def inverse(rows):
        return lax.rsqrt(jnp.sum(squares[rows], axis=1, keepdims=True) / width + 1e-06)

    tail_inv = inverse(slice(body, tok))
    proj_kv[body:] = acc_kv[body:] * tail_inv
    pl.semaphore_wait(barrier, pairs - pair + side * jnp.minimum(pairs - 1 - pair, 1))

    def near_copy(i, source, target, device):
        return pltpu.make_async_remote_copy(
            src_ref=source, dst_ref=target, send_sem=small_sem.at[i], recv_sem=near_recv.at[i],
            device_id=(device,), device_id_type=MESH,
        )

    before, first = pl.ds(0, EDGE), pl.ds(EDGE, EDGE)
    last = proj_kv.at[pl.ds(tok - EDGE, EDGE)]
    halo = near_copy(0, last, lead.at[before], following)
    far_halo = near_copy(1, last, other_lead.at[before], lax.rem(me + 2, n))
    heading = near_copy(2, proj_kv.at[before], other_lead.at[first], sibling)
    swap = near_copy(3, mine_state, other_state, sibling)
    q_halo = near_copy(4, proj_q.at[pl.ds(tok, EDGE)], proj_q.at[before], following)
    has_next = me < n - 1
    sends_far = jnp.logical_and(side == 1, has_next)

    @pl.when(has_next)
    def _():
        halo.start()

    @pl.when(sends_far)
    def _():
        far_halo.start()

    def feature(buf, r, rows, first, tap_first):
        shifted = [buf[pl.ds(r - EDGE, EDGE + rows), first : first + chan]]
        for i in range(1, GROUP):
            shifted.append(pltpu.roll(shifted[0], i, 0))
        total = None
        for t in reversed(range(0, taps.shape[0], GROUP)):
            if total is not None:
                total = pltpu.roll(total, GROUP, 0)
            for i in range(min(GROUP, taps.shape[0] - t)):
                term = taps[t + i : t + i + 1, tap_first : tap_first + chan] * shifted[i]
                total = term if total is None else total + term
        return total[EDGE:]

    def key_value(buf, r, rows):
        keyed = feature(buf, r, rows, 0, chan)
        valued = feature(buf, r, rows, chan, 2 * chan)
        return (keyed * valued).astype(BF16)

    def edge_state(product):
        total = jnp.zeros((modes, chan), F32)
        for r in range(EDGE):
            total = total + edge_fall[r] * product[r : r + 1].astype(F32)
        return total

    strip = 64 if tok % 64 == 0 else 32
    mid = tok // 2 // strip * strip
    zeros = jnp.zeros((EDGE, chan), BF16)
    for k in range(late, chunks):
        held_copy(k, body).wait()
        ingest(k, 0, mid)
    for k in range(late, chunks):
        ingest(k, mid, body)
    top_inv = inverse(slice(0, mid))
    proj_kv[:mid] = acc_kv[:mid] * top_inv
    prod[:strip] = jnp.concatenate([zeros, key_value(proj_kv, EDGE, strip - EDGE)], axis=0)
    for r in range(strip, mid, strip):
        prod[r : r + strip] = key_value(proj_kv, r, strip)

    low_inv = inverse(slice(mid, body))
    proj_kv[mid:body] = acc_kv[mid:body] * low_inv
    inv = jnp.concatenate([top_inv, low_inv, tail_inv], axis=0)

    @pl.when(side == 0)
    def _():
        heading.start()

    lead[EDGE:] = proj_kv[:EDGE]

    @pl.when(me == 0)
    def _():
        lead[:EDGE] = jnp.zeros((EDGE, 2 * chan), F32)
        proj_q[:EDGE] = jnp.zeros((EDGE, chan), F32)

    @pl.when(me == 1)
    def _():
        other_lead[:EDGE] = jnp.zeros((EDGE, 2 * chan), F32)

    half = tok // 2

    quarter = tok // 4

    def query_steps(some, starts, first):
        for r in starts:
            total = None
            for k in some:
                term = dot(held[k, r : r + quarter], w_q[k * depth : (k + 1) * depth])
                total = term if total is None else total + term
            acc_q[r : r + quarter] = total if first else acc_q[r : r + quarter] + total

    for r in range(mid, tok, strip):
        prod[r : r + strip] = key_value(proj_kv, r, strip)

    wide = []
    for m in (0, every // 2):
        low_part = dot(fall[every + m : every + m + every // 2], prod[...])
        wide.append(dot(fall[m : m + every // 2], prod[...]) + low_part)
    wide = jnp.concatenate(wide, axis=0)
    group_of = iota((modes, chan), 1) // per_group
    packed = jnp.zeros((modes, chan), F32)
    for g in range(groups):
        packed = packed + jnp.where(group_of == g, wide[g * modes : (g + 1) * modes], 0.0)

    @pl.when(side == 0)
    def _():
        mine_state[...] = packed
        swap.start()

    @pl.when(side == 1)
    def _():
        halo.wait_recv()
        rows = key_value(lead, EDGE, EDGE)
        prod[:EDGE] = rows
        mine_state[...] = packed + edge_state(rows)
        swap.start()

    early, later = max(1, chunks * 3 // 8), max(1, chunks * 3 // 4)
    for i in range(parts):
        q_copy(i).wait()
    query_steps(range(early), (half, half + quarter), True)
    decay = jnp.exp(-rate_mc * float(tok))
    side_chan = chan // 2
    low_rows = (half, half + quarter)

    def more_low():
        if early < later:
            query_steps(range(early, later), low_rows, False)

    pl.when(side == 1)(more_low)

    @pl.when(jnp.logical_and(side == 0, me > 0))
    def _():
        halo.wait_recv()

    @pl.when(side == 0)
    def _():
        rows = key_value(lead, EDGE, EDGE)
        prod[:EDGE] = rows
        whole = packed + edge_state(rows)
        swap.wait_recv()
        own[...] = (decay * whole + other_state[...])[:, :side_chan].astype(BF16)

    @pl.when(jnp.logical_and(side == 1, pair > 0))
    def _():
        far_halo.wait_recv()

    @pl.when(side == 1)
    def _():
        heading.wait_recv()
        swap.wait_recv()
        whole = other_state[...] + edge_state(key_value(other_lead, EDGE, EDGE))
        even_state[...] = whole
        own[...] = (decay * whole + mine_state[...])[:, side_chan:].astype(BF16)

    def state_copy(source, target):
        return pltpu.make_async_remote_copy(
            src_ref=own, dst_ref=slots.at[source],
            send_sem=load_sem.at[target], recv_sem=recv_sem.at[source],
            device_id=(2 * target + side,), device_id_type=MESH,
        )

    @pl.loop(0, pairs - 1 - pair)
    def _(i):
        state_copy(pair, pairs - 1 - i).start()

    pl.when(side == 0)(more_low)
    if later < chunks:
        query_steps(range(later, chunks), low_rows, False)
    proj_q[EDGE + half :] = acc_q[half:] * inv[half:]

    @pl.when(has_next)
    def _():
        q_halo.start()

    query_steps(range(chunks), (0, quarter), True)
    make_toeplitz(range(groups))
    proj_q[EDGE : EDGE + half] = acc_q[:half] * inv[:half]

    product = prod[...]
    channel_group = iota((tok, chan), 1) // per_group
    block = 2 * LANES

    def convolve(some):
        for s0 in range(0, tok, block):
            s1 = min(s0 + block, tok)
            parts = [
                jnp.where(channel_group[s0:s1] == g, product[s0:s1], jnp.zeros_like(product[s0:s1])) for g in some
            ]
            step = (tok - s0) // 2
            for r in (s0, s0 + step):
                total = None
                for g, part in zip(some, parts):
                    term = dot(toeplitz[g, r : r + step, s0:s1], part)
                    total = term if total is None else total + term
                acc_q[r : r + step] += total

    acc_q[...] = skip[...] * product.astype(F32)
    convolve(range(groups // 2))
    make_rise()

    for r in range(strip, tok, strip):
        feat_q[r : r + strip] = feature(proj_q, EDGE + r, strip, 0, 0)
    convolve(range(groups // 2, groups))

    pair_decay = jnp.exp(-rate_mc * float(2 * tok))
    pair_decay = jnp.where(side == 1, pair_decay[:, side_chan:], pair_decay[:, :side_chan])
    trade = near_copy(5, carried.at[side], carried.at[side], sibling)

    def gather(p, state):
        state_copy(p, pair).wait_recv()
        return pair_decay * state + slots[p].astype(F32)

    carried[side] = lax.fori_loop(0, pair, gather, jnp.zeros((modes, side_chan), F32))
    trade.start()

    @pl.when(me > 0)
    def _():
        q_halo.wait_recv()

    feat_q[:strip] = feature(proj_q, EDGE, strip, 0, 0)
    trade.wait_recv()
    state = jnp.concatenate([carried[0], carried[1]], axis=1)
    state = jnp.where(side == 1, decay * state + even_state[...], state) * weight_mc
    stacked = jnp.concatenate([state] * groups, axis=0)
    same = iota((every, chan), 0) // modes == iota((every, chan), 1) // per_group
    high, low = split(jnp.where(same, stacked, 0.0))
    paired = jnp.concatenate([high, high], axis=0)
    for r in (0, half):
        rows = slice(r, r + half)
        far = dot(rise[rows], paired) + dot(rise[rows, :every], low)
        out[rows] = (feat_q[rows] * (acc_q[rows] + far)).astype(BF16)

    out_copy.wait()

    swap.wait_send()
    trade.wait_send()

    @pl.when(has_next)
    def _():
        halo.wait_send()
        q_halo.wait_send()

    @pl.when(sends_far)
    def _():
        far_halo.wait_send()

    @pl.when(side == 0)
    def _():
        heading.wait_send()

    @pl.loop(pair + 1, pairs)
    def _(p):
        state_copy(pair, p).wait_send()


def project_out(gated, w_out, mixed, held, sem):
    width = mixed.shape[1]
    block = width // PARTS
    for k in range(PARTS):
        cols = slice(k * block, (k + 1) * block)
        held[:, cols] = dot(gated[...], w_out[:, cols]).astype(BF16)
        pltpu.make_async_copy(held.at[:, cols], mixed.at[:, cols], sem).start()
    pltpu.make_async_copy(held, mixed, sem).wait()


def on_device(n, hidden, norm_gain, w_in, w_short, residues, rates, skip, w_out):
    tok, width = hidden.shape
    chan = w_short.shape[0] // 3
    groups, modes = rates.shape
    every = groups * modes
    depth = min(1024, width)
    chunks = width // depth
    vmem = pl.BlockSpec(memory_space=pltpu.VMEM)
    in_hbm = pl.BlockSpec(memory_space=pltpu.HBM)
    gated, w_out_near = pl.pallas_call(
        functools.partial(mixer, n, depth),
        out_shape=[pltpu.VMEM((tok, chan), BF16), pltpu.VMEM((chan, width), BF16)],
        in_specs=[in_hbm] * 8,
        out_specs=[vmem, vmem],
        scratch_shapes=[
            pltpu.VMEM((1, width), F32),
            pltpu.VMEM((w_short.shape[1], 3 * chan), F32),
            pltpu.VMEM((groups, modes), F32),
            pltpu.VMEM((groups, modes), F32),
            pltpu.VMEM((1, chan), F32),
            pltpu.VMEM((chunks, tok, depth), BF16),
            pltpu.VMEM((chunks, depth, 2 * chan), BF16),
            pltpu.VMEM((width, chan), BF16),
            pltpu.VMEM((TAIL, width - chunks * 6 // 8 * depth), BF16),
            pltpu.VMEM((tok, 2 * chan), F32),
            pltpu.VMEM((tok, chan), F32),
            pltpu.VMEM((tok, LANES), F32),
            pltpu.VMEM((tok, 2 * chan), F32),
            pltpu.VMEM((EDGE + tok, chan), F32),
            pltpu.VMEM((tok, chan), BF16),
            pltpu.VMEM((tok, chan), F32),
            pltpu.VMEM((2 * every, tok), BF16),
            pltpu.VMEM((tok, 2 * every), BF16),
            pltpu.VMEM((groups, tok), F32),
            pltpu.VMEM((groups, tok, tok), BF16),
            pltpu.VMEM((2 * EDGE, 2 * chan), F32),
            pltpu.VMEM((2 * EDGE, 2 * chan), F32),
            pltpu.VMEM((EDGE, modes, chan), F32),
            pltpu.VMEM((modes, chan), F32),
            pltpu.VMEM((modes, chan), F32),
            pltpu.VMEM((modes, chan), F32),
            pltpu.VMEM((modes, chan // 2), BF16),
            pltpu.VMEM((n // 2, modes, chan // 2), BF16),
            pltpu.VMEM((2, modes, chan // 2), F32),
            pltpu.SemaphoreType.DMA((max(2 * chunks, n // 2),)),
            pltpu.SemaphoreType.DMA((6,)),
            pltpu.SemaphoreType.DMA((n // 2,)),
            pltpu.SemaphoreType.DMA((6,)),
        ],
        compiler_params=pltpu.CompilerParams(
            collective_id=0, has_side_effects=True, vmem_limit_bytes=48 * 1024 * 1024
        ),
        name="mixer",
        cost_estimate=pl.CostEstimate(
            flops=2 * tok * width * 3 * chan, bytes_accessed=2 * width * (tok + 3 * chan), transcendentals=0
        ),
    )(
        hidden, w_in, w_out,
        *(
            pltpu.with_memory_space_constraint(x, pltpu.HBM)
            for x in (norm_gain.reshape(1, width), w_short.T, rates, residues, skip.reshape(1, chan))
        ),
    )
    return pl.pallas_call(
        project_out,
        out_shape=jax.ShapeDtypeStruct((tok, width), BF16),
        in_specs=[vmem, vmem],
        out_specs=in_hbm,
        scratch_shapes=[
            pltpu.VMEM((tok, width), BF16),
            pltpu.SemaphoreType.DMA,
        ],
        name="project_out",
        compiler_params=pltpu.CompilerParams(vmem_limit_bytes=24 * 1024 * 1024),
        cost_estimate=pl.CostEstimate(
            flops=2 * tok * width * chan, bytes_accessed=2 * width * (tok + chan), transcendentals=0
        ),
    )(gated, w_out_near)


def solution(mesh):
    return jax.shard_map(
        functools.partial(on_device, mesh.shape["tm"]),
        mesh=mesh,
        in_specs=(P("tm", None), P(), P(), P(), P(), P(), P(), P()),
        out_specs=P("tm", None),
        check_vma=False,
    )
```

```python
import functools

import jax
import jax.numpy as jnp
from jax import lax
from jax.experimental import pallas as pl
from jax.experimental.pallas import tpu as pltpu
from jax.sharding import PartitionSpec as P

HIGHEST = lax.Precision.HIGHEST
MESH = pl.DeviceIdType.MESH
LANES = 128
EDGE = 8
TAIL = 16
GROUP = 3
PARTS = 16
F32 = jnp.float32
BF16 = jnp.bfloat16


def iota(shape, dim):
    return lax.broadcasted_iota(jnp.int32, shape, dim)


def dot(a, b):
    return jnp.dot(a, b, preferred_element_type=F32)


def split(x):
    high = x.astype(BF16)
    return high, (x - high.astype(F32)).astype(BF16)


def mixer(
    n, depth, hidden, w_in, w_out, gain_far, taps_far, rates_far, residues_far, skip_far, out, w_out_near,
    gain, taps, rates, residues, skip,
    held, w_kv, w_q, tail, acc_kv, acc_q, squares, proj_kv, proj_q, prod, feat_q,
    fall, rise, lag_row, toeplitz, lead, other_lead, edge_fall, mine_state, other_state, even_state, own, slots, carried,
    load_sem, near_recv, recv_sem, small_sem,
):
    me = lax.axis_index("tm")
    following = lax.rem(me + 1, n)
    pairs = n // 2
    pair, side = me // 2, lax.rem(me, 2)
    sibling = me + 1 - 2 * side
    tok, width = hidden.shape
    chan = prod.shape[1]
    groups, modes = rates.shape
    every = groups * modes
    per_group = chan // groups
    chunks = width // depth

    small = [
        pltpu.make_async_copy(source, target, small_sem.at[i])
        for i, (source, target) in enumerate(
            [(rates_far, rates), (residues_far, residues), (gain_far, gain), (taps_far, taps), (skip_far, skip)]
        )
    ]
    for copy in small:
        copy.start()

    late = chunks * 7 // 8
    body = tok - TAIL

    def held_copy(k, rows):
        rows, cols = pl.ds(0, rows), pl.ds(pl.multiple_of(k * depth, depth), depth)
        return pltpu.make_async_copy(hidden.at[rows, cols], held.at[k, rows], load_sem.at[k])

    tail_copy = pltpu.make_async_copy(
        hidden.at[pl.ds(body, TAIL), pl.ds(late * depth, width - late * depth)], tail, small_sem.at[5]
    )

    def kv_copy(k):
        rows = pl.ds(pl.multiple_of(k * depth, depth), depth)
        return pltpu.make_async_copy(w_in.at[rows, pl.ds(chan, 2 * chan)], w_kv.at[k], load_sem.at[chunks + k])

    parts = 2 if chunks % 2 == 0 else 1
    deep = width // parts

    def q_copy(i):
        rows = pl.ds(i * deep, deep)
        return pltpu.make_async_copy(w_in.at[rows, pl.ds(0, chan)], w_q.at[rows], load_sem.at[1 + i])

    @pl.loop(0, late)
    def _(k):
        held_copy(k, tok).start()
        kv_copy(k).start()

    tail_copy.start()

    @pl.loop(late, chunks)
    def _(k):
        kv_copy(k).start()

    @pl.loop(late, chunks)
    def _(k):
        held_copy(k, body).start()

    out_copy = pltpu.make_async_copy(w_out, w_out_near, load_sem.at[0])

    barrier = pltpu.get_barrier_semaphore()

    def greet(d):
        pl.semaphore_signal(barrier, inc=1, device_id=(d,), device_id_type=MESH)

    @pl.loop(0, pair)
    def _(p):
        greet(2 * p + side)

    greet(sibling)

    @pl.when(jnp.logical_and(side == 0, pair > 0))
    def _():
        greet(me - 1)

    for copy in small:
        copy.wait()

    pick = (iota((modes, every), 1) % modes == iota((modes, every), 0)).astype(F32)
    mine = iota((groups, every), 1) // modes == iota((groups, every), 0)
    spread = (iota((groups, chan), 1) // per_group == iota((groups, chan), 0)).astype(F32)
    diagonal = iota((every, every), 0) == iota((every, every), 1)
    weights = residues[...] * jnp.sqrt(2.0 * rates[...])

    def as_row(x):
        wide = jnp.dot(x, pick, precision=HIGHEST, preferred_element_type=F32)
        return jnp.sum(jnp.where(mine, wide, 0.0), axis=0, keepdims=True)

    def as_column(row):
        return jnp.sum(jnp.where(diagonal, row, 0.0), axis=1, keepdims=True)

    def by_channel(x):
        return lax.dot_general(
            x, spread, (((0,), (0,)), ((), ())), precision=HIGHEST, preferred_element_type=F32
        )

    rate_row = as_row(rates[...])
    rate_col = as_column(rate_row)
    weight_col = as_column(as_row(weights))
    rate_mc = by_channel(rates[...])
    weight_mc = by_channel(weights)
    tiles = tok // LANES
    causal = iota((LANES, LANES), 0) >= iota((LANES, LANES), 1)

    def make_fall():
        high, low = split(jnp.exp(-rate_col * (tok - 1 - iota((every, tok), 1)).astype(F32)))
        early_rows = iota((every, tok), 1) < EDGE
        fall[:every] = jnp.where(early_rows, jnp.zeros_like(high), high)
        fall[every:] = jnp.where(early_rows, jnp.zeros_like(low), low)

    def make_rise():
        high, low = split(jnp.exp(-rate_row * (iota((tok, every), 0) + 1).astype(F32)))
        rise[:, :every], rise[:, every:] = high, low

    def make_lags():
        for r in range(EDGE):
            edge_fall[r] = jnp.exp(-rate_mc * float(tok - 1 - r))
        back = lax.rem(tok - iota((every, tok), 1), tok).astype(F32)
        terms = weight_col * jnp.exp(-rate_col * back)
        for g in range(groups):
            lag_row[g : g + 1] = jnp.sum(terms[g * modes : (g + 1) * modes], axis=0, keepdims=True)

    def make_toeplitz(some):
        for g in some:
            top = jnp.broadcast_to(lag_row[g : g + 1], (LANES, tok))
            moved = pltpu.roll(top, 0, 1, stride=1, stride_axis=0)
            lags = []
            for i in range(tiles):
                at = (tiles - i) % tiles * LANES
                tile = moved[:, at : at + LANES]
                lags.append((jnp.where(causal, tile, 0.0) if i == 0 else tile).astype(BF16))
            for i in range(tiles):
                for j in range(tiles):
                    value = lags[i - j] if i >= j else jnp.zeros((LANES, LANES), BF16)
                    toeplitz[g, i * LANES : (i + 1) * LANES, j * LANES : (j + 1) * LANES] = value

    even_state[...] = jnp.zeros_like(even_state)

    def ingest(k, first, stop):
        scale = gain[:, k * depth : (k + 1) * depth]
        parts = []
        for r in range(first, stop, 16):
            x = held[k, r : r + 16].astype(F32)
            sq = x * x
            total = sq[:, :LANES] if k == 0 else squares[r : r + 16] + sq[:, :LANES]
            for j in range(LANES, depth, LANES):
                total = total + sq[:, j : j + LANES]
            squares[r : r + 16] = total
            parts.append((x * scale).astype(BF16))
        scaled = jnp.concatenate(parts, axis=0)
        held[k, first:stop] = scaled
        if k == 0:
            acc_kv[first:stop] = dot(scaled, w_kv[k])
        else:
            acc_kv[first:stop] += dot(scaled, w_kv[k])

    jobs = [make_lags, make_fall]
    where = [k for k in range(late) if k > 0] or [0]

    def beside(k):
        for i, job in enumerate(jobs):
            if where[i * len(where) // len(jobs)] == k:
                job()

    for k in range(late):
        held_copy(k, tok).wait()
        kv_copy(k).wait()
        ingest(k, 0, tok)
        beside(k)
    for i in range(parts):
        q_copy(i).start(priority=1)
    out_copy.start(priority=1)
    tail_copy.wait()
    for k in range(late, chunks):
        held[k, body:] = tail[:, (k - late) * depth : (k - late + 1) * depth]
    for k in range(late, chunks):
        kv_copy(k).wait()
        ingest(k, body, tok)

    def inverse(rows):
        return lax.rsqrt(jnp.sum(squares[rows], axis=1, keepdims=True) / width + 1e-06)

    tail_inv = inverse(slice(body, tok))
    proj_kv[body:] = acc_kv[body:] * tail_inv
    pl.semaphore_wait(barrier, pairs - pair + side * jnp.minimum(pairs - 1 - pair, 1))

    def near_copy(i, source, target, device):
        return pltpu.make_async_remote_copy(
            src_ref=source, dst_ref=target, send_sem=small_sem.at[i], recv_sem=near_recv.at[i],
            device_id=(device,), device_id_type=MESH,
        )

    before, first = pl.ds(0, EDGE), pl.ds(EDGE, EDGE)
    last = proj_kv.at[pl.ds(tok - EDGE, EDGE)]
    halo = near_copy(0, last, lead.at[before], following)
    far_halo = near_copy(1, last, other_lead.at[before], lax.rem(me + 2, n))
    heading = near_copy(2, proj_kv.at[before], other_lead.at[first], sibling)
    swap = near_copy(3, mine_state, other_state, sibling)
    q_halo = near_copy(4, proj_q.at[pl.ds(tok, EDGE)], proj_q.at[before], following)
    has_next = me < n - 1
    sends_far = jnp.logical_and(side == 1, has_next)

    @pl.when(has_next)
    def _():
        halo.start()

    @pl.when(sends_far)
    def _():
        far_halo.start()

    def feature(buf, r, rows, first, tap_first):
        shifted = [buf[pl.ds(r - EDGE, EDGE + rows), first : first + chan]]
        for i in range(1, GROUP):
            shifted.append(pltpu.roll(shifted[0], i, 0))
        total = None
        for t in reversed(range(0, taps.shape[0], GROUP)):
            if total is not None:
                total = pltpu.roll(total, GROUP, 0)
            for i in range(min(GROUP, taps.shape[0] - t)):
                term = taps[t + i : t + i + 1, tap_first : tap_first + chan] * shifted[i]
                total = term if total is None else total + term
        return total[EDGE:]

    def key_value(buf, r, rows):
        keyed = feature(buf, r, rows, 0, chan)
        valued = feature(buf, r, rows, chan, 2 * chan)
        return (keyed * valued).astype(BF16)

    def edge_state(product):
        total = jnp.zeros((modes, chan), F32)
        for r in range(EDGE):
            total = total + edge_fall[r] * product[r : r + 1].astype(F32)
        return total

    strip = 64 if tok % 64 == 0 else 32
    mid = tok // 2 // strip * strip
    zeros = jnp.zeros((EDGE, chan), BF16)
    for k in range(late, chunks):
        held_copy(k, body).wait()
        ingest(k, 0, mid)
    for k in range(late, chunks):
        ingest(k, mid, body)
    top_inv = inverse(slice(0, mid))
    proj_kv[:mid] = acc_kv[:mid] * top_inv
    prod[:strip] = jnp.concatenate([zeros, key_value(proj_kv, EDGE, strip - EDGE)], axis=0)
    for r in range(strip, mid, strip):
        prod[r : r + strip] = key_value(proj_kv, r, strip)

    low_inv = inverse(slice(mid, body))
    proj_kv[mid:body] = acc_kv[mid:body] * low_inv
    inv = jnp.concatenate([top_inv, low_inv, tail_inv], axis=0)

    @pl.when(side == 0)
    def _():
        heading.start()

    lead[EDGE:] = proj_kv[:EDGE]

    @pl.when(me == 0)
    def _():
        lead[:EDGE] = jnp.zeros((EDGE, 2 * chan), F32)
        proj_q[:EDGE] = jnp.zeros((EDGE, chan), F32)

    @pl.when(me == 1)
    def _():
        other_lead[:EDGE] = jnp.zeros((EDGE, 2 * chan), F32)

    half = tok // 2

    quarter = tok // 4

    def query_steps(some, starts, first):
        for r in starts:
            total = None
            for k in some:
                term = dot(held[k, r : r + quarter], w_q[k * depth : (k + 1) * depth])
                total = term if total is None else total + term
            acc_q[r : r + quarter] = total if first else acc_q[r : r + quarter] + total

    for r in range(mid, tok, strip):
        prod[r : r + strip] = key_value(proj_kv, r, strip)

    wide = []
    for m in (0, every // 2):
        low_part = dot(fall[every + m : every + m + every // 2], prod[...])
        wide.append(dot(fall[m : m + every // 2], prod[...]) + low_part)
    wide = jnp.concatenate(wide, axis=0)
    group_of = iota((modes, chan), 1) // per_group
    packed = jnp.zeros((modes, chan), F32)
    for g in range(groups):
        packed = packed + jnp.where(group_of == g, wide[g * modes : (g + 1) * modes], 0.0)

    @pl.when(side == 0)
    def _():
        mine_state[...] = packed
        swap.start()

    @pl.when(side == 1)
    def _():
        halo.wait_recv()
        rows = key_value(lead, EDGE, EDGE)
        prod[:EDGE] = rows
        mine_state[...] = packed + edge_state(rows)
        swap.start()

    early, later = max(1, chunks * 3 // 8), max(1, chunks * 3 // 4)
    for i in range(parts):
        q_copy(i).wait()
    query_steps(range(early), (half, half + quarter), True)
    decay = jnp.exp(-rate_mc * float(tok))
    side_chan = chan // 2
    low_rows = (half, half + quarter)

    def more_low():
        if early < later:
            query_steps(range(early, later), low_rows, False)

    pl.when(side == 1)(more_low)

    @pl.when(jnp.logical_and(side == 0, me > 0))
    def _():
        halo.wait_recv()

    @pl.when(side == 0)
    def _():
        rows = key_value(lead, EDGE, EDGE)
        prod[:EDGE] = rows
        whole = packed + edge_state(rows)
        swap.wait_recv()
        own[...] = (decay * whole + other_state[...])[:, :side_chan].astype(BF16)

    @pl.when(jnp.logical_and(side == 1, pair > 0))
    def _():
        far_halo.wait_recv()

    @pl.when(side == 1)
    def _():
        heading.wait_recv()
        swap.wait_recv()
        whole = other_state[...] + edge_state(key_value(other_lead, EDGE, EDGE))
        even_state[...] = whole
        own[...] = (decay * whole + mine_state[...])[:, side_chan:].astype(BF16)

    def state_copy(source, target):
        return pltpu.make_async_remote_copy(
            src_ref=own, dst_ref=slots.at[source],
            send_sem=load_sem.at[target], recv_sem=recv_sem.at[source],
            device_id=(2 * target + side,), device_id_type=MESH,
        )

    @pl.loop(0, pairs - 1 - pair)
    def _(i):
        state_copy(pair, pairs - 1 - i).start()

    pl.when(side == 0)(more_low)
    if later < chunks:
        query_steps(range(later, chunks), low_rows, False)
    proj_q[EDGE + half :] = acc_q[half:] * inv[half:]

    @pl.when(has_next)
    def _():
        q_halo.start()

    query_steps(range(chunks), (0, quarter), True)
    make_toeplitz(range(groups))
    proj_q[EDGE : EDGE + half] = acc_q[:half] * inv[:half]

    product = prod[...]
    channel_group = iota((tok, chan), 1) // per_group
    block = 2 * LANES

    def convolve(some):
        for s0 in range(0, tok, block):
            s1 = min(s0 + block, tok)
            parts = [
                jnp.where(channel_group[s0:s1] == g, product[s0:s1], jnp.zeros_like(product[s0:s1])) for g in some
            ]
            step = (tok - s0) // 2
            for r in (s0, s0 + step):
                total = None
                for g, part in zip(some, parts):
                    term = dot(toeplitz[g, r : r + step, s0:s1], part)
                    total = term if total is None else total + term
                acc_q[r : r + step] += total

    acc_q[...] = skip[...] * product.astype(F32)
    convolve(range(groups // 2))
    make_rise()

    for r in range(strip, tok, strip):
        feat_q[r : r + strip] = feature(proj_q, EDGE + r, strip, 0, 0)
    convolve(range(groups // 2, groups))

    pair_decay = jnp.exp(-rate_mc * float(2 * tok))
    pair_decay = jnp.where(side == 1, pair_decay[:, side_chan:], pair_decay[:, :side_chan])
    trade = near_copy(5, carried.at[side], carried.at[side], sibling)

    def gather(p, state):
        state_copy(p, pair).wait_recv()
        return pair_decay * state + slots[p].astype(F32)

    carried[side] = lax.fori_loop(0, pair, gather, jnp.zeros((modes, side_chan), F32))
    trade.start()

    @pl.when(me > 0)
    def _():
        q_halo.wait_recv()

    feat_q[:strip] = feature(proj_q, EDGE, strip, 0, 0)
    trade.wait_recv()
    state = jnp.concatenate([carried[0], carried[1]], axis=1)
    state = jnp.where(side == 1, decay * state + even_state[...], state) * weight_mc
    stacked = jnp.concatenate([state] * groups, axis=0)
    same = iota((every, chan), 0) // modes == iota((every, chan), 1) // per_group
    high, low = split(jnp.where(same, stacked, 0.0))
    paired = jnp.concatenate([high, high], axis=0)
    for r in (0, half):
        rows = slice(r, r + half)
        far = dot(rise[rows], paired) + dot(rise[rows, :every], low)
        out[rows] = (feat_q[rows] * (acc_q[rows] + far)).astype(BF16)

    out_copy.wait()

    swap.wait_send()
    trade.wait_send()

    @pl.when(has_next)
    def _():
        halo.wait_send()
        q_halo.wait_send()

    @pl.when(sends_far)
    def _():
        far_halo.wait_send()

    @pl.when(side == 0)
    def _():
        heading.wait_send()

    @pl.loop(pair + 1, pairs)
    def _(p):
        state_copy(pair, p).wait_send()


def project_out(gated, w_out, mixed, held, sem):
    width = mixed.shape[1]
    block = width // PARTS
    for k in range(PARTS):
        cols = slice(k * block, (k + 1) * block)
        held[:, cols] = dot(gated[...], w_out[:, cols]).astype(BF16)
        pltpu.make_async_copy(held.at[:, cols], mixed.at[:, cols], sem).start()
    pltpu.make_async_copy(held, mixed, sem).wait()


def on_device(n, hidden, norm_gain, w_in, w_short, residues, rates, skip, w_out):
    tok, width = hidden.shape
    chan = w_short.shape[0] // 3
    groups, modes = rates.shape
    every = groups * modes
    depth = min(1024, width)
    chunks = width // depth
    vmem = pl.BlockSpec(memory_space=pltpu.VMEM)
    in_hbm = pl.BlockSpec(memory_space=pltpu.HBM)
    gated, w_out_near = pl.pallas_call(
        functools.partial(mixer, n, depth),
        out_shape=[pltpu.VMEM((tok, chan), BF16), pltpu.VMEM((chan, width), BF16)],
        in_specs=[in_hbm] * 8,
        out_specs=[vmem, vmem],
        scratch_shapes=[
            pltpu.VMEM((1, width), F32),
            pltpu.VMEM((w_short.shape[1], 3 * chan), F32),
            pltpu.VMEM((groups, modes), F32),
            pltpu.VMEM((groups, modes), F32),
            pltpu.VMEM((1, chan), F32),
            pltpu.VMEM((chunks, tok, depth), BF16),
            pltpu.VMEM((chunks, depth, 2 * chan), BF16),
            pltpu.VMEM((width, chan), BF16),
            pltpu.VMEM((TAIL, width - chunks * 7 // 8 * depth), BF16),
            pltpu.VMEM((tok, 2 * chan), F32),
            pltpu.VMEM((tok, chan), F32),
            pltpu.VMEM((tok, LANES), F32),
            pltpu.VMEM((tok, 2 * chan), F32),
            pltpu.VMEM((EDGE + tok, chan), F32),
            pltpu.VMEM((tok, chan), BF16),
            pltpu.VMEM((tok, chan), F32),
            pltpu.VMEM((2 * every, tok), BF16),
            pltpu.VMEM((tok, 2 * every), BF16),
            pltpu.VMEM((groups, tok), F32),
            pltpu.VMEM((groups, tok, tok), BF16),
            pltpu.VMEM((2 * EDGE, 2 * chan), F32),
            pltpu.VMEM((2 * EDGE, 2 * chan), F32),
            pltpu.VMEM((EDGE, modes, chan), F32),
            pltpu.VMEM((modes, chan), F32),
            pltpu.VMEM((modes, chan), F32),
            pltpu.VMEM((modes, chan), F32),
            pltpu.VMEM((modes, chan // 2), BF16),
            pltpu.VMEM((n // 2, modes, chan // 2), BF16),
            pltpu.VMEM((2, modes, chan // 2), F32),
            pltpu.SemaphoreType.DMA((max(2 * chunks, n // 2),)),
            pltpu.SemaphoreType.DMA((6,)),
            pltpu.SemaphoreType.DMA((n // 2,)),
            pltpu.SemaphoreType.DMA((6,)),
        ],
        compiler_params=pltpu.CompilerParams(
            collective_id=0, has_side_effects=True, vmem_limit_bytes=48 * 1024 * 1024
        ),
        name="mixer",
        cost_estimate=pl.CostEstimate(
            flops=2 * tok * width * 3 * chan, bytes_accessed=2 * width * (tok + 3 * chan), transcendentals=0
        ),
    )(
        hidden, w_in, w_out,
        *(
            pltpu.with_memory_space_constraint(x, pltpu.HBM)
            for x in (norm_gain.reshape(1, width), w_short.T, rates, residues, skip.reshape(1, chan))
        ),
    )
    return pl.pallas_call(
        project_out,
        out_shape=jax.ShapeDtypeStruct((tok, width), BF16),
        in_specs=[vmem, vmem],
        out_specs=in_hbm,
        scratch_shapes=[
            pltpu.VMEM((tok, width), BF16),
            pltpu.SemaphoreType.DMA,
        ],
        name="project_out",
        compiler_params=pltpu.CompilerParams(vmem_limit_bytes=24 * 1024 * 1024),
        cost_estimate=pl.CostEstimate(
            flops=2 * tok * width * chan, bytes_accessed=2 * width * (tok + chan), transcendentals=0
        ),
    )(gated, w_out_near)


def solution(mesh):
    return jax.shard_map(
        functools.partial(on_device, mesh.shape["tm"]),
        mesh=mesh,
        in_specs=(P("tm", None), P(), P(), P(), P(), P(), P(), P()),
        out_specs=P("tm", None),
        check_vma=False,
    )
```

```python
import functools

import jax
import jax.numpy as jnp
from jax import lax
from jax.experimental import pallas as pl
from jax.experimental.pallas import tpu as pltpu
from jax.sharding import PartitionSpec as P

HIGHEST = lax.Precision.HIGHEST
MESH = pl.DeviceIdType.MESH
LANES = 128
EDGE = 8
TAIL = 16
GROUP = 3
PARTS = 16
F32 = jnp.float32
BF16 = jnp.bfloat16


def iota(shape, dim):
    return lax.broadcasted_iota(jnp.int32, shape, dim)


def dot(a, b):
    return jnp.dot(a, b, preferred_element_type=F32)


def split(x):
    high = x.astype(BF16)
    return high, (x - high.astype(F32)).astype(BF16)


def mixer(
    n, depth, hidden, w_in, w_out, gain_far, taps_far, rates_far, residues_far, skip_far, out, w_out_near,
    gain, taps, rates, residues, skip,
    held, w_kv, w_q, tail, acc_kv, acc_q, squares, proj_kv, proj_q, prod, feat_q,
    fall, rise, lag_row, toeplitz, lead, other_lead, edge_fall, mine_state, other_state, even_state, own, slots, carried,
    load_sem, near_recv, recv_sem, small_sem,
):
    me = lax.axis_index("tm")
    following = lax.rem(me + 1, n)
    pairs = n // 2
    pair, side = me // 2, lax.rem(me, 2)
    sibling = me + 1 - 2 * side
    tok, width = hidden.shape
    chan = prod.shape[1]
    groups, modes = rates.shape
    every = groups * modes
    per_group = chan // groups
    chunks = width // depth

    small = [
        pltpu.make_async_copy(source, target, small_sem.at[i])
        for i, (source, target) in enumerate(
            [(rates_far, rates), (residues_far, residues), (gain_far, gain), (taps_far, taps), (skip_far, skip)]
        )
    ]
    for copy in small:
        copy.start()

    late = chunks * 7 // 8
    body = tok - TAIL

    def held_copy(k, rows):
        rows, cols = pl.ds(0, rows), pl.ds(pl.multiple_of(k * depth, depth), depth)
        return pltpu.make_async_copy(hidden.at[rows, cols], held.at[k, rows], load_sem.at[k])

    tail_copy = pltpu.make_async_copy(
        hidden.at[pl.ds(body, TAIL), pl.ds(late * depth, width - late * depth)], tail, small_sem.at[5]
    )

    def kv_copy(k):
        rows = pl.ds(pl.multiple_of(k * depth, depth), depth)
        return pltpu.make_async_copy(w_in.at[rows, pl.ds(chan, 2 * chan)], w_kv.at[k], load_sem.at[chunks + k])

    parts = 2 if chunks % 2 == 0 else 1
    deep = width // parts

    def q_copy(i):
        rows = pl.ds(i * deep, deep)
        return pltpu.make_async_copy(w_in.at[rows, pl.ds(0, chan)], w_q.at[rows], load_sem.at[1 + i])

    @pl.loop(0, late)
    def _(k):
        held_copy(k, tok).start()
        kv_copy(k).start()

    tail_copy.start()

    @pl.loop(late, chunks)
    def _(k):
        kv_copy(k).start()

    @pl.loop(late, chunks)
    def _(k):
        held_copy(k, body).start()

    out_copy = pltpu.make_async_copy(w_out, w_out_near, load_sem.at[0])

    barrier = pltpu.get_barrier_semaphore()

    def greet(d):
        pl.semaphore_signal(barrier, inc=1, device_id=(d,), device_id_type=MESH)

    @pl.loop(0, pair)
    def _(p):
        greet(2 * p + side)

    greet(sibling)

    @pl.when(jnp.logical_and(side == 0, pair > 0))
    def _():
        greet(me - 1)

    for copy in small:
        copy.wait()

    pick = (iota((modes, every), 1) % modes == iota((modes, every), 0)).astype(F32)
    mine = iota((groups, every), 1) // modes == iota((groups, every), 0)
    spread = (iota((groups, chan), 1) // per_group == iota((groups, chan), 0)).astype(F32)
    diagonal = iota((every, every), 0) == iota((every, every), 1)
    weights = residues[...] * jnp.sqrt(2.0 * rates[...])

    def as_row(x):
        wide = jnp.dot(x, pick, precision=HIGHEST, preferred_element_type=F32)
        return jnp.sum(jnp.where(mine, wide, 0.0), axis=0, keepdims=True)

    def as_column(row):
        return jnp.sum(jnp.where(diagonal, row, 0.0), axis=1, keepdims=True)

    def by_channel(x):
        return lax.dot_general(
            x, spread, (((0,), (0,)), ((), ())), precision=HIGHEST, preferred_element_type=F32
        )

    rate_row = as_row(rates[...])
    rate_col = as_column(rate_row)
    weight_col = as_column(as_row(weights))
    rate_mc = by_channel(rates[...])
    weight_mc = by_channel(weights)
    tiles = tok // LANES
    causal = iota((LANES, LANES), 0) >= iota((LANES, LANES), 1)

    def make_fall():
        high, low = split(jnp.exp(-rate_col * (tok - 1 - iota((every, tok), 1)).astype(F32)))
        early_rows = iota((every, tok), 1) < EDGE
        fall[:every] = jnp.where(early_rows, jnp.zeros_like(high), high)
        fall[every:] = jnp.where(early_rows, jnp.zeros_like(low), low)

    def make_rise():
        high, low = split(jnp.exp(-rate_row * (iota((tok, every), 0) + 1).astype(F32)))
        rise[:, :every], rise[:, every:] = high, low

    def make_lags():
        for r in range(EDGE):
            edge_fall[r] = jnp.exp(-rate_mc * float(tok - 1 - r))
        back = lax.rem(tok - iota((every, tok), 1), tok).astype(F32)
        terms = weight_col * jnp.exp(-rate_col * back)
        for g in range(groups):
            lag_row[g : g + 1] = jnp.sum(terms[g * modes : (g + 1) * modes], axis=0, keepdims=True)

    def make_toeplitz(some):
        for g in some:
            top = jnp.broadcast_to(lag_row[g : g + 1], (LANES, tok))
            moved = pltpu.roll(top, 0, 1, stride=1, stride_axis=0)
            lags = []
            for i in range(tiles):
                at = (tiles - i) % tiles * LANES
                tile = moved[:, at : at + LANES]
                lags.append((jnp.where(causal, tile, 0.0) if i == 0 else tile).astype(BF16))
            for i in range(tiles):
                for j in range(tiles):
                    value = lags[i - j] if i >= j else jnp.zeros((LANES, LANES), BF16)
                    toeplitz[g, i * LANES : (i + 1) * LANES, j * LANES : (j + 1) * LANES] = value

    even_state[...] = jnp.zeros_like(even_state)

    def ingest(k, first, stop):
        scale = gain[:, k * depth : (k + 1) * depth]
        parts = []
        for r in range(first, stop, 16):
            x = held[k, r : r + 16].astype(F32)
            sq = x * x
            total = sq[:, :LANES] if k == 0 else squares[r : r + 16] + sq[:, :LANES]
            for j in range(LANES, depth, LANES):
                total = total + sq[:, j : j + LANES]
            squares[r : r + 16] = total
            parts.append((x * scale).astype(BF16))
        scaled = jnp.concatenate(parts, axis=0)
        held[k, first:stop] = scaled
        if k == 0:
            acc_kv[first:stop] = dot(scaled, w_kv[k])
        else:
            acc_kv[first:stop] += dot(scaled, w_kv[k])

    jobs = [make_lags, make_fall]
    where = [k for k in range(late) if k > 0] or [0]

    def beside(k):
        for i, job in enumerate(jobs):
            if where[i * len(where) // len(jobs)] == k:
                job()

    for k in range(late):
        held_copy(k, tok).wait()
        kv_copy(k).wait()
        ingest(k, 0, tok)
        beside(k)
    for i in range(parts):
        q_copy(i).start(priority=1)
    out_copy.start(priority=1)
    tail_copy.wait()
    for k in range(late, chunks):
        held[k, body:] = tail[:, (k - late) * depth : (k - late + 1) * depth]
    for k in range(late, chunks):
        kv_copy(k).wait()
        ingest(k, body, tok)

    def inverse(rows):
        return lax.rsqrt(jnp.sum(squares[rows], axis=1, keepdims=True) / width + 1e-06)

    tail_inv = inverse(slice(body, tok))
    proj_kv[body:] = acc_kv[body:] * tail_inv
    pl.semaphore_wait(barrier, pairs - pair + side * jnp.minimum(pairs - 1 - pair, 1))

    def near_copy(i, source, target, device):
        return pltpu.make_async_remote_copy(
            src_ref=source, dst_ref=target, send_sem=small_sem.at[i], recv_sem=near_recv.at[i],
            device_id=(device,), device_id_type=MESH,
        )

    before, first = pl.ds(0, EDGE), pl.ds(EDGE, EDGE)
    last = proj_kv.at[pl.ds(tok - EDGE, EDGE)]
    halo = near_copy(0, last, lead.at[before], following)
    far_halo = near_copy(1, last, other_lead.at[before], lax.rem(me + 2, n))
    heading = near_copy(2, proj_kv.at[before], other_lead.at[first], sibling)
    swap = near_copy(3, mine_state, other_state, sibling)
    q_halo = near_copy(4, proj_q.at[pl.ds(tok, EDGE)], proj_q.at[before], following)
    has_next = me < n - 1
    sends_far = jnp.logical_and(side == 1, has_next)

    @pl.when(has_next)
    def _():
        halo.start()

    @pl.when(sends_far)
    def _():
        far_halo.start()

    def feature(buf, r, rows, first, tap_first):
        shifted = [buf[pl.ds(r - EDGE, EDGE + rows), first : first + chan]]
        for i in range(1, GROUP):
            shifted.append(pltpu.roll(shifted[0], i, 0))
        total = None
        for t in reversed(range(0, taps.shape[0], GROUP)):
            if total is not None:
                total = pltpu.roll(total, GROUP, 0)
            for i in range(min(GROUP, taps.shape[0] - t)):
                term = taps[t + i : t + i + 1, tap_first : tap_first + chan] * shifted[i]
                total = term if total is None else total + term
        return total[EDGE:]

    def key_value(buf, r, rows):
        keyed = feature(buf, r, rows, 0, chan)
        valued = feature(buf, r, rows, chan, 2 * chan)
        return (keyed * valued).astype(BF16)

    def edge_state(product):
        total = jnp.zeros((modes, chan), F32)
        for r in range(EDGE):
            total = total + edge_fall[r] * product[r : r + 1].astype(F32)
        return total

    strip = 64 if tok % 64 == 0 else 32
    mid = tok // 2 // strip * strip
    zeros = jnp.zeros((EDGE, chan), BF16)
    for k in range(late, chunks):
        held_copy(k, body).wait()
        ingest(k, 0, mid)
    for k in range(late, chunks):
        ingest(k, mid, body)
    top_inv = inverse(slice(0, mid))
    proj_kv[:mid] = acc_kv[:mid] * top_inv
    prod[:strip] = jnp.concatenate([zeros, key_value(proj_kv, EDGE, strip - EDGE)], axis=0)
    for r in range(strip, mid, strip):
        prod[r : r + strip] = key_value(proj_kv, r, strip)

    low_inv = inverse(slice(mid, body))
    proj_kv[mid:body] = acc_kv[mid:body] * low_inv
    inv = jnp.concatenate([top_inv, low_inv, tail_inv], axis=0)

    @pl.when(side == 0)
    def _():
        heading.start()

    lead[EDGE:] = proj_kv[:EDGE]

    @pl.when(me == 0)
    def _():
        lead[:EDGE] = jnp.zeros((EDGE, 2 * chan), F32)
        proj_q[:EDGE] = jnp.zeros((EDGE, chan), F32)

    @pl.when(me == 1)
    def _():
        other_lead[:EDGE] = jnp.zeros((EDGE, 2 * chan), F32)

    half = tok // 2

    quarter = tok // 4

    def query_steps(some, starts, first):
        for r in starts:
            total = None
            for k in some:
                term = dot(held[k, r : r + quarter], w_q[k * depth : (k + 1) * depth])
                total = term if total is None else total + term
            acc_q[r : r + quarter] = total if first else acc_q[r : r + quarter] + total

    for r in range(mid, tok, strip):
        prod[r : r + strip] = key_value(proj_kv, r, strip)

    wide = []
    for m in (0, every // 2):
        low_part = dot(fall[every + m : every + m + every // 2], prod[...])
        wide.append(dot(fall[m : m + every // 2], prod[...]) + low_part)
    wide = jnp.concatenate(wide, axis=0)
    group_of = iota((modes, chan), 1) // per_group
    packed = jnp.zeros((modes, chan), F32)
    for g in range(groups):
        packed = packed + jnp.where(group_of == g, wide[g * modes : (g + 1) * modes], 0.0)

    @pl.when(side == 0)
    def _():
        mine_state[...] = packed
        swap.start()

    @pl.when(side == 1)
    def _():
        halo.wait_recv()
        rows = key_value(lead, EDGE, EDGE)
        prod[:EDGE] = rows
        mine_state[...] = packed + edge_state(rows)
        swap.start()

    early, later = max(1, chunks // 4), max(1, chunks * 5 // 8)
    for i in range(parts):
        q_copy(i).wait()
    query_steps(range(early), (half, half + quarter), True)
    decay = jnp.exp(-rate_mc * float(tok))
    side_chan = chan // 2
    low_rows = (half, half + quarter)

    def more_low():
        if early < later:
            query_steps(range(early, later), low_rows, False)

    pl.when(side == 1)(more_low)

    @pl.when(jnp.logical_and(side == 0, me > 0))
    def _():
        halo.wait_recv()

    @pl.when(side == 0)
    def _():
        rows = key_value(lead, EDGE, EDGE)
        prod[:EDGE] = rows
        whole = packed + edge_state(rows)
        swap.wait_recv()
        own[...] = (decay * whole + other_state[...])[:, :side_chan].astype(BF16)

    @pl.when(jnp.logical_and(side == 1, pair > 0))
    def _():
        far_halo.wait_recv()

    @pl.when(side == 1)
    def _():
        heading.wait_recv()
        swap.wait_recv()
        whole = other_state[...] + edge_state(key_value(other_lead, EDGE, EDGE))
        even_state[...] = whole
        own[...] = (decay * whole + mine_state[...])[:, side_chan:].astype(BF16)

    def state_copy(source, target):
        return pltpu.make_async_remote_copy(
            src_ref=own, dst_ref=slots.at[source],
            send_sem=load_sem.at[target], recv_sem=recv_sem.at[source],
            device_id=(2 * target + side,), device_id_type=MESH,
        )

    @pl.loop(0, pairs - 1 - pair)
    def _(i):
        state_copy(pair, pairs - 1 - i).start()

    pl.when(side == 0)(more_low)
    if later < chunks:
        query_steps(range(later, chunks), low_rows, False)
    proj_q[EDGE + half :] = acc_q[half:] * inv[half:]

    @pl.when(has_next)
    def _():
        q_halo.start()

    query_steps(range(chunks), (0, quarter), True)
    make_toeplitz(range(groups))
    proj_q[EDGE : EDGE + half] = acc_q[:half] * inv[:half]

    product = prod[...]
    channel_group = iota((tok, chan), 1) // per_group
    block = 2 * LANES

    def convolve(some):
        for s0 in range(0, tok, block):
            s1 = min(s0 + block, tok)
            parts = [
                jnp.where(channel_group[s0:s1] == g, product[s0:s1], jnp.zeros_like(product[s0:s1])) for g in some
            ]
            step = (tok - s0) // 2
            for r in (s0, s0 + step):
                total = None
                for g, part in zip(some, parts):
                    term = dot(toeplitz[g, r : r + step, s0:s1], part)
                    total = term if total is None else total + term
                acc_q[r : r + step] += total

    acc_q[...] = skip[...] * product.astype(F32)
    convolve(range(groups // 2))
    make_rise()

    for r in range(strip, tok, strip):
        feat_q[r : r + strip] = feature(proj_q, EDGE + r, strip, 0, 0)
    convolve(range(groups // 2, groups))

    pair_decay = jnp.exp(-rate_mc * float(2 * tok))
    pair_decay = jnp.where(side == 1, pair_decay[:, side_chan:], pair_decay[:, :side_chan])
    trade = near_copy(5, carried.at[side], carried.at[side], sibling)

    def gather(p, state):
        state_copy(p, pair).wait_recv()
        return pair_decay * state + slots[p].astype(F32)

    carried[side] = lax.fori_loop(0, pair, gather, jnp.zeros((modes, side_chan), F32))
    trade.start()

    @pl.when(me > 0)
    def _():
        q_halo.wait_recv()

    feat_q[:strip] = feature(proj_q, EDGE, strip, 0, 0)
    trade.wait_recv()
    state = jnp.concatenate([carried[0], carried[1]], axis=1)
    state = jnp.where(side == 1, decay * state + even_state[...], state) * weight_mc
    stacked = jnp.concatenate([state] * groups, axis=0)
    same = iota((every, chan), 0) // modes == iota((every, chan), 1) // per_group
    high, low = split(jnp.where(same, stacked, 0.0))
    paired = jnp.concatenate([high, high], axis=0)
    for r in (0, half):
        rows = slice(r, r + half)
        far = dot(rise[rows], paired) + dot(rise[rows, :every], low)
        out[rows] = (feat_q[rows] * (acc_q[rows] + far)).astype(BF16)

    out_copy.wait()

    swap.wait_send()
    trade.wait_send()

    @pl.when(has_next)
    def _():
        halo.wait_send()
        q_halo.wait_send()

    @pl.when(sends_far)
    def _():
        far_halo.wait_send()

    @pl.when(side == 0)
    def _():
        heading.wait_send()

    @pl.loop(pair + 1, pairs)
    def _(p):
        state_copy(pair, p).wait_send()


def project_out(gated, w_out, mixed, held, sem):
    width = mixed.shape[1]
    block = width // PARTS
    for k in range(PARTS):
        cols = slice(k * block, (k + 1) * block)
        held[:, cols] = dot(gated[...], w_out[:, cols]).astype(BF16)
        pltpu.make_async_copy(held.at[:, cols], mixed.at[:, cols], sem).start()
    pltpu.make_async_copy(held, mixed, sem).wait()


def on_device(n, hidden, norm_gain, w_in, w_short, residues, rates, skip, w_out):
    tok, width = hidden.shape
    chan = w_short.shape[0] // 3
    groups, modes = rates.shape
    every = groups * modes
    depth = min(1024, width)
    chunks = width // depth
    vmem = pl.BlockSpec(memory_space=pltpu.VMEM)
    in_hbm = pl.BlockSpec(memory_space=pltpu.HBM)
    gated, w_out_near = pl.pallas_call(
        functools.partial(mixer, n, depth),
        out_shape=[pltpu.VMEM((tok, chan), BF16), pltpu.VMEM((chan, width), BF16)],
        in_specs=[in_hbm] * 8,
        out_specs=[vmem, vmem],
        scratch_shapes=[
            pltpu.VMEM((1, width), F32),
            pltpu.VMEM((w_short.shape[1], 3 * chan), F32),
            pltpu.VMEM((groups, modes), F32),
            pltpu.VMEM((groups, modes), F32),
            pltpu.VMEM((1, chan), F32),
            pltpu.VMEM((chunks, tok, depth), BF16),
            pltpu.VMEM((chunks, depth, 2 * chan), BF16),
            pltpu.VMEM((width, chan), BF16),
            pltpu.VMEM((TAIL, width - chunks * 7 // 8 * depth), BF16),
            pltpu.VMEM((tok, 2 * chan), F32),
            pltpu.VMEM((tok, chan), F32),
            pltpu.VMEM((tok, LANES), F32),
            pltpu.VMEM((tok, 2 * chan), F32),
            pltpu.VMEM((EDGE + tok, chan), F32),
            pltpu.VMEM((tok, chan), BF16),
            pltpu.VMEM((tok, chan), F32),
            pltpu.VMEM((2 * every, tok), BF16),
            pltpu.VMEM((tok, 2 * every), BF16),
            pltpu.VMEM((groups, tok), F32),
            pltpu.VMEM((groups, tok, tok), BF16),
            pltpu.VMEM((2 * EDGE, 2 * chan), F32),
            pltpu.VMEM((2 * EDGE, 2 * chan), F32),
            pltpu.VMEM((EDGE, modes, chan), F32),
            pltpu.VMEM((modes, chan), F32),
            pltpu.VMEM((modes, chan), F32),
            pltpu.VMEM((modes, chan), F32),
            pltpu.VMEM((modes, chan // 2), BF16),
            pltpu.VMEM((n // 2, modes, chan // 2), BF16),
            pltpu.VMEM((2, modes, chan // 2), F32),
            pltpu.SemaphoreType.DMA((max(2 * chunks, n // 2),)),
            pltpu.SemaphoreType.DMA((6,)),
            pltpu.SemaphoreType.DMA((n // 2,)),
            pltpu.SemaphoreType.DMA((6,)),
        ],
        compiler_params=pltpu.CompilerParams(
            collective_id=0, has_side_effects=True, vmem_limit_bytes=48 * 1024 * 1024
        ),
        name="mixer",
        cost_estimate=pl.CostEstimate(
            flops=2 * tok * width * 3 * chan, bytes_accessed=2 * width * (tok + 3 * chan), transcendentals=0
        ),
    )(
        hidden, w_in, w_out,
        *(
            pltpu.with_memory_space_constraint(x, pltpu.HBM)
            for x in (norm_gain.reshape(1, width), w_short.T, rates, residues, skip.reshape(1, chan))
        ),
    )
    return pl.pallas_call(
        project_out,
        out_shape=jax.ShapeDtypeStruct((tok, width), BF16),
        in_specs=[vmem, vmem],
        out_specs=in_hbm,
        scratch_shapes=[
            pltpu.VMEM((tok, width), BF16),
            pltpu.SemaphoreType.DMA,
        ],
        name="project_out",
        compiler_params=pltpu.CompilerParams(vmem_limit_bytes=24 * 1024 * 1024),
        cost_estimate=pl.CostEstimate(
            flops=2 * tok * width * chan, bytes_accessed=2 * width * (tok + chan), transcendentals=0
        ),
    )(gated, w_out_near)


def solution(mesh):
    return jax.shard_map(
        functools.partial(on_device, mesh.shape["tm"]),
        mesh=mesh,
        in_specs=(P("tm", None), P(), P(), P(), P(), P(), P(), P()),
        out_specs=P("tm", None),
        check_vma=False,
    )
```
